32 devices in a mesh: dom: 8 (over z, x), cls: 4 (over y, core).
Axes of the slice: x: 2, y: 2, z: 4, core: 2. Of those that a mesh axis runs over, the one named last changes fastest.
Arguments:
- spectra: bfloat16 [512, 128, 512], P(('dom', 'cls')), may hold values from -6 to 6
- ctf: bfloat16 [512, 128], P(('dom', 'cls')), may hold values from -1 to 1
- noise_power: float32 [128], replicated, may hold values from 0.5 to 8
- references: bfloat16 [48, 32, 512], P('cls'), may hold values from -3 to 3
- owner: int32 [512, 1], P(('dom', 'cls')), may hold values from 0 to 3; in each aligned block of 16 rows (0 to 15, 16 to 31, ...) at most 8 rows name the same one
- sub_class: int32 [512], P(('dom', 'cls')), may hold values from 0 to 11
- rotation: int32 [512], P(('dom', 'cls')), may hold values from 0 to 511
Outputs:
- new_refs: float32 [48, 128, 512], P('cls', 'dom')
- log_evidence: float32 [512], P(('dom', 'cls'))
The draws below stay inside these ranges and needn't reach their ends.
Inputs may be any that keep to these rules, and one draw needn't show every extreme that they name: Among the 16 particles of one device, at most 8 have the same owner, a bound that some block reaches of them.
All inputs are finite; a program needn't handle non-finite values.
Results may differ from the reference program's by a relative error of at most 0.00067.
Values may be sent and summed in bfloat16 or wider, within the bound.
No kernel may reach another device: no remote copies, remote signals or barrier semaphores. Data moves between devices by JAX's collectives and lax.ppermute only.
A program may use at most 128 MiB of HBM per device.

```python
import math
import jax
import jax.numpy as jnp
import numpy as np
from jax import lax

R = 128
F = 256
RE = 32
K_DEV = 12
NP_DEV = 16
K = 48
S = 512
CAP = 8
PARTICLES = 512
N_CLS = 4


def with_ends(drawn, own_key, least, top_value):
    longest = drawn.shape.index(max(drawn.shape))
    spots = []
    for shift in (0, 1):
        where = [jax.random.randint(jax.random.fold_in(own_key, axis), (), 0, length) for axis, length in enumerate(drawn.shape)]
        where[longest] = (where[longest] + shift) % drawn.shape[longest]
        spots.append(tuple(where))
    return drawn.at[spots[0]].set(least).at[spots[1]].set(top_value)


def level_of(own_key, shape, shards, least, largest):
    factor_of = 1.0
    for axis_at, parts in shards:
        steps = jax.random.uniform(jax.random.fold_in(jax.random.fold_in(own_key, 6), axis_at), (parts,), jnp.float32, least / len(shards), largest / len(shards))
        factor_of = factor_of * jnp.repeat(jnp.exp(steps), shape[axis_at] // parts).reshape((-1,) + (1,) * (len(shape) - 1 - axis_at))
    return factor_of


def shared_out(key, own, number, rows, count, top, reach, skew):
    order = jax.random.permutation(key, count)
    crowded, ordinary = portions_of(count, rows * top, reach, skew, True), portions_of(count, rows * top, reach, skew, False)
    places = jnp.arange(count)

    def named(sizes, turn):
        used = int((sizes > 0).sum())
        fixed = max(1, used // 4)
        shifted = fixed + (places - fixed + turn * (used - fixed)) % max(1, count - fixed)
        return jnp.zeros((count,), jnp.int32).at[order[jnp.where(places < fixed, places, shifted)]].set(jnp.asarray(sizes, jnp.int32))

    sizes = jnp.where(number % 4 == 0, named(crowded, number // 4), named(ordinary, number - number // 4 - 1))
    mixed = jax.random.permutation(jax.random.fold_in(own, 3), count)
    donor, receiver = mixed[0:count // 2 * 2:2], mixed[1:count // 2 * 2:2]
    room = jnp.minimum(sizes[donor] - 1, reach - sizes[receiver]) // 2
    room = jnp.where((donor == order[0]) | (receiver == order[0]) | (sizes[receiver] == 0), 0, jnp.maximum(room, 0))
    shifted = jax.random.randint(jax.random.fold_in(own, 4), (count // 2,), 0, 1 << 20) % (room + 1)
    sizes = sizes.at[donor].add(-shifted).at[receiver].add(shifted)
    members = jnp.searchsorted(jnp.cumsum(sizes), jnp.arange(rows * top), side="right").astype(jnp.int32)
    grid = members.reshape(top, rows).T
    grid = grid[jax.random.permutation(jax.random.fold_in(own, 1), rows)]
    turn = jax.random.randint(jax.random.fold_in(own, 2), (rows, 1), 0, top)
    return jnp.take_along_axis(grid, (jnp.arange(top)[None, :] + turn) % top, axis=1)


def portions_of(number_of, total, limit, lean, full):
    loads = [(1 << 20) // math.isqrt(grade ** lean) + 1 for grade in range(1, number_of + 1)]
    largest = limit if full else min(limit, max(-(-total // number_of), total * loads[0] // sum(loads)))
    least = 1 if total - largest >= number_of - 1 else 0
    holding, rest = [largest] + [least] * (number_of - 1), total - largest - least * (number_of - 1)
    while rest > 0:
        candidates = [i for i in range(1, number_of) if holding[i] < largest] or [i for i in range(1, number_of) if holding[i] < limit]
        whole, left = sum([loads[i] for i in candidates]), rest
        for i in candidates:
            more = min(limit - holding[i], max(1, left * loads[i] // whole), rest)
            holding[i] = holding[i] + more
            rest = rest - more
    return np.array(holding)


def centred(stream_key, extent, deviation, most, cuts=(), held_as=jnp.bfloat16):
    array = deviation * jax.random.normal(stream_key, extent, jnp.float32)
    if cuts:
        array = array * level_of(stream_key, extent, cuts, -0.22, 0.18)
    return jnp.clip(array, -most, most).astype(held_as)


def setup_inputs(seed: int = 0) -> dict:
    arg_keys = jax.random.split(jax.random.key(seed), 8)
    spectra = centred(arg_keys[0], (PARTICLES, R, 2 * F), 1.0, 6.0, ((0, 32),))
    ctf = jnp.clip(jax.random.uniform(arg_keys[1], (PARTICLES, R), jnp.float32, -1.0, 1.0) * level_of(arg_keys[1], (PARTICLES, R), ((0, 32),), -0.4, 0.0), -1.0, 1.0).astype(jnp.bfloat16)
    noise_power = jnp.clip(jnp.exp(jax.random.uniform(arg_keys[2], (R,), jnp.float32, math.log(0.5), math.log(8.0))), 0.5, 8.0)
    references = centred(arg_keys[3], (K, RE, 2 * F), 0.5, 3.0, ((0, 4),))
    owner_keys = jax.random.split(jax.random.fold_in(arg_keys[4], 1), PARTICLES // NP_DEV)
    owner_turns = jax.random.permutation(jax.random.fold_in(arg_keys[4], 3), PARTICLES // NP_DEV)
    owner = jax.vmap(lambda own, number: shared_out(jax.random.fold_in(arg_keys[4], 2), own, number, NP_DEV, N_CLS, 1, CAP, 2))(owner_keys, owner_turns).reshape((PARTICLES, 1))
    sub_class = with_ends(jax.random.randint(arg_keys[5], (PARTICLES,), 0, K_DEV), jax.random.fold_in(arg_keys[5], 1), 0, K_DEV - 1).astype(jnp.int32)
    rotation = with_ends(jax.random.randint(arg_keys[6], (PARTICLES,), 0, S), jax.random.fold_in(arg_keys[6], 1), 0, S - 1).astype(jnp.int32)
    return dict(spectra=spectra, ctf=ctf, noise_power=noise_power, references=references, owner=owner, sub_class=sub_class, rotation=rotation)


def rotation_table():
    freq = jnp.arange(F, dtype=jnp.int32)
    steps = jnp.arange(S, dtype=jnp.int32)
    turns = (freq[:, None] * steps[None, :]) % S
    angle = turns.astype(jnp.float32) * (2.0 * math.pi / S)
    return jnp.concatenate([jnp.cos(angle), -jnp.sin(angle)], axis=0).astype(jnp.bfloat16)


def block_evidence(spectra_blk, ctf_blk, noise_power, references, table):
    weight = ctf_blk.astype(jnp.float32) / noise_power[None, :]
    low = spectra_blk[:, :RE, :].astype(jnp.float32)
    weighted = (weight[:, :RE, None] * low).astype(jnp.bfloat16)
    weighted = lax.optimization_barrier(weighted).astype(jnp.float32)
    w_re = weighted[..., :F]
    w_im = weighted[..., F:]
    refs = references.astype(jnp.float32)
    y_re = refs[..., :F]
    y_im = refs[..., F:]
    cross_re = jnp.einsum('nrf,krf->nkf', w_re, y_re) + jnp.einsum('nrf,krf->nkf', w_im, y_im)
    cross_im = jnp.einsum('nrf,krf->nkf', w_im, y_re) - jnp.einsum('nrf,krf->nkf', w_re, y_im)
    cross = jnp.concatenate([cross_re, cross_im], axis=-1).astype(jnp.bfloat16)
    count = spectra_blk.shape[0]
    corr = jnp.dot(cross.reshape(count * K, 2 * F), table, preferred_element_type=jnp.float32)
    corr = corr.reshape(count, K, S)
    cw_low = ctf_blk[:, :RE].astype(jnp.float32) * weight[:, :RE]
    ynorm = jnp.sum(refs * refs, axis=-1)
    energy = jnp.dot(cw_low, ynorm.T, precision=lax.Precision.HIGHEST)
    score = corr - 0.5 * energy[:, :, None]
    top = jnp.max(score, axis=(1, 2))
    total = jnp.sum(jnp.exp(score - top[:, None, None]), axis=(1, 2))
    return top + jnp.log(total)


def reference(spectra, ctf, noise_power, references, owner, sub_class, rotation):
    blk = 64 if PARTICLES % 64 == 0 else PARTICLES
    groups = PARTICLES // blk
    table = rotation_table()
    spec_blocks = spectra.reshape(groups, blk, R, 2 * F)
    ctf_blocks = ctf.reshape(groups, blk, R)

    def evidence_of(pair):
        return block_evidence(pair[0], pair[1], noise_power, references, table)

    log_evidence = lax.map(evidence_of, (spec_blocks, ctf_blocks)).reshape(PARTICLES)

    class_id = (owner[:, 0] * K_DEV + sub_class).astype(jnp.int32)
    class_blocks = class_id.reshape(groups, blk)
    rot_blocks = rotation.reshape(groups, blk)

    def accumulate(carry, pieces):
        spec, cvals, cls_id, rot = pieces
        cfl = cvals.astype(jnp.float32)
        weight = cfl / noise_power[None, :]
        turns = (jnp.arange(F, dtype=jnp.int32)[None, :] * rot[:, None]) % S
        angle = turns.astype(jnp.float32) * (2.0 * math.pi / S)
        cosv = jnp.cos(angle)[:, None, :]
        sinv = jnp.sin(angle)[:, None, :]
        x = spec.astype(jnp.float32)
        x_re = x[..., :F]
        x_im = x[..., F:]
        a_re = weight[:, :, None] * (x_re * cosv - x_im * sinv)
        a_im = weight[:, :, None] * (x_re * sinv + x_im * cosv)
        aligned = jnp.concatenate([a_re, a_im], axis=-1).reshape(blk, R * 2 * F)
        member = (cls_id[:, None] == jnp.arange(K, dtype=jnp.int32)[None, :]).astype(jnp.float32)
        numer = carry[0] + jnp.dot(member.T, aligned, precision=lax.Precision.HIGHEST)
        denom = carry[1] + jnp.dot(member.T, cfl * weight, precision=lax.Precision.HIGHEST)
        return (numer, denom), None

    start = (jnp.zeros((K, R * 2 * F), jnp.float32), jnp.zeros((K, R), jnp.float32))
    (numer, denom), _ = lax.scan(accumulate, start, (spec_blocks, ctf_blocks, class_blocks, rot_blocks))
    new_refs = numer.reshape(K, R, 2 * F) / (denom + 1.0)[:, :, None]
    return new_refs, log_evidence
```

```python
import math

import jax
import jax.numpy as jnp
from jax import lax
from jax.experimental import pallas as pl
from jax.experimental.pallas import tpu as pltpu
from jax.sharding import PartitionSpec as P


CHUNKS = 2
GROUP = 4


def rotation_table(half, turns_all):
    freq = jnp.arange(half, dtype=jnp.int32)
    steps = jnp.arange(turns_all, dtype=jnp.int32)
    turns = freq[:, None] * steps[None, :] % turns_all
    angle = turns.astype(jnp.float32) * (2.0 * math.pi / turns_all)
    return jnp.concatenate([jnp.cos(angle), -jnp.sin(angle)], axis=0).astype(jnp.bfloat16)


def swap(value, axis, mask):
    size = lax.axis_size(axis)
    return lax.ppermute(value, axis, [(i, i ^ mask) for i in range(size)])


def score_kernel(
    low_ref, weight_ref, first_ref, second_ref, energy_ref, table_ref, out_ref,
    image, image_sum, classes, class_diff, class_sum, cross,
):
    count = out_ref.shape[0]
    tiles, rows, lanes = image.shape
    cycles = rows // count
    width = tiles * lanes
    half = width // 2
    kinds = cross.shape[0] // count
    part = first_ref.shape[0]
    low = low_ref[...].reshape(rows, width).astype(jnp.float32)
    weighted = (weight_ref[...] * low).astype(jnp.bfloat16).astype(jnp.float32)
    for f in range(tiles):
        image[f] = weighted[:, f * lanes : (f + 1) * lanes]
    for f in range(tiles // 2):
        image_sum[f] = image[f] + image[f + tiles // 2]
    for at, ref in ((0, first_ref), (part, second_ref)):
        for f in range(tiles // 2):
            re = ref[:, f * lanes : (f + 1) * lanes].astype(jnp.float32)
            im = ref[:, half + f * lanes : half + (f + 1) * lanes].astype(jnp.float32)
            classes[f, at : at + part, :] = re
            class_diff[f, at : at + part, :] = re - im
            class_sum[f, at : at + part, :] = re + im
    block = 8

    def tile(k, _):
        base = k * 8 * cycles
        for f in range(tiles // 2):
            for start in range(0, count, block):

                def cycle(r, sums):
                    rows_k = pl.ds(base + r, 8, stride=cycles)
                    y_re = classes[f, rows_k, :]
                    y_diff = class_diff[f, rows_k, :]
                    y_sum = class_sum[f, rows_k, :]
                    new = []
                    for i in range(block):
                        row = pl.ds((start + i) * cycles + r, 8, stride=0)
                        s1, s2, s3 = sums[3 * i : 3 * i + 3]
                        new.append(s1 + y_re * image_sum[f, row, :])
                        new.append(s2 + y_diff * image[f + tiles // 2, row, :])
                        new.append(s3 + y_sum * image[f, row, :])
                    return tuple(new)

                zero = jnp.zeros((8, lanes), jnp.float32)
                sums = lax.fori_loop(0, cycles, cycle, (zero,) * (3 * block), unroll=2)
                for i in range(block):
                    s1, s2, s3 = sums[3 * i : 3 * i + 3]
                    at = pl.ds(pl.multiple_of((start + i) * kinds + k * 8, 8), 8)
                    cross[at, f * lanes : (f + 1) * lanes] = s1 - s2
                    cross[at, half + f * lanes : half + (f + 1) * lanes] = s1 - s3
        return 0

    lax.fori_loop(0, kinds // 8, tile, 0)
    step = 2

    def finish(g, _):
        at = pl.ds(pl.multiple_of(g * step * kinds, 8), step * kinds)
        score = jnp.dot(
            cross[at, :].astype(jnp.bfloat16), table_ref[...], preferred_element_type=jnp.float32
        )
        score = score - energy_ref[at, :]
        for i in range(step):
            mine = score[i * kinds : (i + 1) * kinds]
            top = jnp.max(mine, axis=(0, 1), keepdims=True)
            total = jnp.sum(jnp.exp(mine - top), axis=(0, 1), keepdims=True)
            out_ref[pl.ds(g * step + i, 1), :] = jnp.broadcast_to(top + jnp.log(total), (1, lanes))
        return 0

    lax.fori_loop(0, count // step, finish, 0)


def log_evidence_of(spectra, weight, cw_low, first, second, table):
    count, _, width = spectra.shape
    cycles = cw_low.shape[1]
    kinds = 2 * first.shape[0]
    rows = count * cycles
    both = jnp.stack([first, second]).astype(jnp.float32)
    norms = jnp.sum(both * both, axis=-1).reshape(kinds, cycles)
    energy = 0.5 * jnp.dot(cw_low, norms.T, precision=lax.Precision.HIGHEST)
    out = pl.pallas_call(
        score_kernel,
        out_shape=jax.ShapeDtypeStruct((count, 128), jnp.float32),
        grid=(1,),
        in_specs=[
            pl.BlockSpec((count, cycles, width), lambda i: (0, 0, 0)),
            pl.BlockSpec((rows, 1), lambda i: (0, 0)),
            pl.BlockSpec((kinds * cycles // 2, width), lambda i: (0, 0)),
            pl.BlockSpec((kinds * cycles // 2, width), lambda i: (0, 0)),
            pl.BlockSpec((count * kinds, 1), lambda i: (0, 0)),
            pl.BlockSpec(table.shape, lambda i: (0, 0)),
        ],
        out_specs=pl.BlockSpec((count, 128), lambda i: (0, 0)),
        scratch_shapes=[
            pltpu.VMEM((width // 128, rows, 128), jnp.float32),
            pltpu.VMEM((width // 256, rows, 128), jnp.float32),
            pltpu.VMEM((width // 256, kinds * cycles, 128), jnp.float32),
            pltpu.VMEM((width // 256, kinds * cycles, 128), jnp.float32),
            pltpu.VMEM((width // 256, kinds * cycles, 128), jnp.float32),
            pltpu.VMEM((count * kinds, width), jnp.float32),
        ],
        name="score",
    )(
        spectra,
        weight[:, :cycles].reshape(rows, 1),
        first.reshape(-1, width),
        second.reshape(-1, width),
        energy.reshape(count * kinds, 1),
        table,
    )
    return out[:, 0]


def sums_kernel(place_ref, weight_ref, cos_ref, sin_ref, *refs):
    pieces = refs[:GROUP]
    keep_ref, give_ref, total = refs[GROUP:]
    kinds, cycles, width = total.shape
    half = width // 2
    count = pieces[0].shape[0] // cycles
    total[...] = jnp.zeros_like(total)
    for g, piece in enumerate(pieces):

        def particle(n, _):
            at = g * count + n
            x = piece[pl.ds(pl.multiple_of(n * cycles, cycles), cycles), :].astype(jnp.float32)
            x_re, x_im = x[:, :half], x[:, half:]
            cosv, sinv = cos_ref[pl.ds(at, 1), :], sin_ref[pl.ds(at, 1), :]
            weight = weight_ref[at]
            slot = total.at[place_ref[at]]
            slot[:, :half] += weight * (x_re * cosv - x_im * sinv)
            slot[:, half:] += weight * (x_re * sinv + x_im * cosv)
            return 0

        lax.fori_loop(0, count, particle, 0, unroll=2)
    keep_ref[...] = total[: kinds // 2]
    give_ref[...] = total[kinds // 2 :]


def class_sums(pieces, place, weight, cosv, sinv, kinds):
    particles, cycles, _ = weight.shape
    width = 2 * cosv.shape[1]
    rows = particles // GROUP * cycles
    half_sums = jax.ShapeDtypeStruct((kinds // 2, cycles, width), jnp.float32)
    return pl.pallas_call(
        sums_kernel,
        out_shape=(half_sums, half_sums),
        grid=(1,),
        in_specs=[
            pl.BlockSpec(memory_space=pltpu.SMEM),
            pl.BlockSpec(weight.shape, lambda i: (0, 0, 0)),
            pl.BlockSpec(cosv.shape, lambda i: (0, 0)),
            pl.BlockSpec(sinv.shape, lambda i: (0, 0)),
        ]
        + [pl.BlockSpec((rows, width), lambda i: (0, 0))] * GROUP,
        out_specs=(pl.BlockSpec(half_sums.shape, lambda i: (0, 0, 0)),) * 2,
        scratch_shapes=[pltpu.VMEM((kinds, cycles, width), jnp.float32)],
        name="class_sums",
    )(place, weight, cosv, sinv, *pieces)


def per_device(spectra, ctf, noise_power, references, owner, sub_class, rotation):
    count, cycles, width = spectra.shape
    half = width // 2
    low_cycles = references.shape[1]
    k_local = references.shape[0]
    turns_all = width
    domains, shards = lax.axis_size("dom"), lax.axis_size("cls")
    dom, cls = lax.axis_index("dom"), lax.axis_index("cls")
    far = domains // GROUP
    slice_cycles = cycles // domains
    mine = cycles // GROUP
    near = dom % GROUP
    kinds = shards * k_local

    place_out = owner[:, 0] * k_local + sub_class
    meta_ints = jnp.stack([rotation // 16, rotation % 16, place_out // 16, place_out % 16], axis=-1)
    meta_ints = meta_ints.astype(jnp.bfloat16)
    by_group = spectra.reshape(count, far, GROUP, slice_cycles, width)
    ctf_group = ctf.reshape(count, far, GROUP, slice_cycles)
    lane = half // CHUNKS

    def piece_of(chunk, mask):
        part = lax.dynamic_index_in_dim(by_group, near ^ mask, 2, keepdims=False)
        part = part.reshape(count * mine, width)
        at = chunk * lane
        return jnp.concatenate(
            [part[:, at : at + lane], part[:, half + at : half + at + lane]], axis=-1
        )

    def meta_of(mask):
        ctf_part = lax.dynamic_index_in_dim(ctf_group, near ^ mask, 2, keepdims=False)
        meta = jnp.concatenate([ctf_part.reshape(count, mine), meta_ints], axis=-1)
        return jnp.pad(meta, ((0, 0), (0, 2 * lane - meta.shape[1])))

    got = []
    for chunk in range(CHUNKS):
        row = [piece_of(chunk, 0)]
        for mask in range(1, GROUP):
            piece = piece_of(chunk, mask)
            if chunk == 0:
                piece = jnp.concatenate([piece, meta_of(mask)], axis=0)
            row.append(swap(piece, "dom", mask))
        got.append(row)

    held = references
    mask = 2
    while mask < shards:
        held = jnp.concatenate([held, swap(held, "cls", mask)], axis=0)
        mask *= 2
    table = rotation_table(half, turns_all)
    weight = ctf.astype(jnp.float32) / noise_power[None, :]
    cw_low = ctf[:, :low_cycles].astype(jnp.float32) * weight[:, :low_cycles]
    log_evidence = log_evidence_of(spectra, weight, cw_low, held, swap(held, "cls", 1), table)

    metas = jnp.concatenate(
        [meta_of(0)] + [piece[count * mine :] for piece in got[0][1:]], axis=0
    )
    ctf_all = metas[:, :mine].astype(jnp.float32)
    ints = metas[:, mine : mine + 4].astype(jnp.int32)
    turn = ints[:, 0] * 16 + ints[:, 1]
    kind = ints[:, 2] * 16 + ints[:, 3]
    noise = lax.dynamic_index_in_dim(
        noise_power.reshape(far, GROUP, slice_cycles), near, 1, keepdims=False
    ).reshape(mine)
    wr = ctf_all / noise[None, :]
    cw = ctf_all * wr
    angle_at = jnp.arange(half, dtype=jnp.int32) * turn[:, None] % turns_all
    angle = angle_at.astype(jnp.float32) * (2.0 * math.pi / turns_all)
    cosv, sinv = jnp.cos(angle), jnp.sin(angle)
    shard, inside = kind // k_local, kind % k_local
    core_off = (shard % 2) ^ (cls % 2)
    place = core_off * (kinds // 2) + (shard // 2) * k_local + inside
    member = (jnp.arange(kinds, dtype=jnp.int32)[:, None] == place[None, :]).astype(jnp.float32)
    denom = jnp.dot(member, cw, precision=lax.Precision.HIGHEST)

    numer_parts = []
    for chunk in range(CHUNKS):
        here = slice(chunk * lane, (chunk + 1) * lane)
        keep, give = class_sums(
            got[chunk], place, wr[:, :, None], cosv[:, here], sinv[:, here], kinds
        )
        keep = keep.reshape(kinds // 2 * mine, 2 * lane)
        give = give.reshape(kinds // 2 * mine, 2 * lane)
        if chunk == 0:
            den = jnp.pad(denom, ((0, 0), (0, 2 * lane - mine)))
            keep = jnp.concatenate([keep, den[: kinds // 2]], axis=0)
            give = jnp.concatenate([give, den[kinds // 2 :]], axis=0)
        numer_parts.append((keep, swap(give, "cls", 1)))

    outs = []
    for chunk, (keep, get) in enumerate(numer_parts):
        total = keep + get
        body = total[: kinds // 2 * mine].reshape(kinds // 2, mine * 2 * lane)
        tail = total[kinds // 2 * mine :] if chunk == 0 else None
        if tail is not None:
            body = jnp.concatenate([body.reshape(kinds // 2, mine, 2 * lane), tail[:, None, :]], axis=1)
        else:
            body = body.reshape(kinds // 2, mine, 2 * lane)
        mask = shards // 2
        while mask >= 2:
            bit = (cls // mask) % 2
            size = body.shape[0] // 2
            own = lax.dynamic_slice_in_dim(body, bit * size, size, 0)
            other = lax.dynamic_slice_in_dim(body, (1 - bit) * size, size, 0)
            body = own + swap(other, "cls", mask)
            mask //= 2
        outs.append(body)

    finals = []
    for chunk, body in enumerate(outs):
        numer = body[:, :mine].reshape(k_local, far, slice_cycles, 2 * lane)
        if chunk == 0:
            den = body[:, mine, :mine].reshape(k_local, far, slice_cycles)
            den = jnp.pad(den[..., None, :], ((0, 0), (0, 0), (0, 0), (0, 2 * lane - slice_cycles)))
            numer = jnp.concatenate([numer, den], axis=2)
        mask = domains // 2
        while mask >= GROUP:
            bit = (dom // mask) % 2
            size = numer.shape[1] // 2
            own = lax.dynamic_slice_in_dim(numer, bit * size, size, 1)
            other = lax.dynamic_slice_in_dim(numer, (1 - bit) * size, size, 1)
            numer = own + swap(other, "dom", mask)
            mask //= 2
        finals.append(numer[:, 0])
    den = finals[0][:, slice_cycles, :slice_cycles]
    parts = [f[:, :slice_cycles] for f in finals]
    numer = jnp.concatenate([p[..., :lane] for p in parts] + [p[..., lane:] for p in parts], axis=-1)
    new_refs = numer / (den + 1.0)[:, :, None]
    return (new_refs, log_evidence)


def solution(mesh):
    return jax.shard_map(
        per_device,
        mesh=mesh,
        in_specs=(
            P(("dom", "cls"), None, None),
            P(("dom", "cls"), None),
            P(),
            P("cls", None, None),
            P(("dom", "cls"), None),
            P(("dom", "cls")),
            P(("dom", "cls")),
        ),
        out_specs=(P("cls", "dom", None), P(("dom", "cls"))),
        check_vma=False,
    )
```

```python
import functools
import math

import jax
import jax.numpy as jnp
from jax import lax
from jax.experimental import pallas as pl
from jax.experimental.pallas import tpu as pltpu
from jax.sharding import PartitionSpec as P


CHUNKS = 2
GROUP = 4
LANES = 128
PAD = 16
STEPS = 64.0
UNIT = math.log(2.0) / STEPS


def rotation_table(half, turns_all):
    freq = jnp.arange(half, dtype=jnp.int32)
    steps = jnp.arange(turns_all, dtype=jnp.int32)
    turns = freq[:, None] * steps[None, :] % turns_all
    angle = turns.astype(jnp.float32) * (2.0 * math.pi / turns_all)
    return jnp.concatenate([jnp.cos(angle), -jnp.sin(angle)], axis=0).astype(jnp.bfloat16)


def swap(value, axis, mask, name):
    size = lax.axis_size(axis)
    with jax.named_scope(name):
        return lax.ppermute(value, axis, [(i, i ^ mask) for i in range(size)])


def iota(shape, axis):
    return lax.broadcasted_iota(jnp.int32, shape, axis)


def whole(shape):
    return pl.BlockSpec(shape, lambda *_: (0,) * len(shape))


def cost(us):
    return pl.CostEstimate(flops=0, transcendentals=0, bytes_accessed=int(us * 3.6e6))


def score_kernel(
    low_ref, ctf_ref, noise_ref, first_ref, second_ref, table_ref, *refs, merge
):
    before = refs[:2] if merge else None
    outs = refs[2:3] if merge else refs[:2]
    image, image_sum, staged, classes, cross = refs[3 if merge else 2 :]
    count, cycles, width = low_ref.shape
    tiles = width // LANES
    pairs = tiles // 2
    kinds = cross.shape[0] // count
    part = first_ref.shape[0]
    ctf = ctf_ref[...].astype(jnp.float32)
    weight = ctf / noise_ref[...]
    power = ctf * weight
    eye = iota((cycles, LANES), 0) == iota((cycles, LANES), 1)
    for n in range(count):
        row = jnp.broadcast_to(weight[n : n + 1, :], (cycles, LANES))
        column = jnp.sum(jnp.where(eye, row, 0.0), axis=1, keepdims=True)
        low = low_ref[n].astype(jnp.float32)
        weighted = (column * low).astype(jnp.bfloat16).astype(jnp.float32)
        for f in range(tiles):
            image[f, n * cycles : (n + 1) * cycles, :] = weighted[:, f * LANES : (f + 1) * LANES]
        for f in range(pairs):
            re = weighted[:, f * LANES : (f + 1) * LANES]
            im = weighted[:, (f + pairs) * LANES : (f + pairs + 1) * LANES]
            image_sum[f, n * cycles : (n + 1) * cycles, :] = re + im
    for at, ref in ((0, first_ref), (part, second_ref)):
        for f in range(tiles):
            staged[f, at : at + part, :] = ref[:, f * LANES : (f + 1) * LANES].astype(jnp.float32)
    blocks = kinds // 8

    def arrange(r, norms):
        new = []
        for b in range(blocks):
            rows = pl.ds(b * 8 * cycles + r, 8, stride=cycles)
            square = jnp.zeros((8, LANES), jnp.float32)
            for f in range(pairs):
                re = staged[f, rows, :]
                im = staged[f + pairs, rows, :]
                at = pl.ds(pl.multiple_of(r * kinds + b * 8, 8), 8)
                classes[3 * f, at, :] = re
                classes[3 * f + 1, at, :] = re - im
                classes[3 * f + 2, at, :] = re + im
                square = square + (re * re + im * im)
            norm = jnp.sum(square, axis=1, keepdims=True)
            new.append(jnp.where(iota((8, LANES), 1) == r, norm, norms[b]))
        return tuple(new)

    zero = jnp.zeros((8, LANES), jnp.float32)
    norms = lax.fori_loop(0, cycles, arrange, (zero,) * blocks)
    group = 4
    for f in range(pairs):

        def particles(g, _):
            def cycle(r, sums):
                new = list(sums)
                for i in range(group):
                    row = pl.ds((g * group + i) * cycles + r, 8, stride=0)
                    a_sum, a_im, a_re = image_sum[f, row, :], image[f + pairs, row, :], image[f, row, :]
                    for b in range(blocks):
                        at = pl.ds(pl.multiple_of(r * kinds + b * 8, 8), 8)
                        j = 3 * (i * blocks + b)
                        new[j] = new[j] + classes[3 * f, at, :] * a_sum
                        new[j + 1] = new[j + 1] + classes[3 * f + 1, at, :] * a_im
                        new[j + 2] = new[j + 2] + classes[3 * f + 2, at, :] * a_re
                return tuple(new)

            sums = lax.fori_loop(0, cycles, cycle, (zero,) * (3 * group * blocks), unroll=2)
            for i in range(group):
                for b in range(blocks):
                    s1, s2, s3 = sums[3 * (i * blocks + b) : 3 * (i * blocks + b) + 3]
                    at = pl.ds(pl.multiple_of((g * group + i) * kinds + b * 8, 8), 8)
                    cross[at, f * LANES : (f + 1) * LANES] = s1 - s2
                    cross[at, (f + pairs) * LANES : (f + pairs + 1) * LANES] = s1 - s3
            return 0

        lax.fori_loop(0, count // group, particles, 0)
    step = 4
    for g in range(count // step):
        score = jnp.dot(
            cross[g * step * kinds : (g + 1) * step * kinds, :].astype(jnp.bfloat16),
            table_ref[...],
            preferred_element_type=jnp.float32,
        )
        for i in range(step):
            n = g * step + i
            low = cycles - 1
            mine = []
            for b in range(blocks):
                row = jnp.broadcast_to(power[n : n + 1, :], (8, LANES))
                row = jnp.where(iota((8, LANES), 1) <= low, row, 0.0)
                energy = jnp.sum(row * norms[b], axis=1, keepdims=True)
                at = i * kinds + b * 8
                mine.append(score[at : at + 8] - 0.5 * energy)
            mine = jnp.concatenate(mine, axis=0)
            top = jnp.max(mine, axis=(0, 1), keepdims=True)
            if merge:
                top_before, total_before = before[0][n : n + 1, :], before[1][n : n + 1, :]
                top = jnp.maximum(top, jnp.max(top_before, axis=1, keepdims=True))
            total = jnp.sum(jnp.exp(mine - top), axis=(0, 1), keepdims=True)
            if merge:
                total = total + total_before * jnp.exp(top_before - top)
                outs[0][n : n + 1, :] = jnp.broadcast_to(top + jnp.log(total), (1, LANES))
            else:
                outs[0][n : n + 1, :] = jnp.broadcast_to(top, (1, LANES))
                outs[1][n : n + 1, :] = jnp.broadcast_to(total, (1, LANES))


def score(spectra, ctf, noise, first, second, table, before, name):
    count, _, width = spectra.shape
    cycles = first.shape[1]
    kinds = 2 * first.shape[0]
    row = jax.ShapeDtypeStruct((count, LANES), jnp.float32)
    merge = before is not None
    part = (kinds // 2 * cycles, width)
    outs = pl.pallas_call(
        functools.partial(score_kernel, merge=merge),
        out_shape=row if merge else (row, row),
        grid=(1,),
        in_specs=[
            pl.BlockSpec((count, cycles, width), lambda i: (0, 0, 0)),
            whole(ctf.shape),
            whole(noise.shape),
            whole(part),
            whole(part),
            whole(table.shape),
        ]
        + [whole(row.shape)] * (2 if merge else 0),
        out_specs=whole(row.shape) if merge else (whole(row.shape),) * 2,
        scratch_shapes=[
            pltpu.VMEM((width // LANES, count * cycles, LANES), jnp.float32),
            pltpu.VMEM((width // LANES // 2, count * cycles, LANES), jnp.float32),
            pltpu.VMEM((width // LANES, kinds * cycles, LANES), jnp.float32),
            pltpu.VMEM((width // LANES // 2 * 3, kinds * cycles, LANES), jnp.float32),
            pltpu.VMEM((count * kinds, width), jnp.float32),
        ],
        cost_estimate=cost(7),
        name=name,
    )(spectra, ctf, noise, first.reshape(part), second.reshape(part), table, *(before or ()))
    return outs


def pieces_kernel(near_ref, image_ref, meta_ref, *outs):
    rows = outs[1].shape[0]
    x = image_ref[...].reshape(rows, image_ref.shape[-1])
    lane = outs[1].shape[1] // 2
    half = x.shape[1] // 2
    for chunk, out in enumerate(outs):
        out[:rows, :lane] = x[:, chunk * lane : (chunk + 1) * lane]
        out[:rows, lane:] = x[:, half + chunk * lane : half + (chunk + 1) * lane]
    outs[0][rows:, :] = meta_ref[...]


def image_spec(view, lanes, mask, lane_block):
    if len(view.shape) == 5:
        count, far, _, cycles, _ = view.shape
        return pl.BlockSpec(
            (count, far, 1, cycles, lanes), lambda i, near: (0, 0, near[0] ^ mask, 0, lane_block)
        )
    return pl.BlockSpec((1, view.shape[1], lanes), lambda i, near: (near[0] ^ mask, 0, lane_block))


def pieces(near, view, meta, rows, mask):
    width = view.shape[-1]
    shapes = [
        jax.ShapeDtypeStruct((rows + (meta.shape[0] if c == 0 else 0), width // CHUNKS), view.dtype)
        for c in range(CHUNKS)
    ]
    return pl.pallas_call(
        pieces_kernel,
        out_shape=shapes,
        grid_spec=pltpu.PrefetchScalarGridSpec(
            num_scalar_prefetch=1,
            grid=(1,),
            in_specs=[image_spec(view, width, mask, 0), whole(meta.shape)],
            out_specs=[whole(s.shape) for s in shapes],
        ),
        cost_estimate=cost(0.7),
        name=f"pieces{mask}",
    )(near, view, meta)


def sums_kernel(
    near_ref, place_ref, power_place_ref, meta_ref, noise_ref, cos_ref, sin_ref, re_ref, im_ref,
    *refs, cycles, slice_cycles, with_power,
):
    given = refs[: GROUP - 1]
    keep_ref, give_ref, total, powers = refs[GROUP - 1 :]
    half = re_ref.shape[-1]
    particles = cos_ref.shape[0]
    count = particles // GROUP
    total[...] = jnp.zeros_like(total)
    powers[...] = jnp.zeros_like(powers)
    own_re = re_ref[...].reshape(count * cycles, half)
    own_im = im_ref[...].reshape(count * cycles, half)
    r = iota((cycles, LANES), 0)
    lane = r // slice_cycles * (GROUP * slice_cycles) + near_ref[0] * slice_cycles + r % slice_cycles
    pick = iota((cycles, LANES), 1) == lane
    batch = 4

    def one(n, source):
        ctf = meta_ref[n : n + 1, :LANES].astype(jnp.float32)
        weight_row = ctf / noise_ref[...]
        weight = jnp.sum(
            jnp.where(pick, jnp.broadcast_to(weight_row, pick.shape), 0.0), axis=1, keepdims=True
        )
        at = (n % count) * cycles
        if source is None:
            x_re = own_re[at : at + cycles].astype(jnp.float32)
            x_im = own_im[at : at + cycles].astype(jnp.float32)
        else:
            x_re = source[at : at + cycles, :half].astype(jnp.float32)
            x_im = source[at : at + cycles, half:].astype(jnp.float32)
        cosv, sinv = cos_ref[n : n + 1, :], sin_ref[n : n + 1, :]
        re = weight * (x_re * cosv - x_im * sinv)
        im = weight * (x_re * sinv + x_im * cosv)
        return re, im, ctf * weight_row

    for g in range(GROUP):
        source = None if g == 0 else given[g - 1]
        for start in range(g * count, (g + 1) * count, batch):
            done = [one(n, source) for n in range(start, start + batch)]
            for n, (re, im, power) in zip(range(start, start + batch), done):
                at = pl.ds(pl.multiple_of(place_ref[n], PAD), cycles)
                total[at, :half] += re
                total[at, half:] += im
                if with_power:
                    powers[pl.ds(power_place_ref[n], 1), :] += power
    size = keep_ref.shape[0]
    if with_power:
        blocks = powers.shape[0] // PAD
        block = total.shape[0] // blocks
        for b in range(blocks):
            total[(b + 1) * block - PAD : (b + 1) * block, :LANES] = powers[b * PAD : (b + 1) * PAD]
    keep_ref[...] = total[:size]
    give_ref[...] = total[size:]


def class_sums(near, view, chunk, given, place, power_place, meta, noise, cosv, sinv, cycles, rows, shards, with_power):
    lane = cosv.shape[1]
    chunks = view.shape[-1] // 2 // lane
    slice_cycles = view.shape[3] if len(view.shape) == 5 else cycles * GROUP // LANES
    out = jax.ShapeDtypeStruct((rows, 2 * lane), jnp.float32)
    smem = pl.BlockSpec(memory_space=pltpu.SMEM)
    piece = (meta.shape[0] // GROUP * cycles, 2 * lane)
    return pl.pallas_call(
        functools.partial(
            sums_kernel, cycles=cycles, slice_cycles=slice_cycles, with_power=with_power
        ),
        out_shape=(out, out),
        grid_spec=pltpu.PrefetchScalarGridSpec(
            num_scalar_prefetch=1,
            grid=(1,),
            in_specs=[
                smem,
                smem,
                whole(meta.shape),
                whole(noise.shape),
                whole(cosv.shape),
                whole(sinv.shape),
                image_spec(view, lane, 0, chunk),
                image_spec(view, lane, 0, chunks + chunk),
            ]
            + [whole(piece)] * (GROUP - 1),
            out_specs=(whole(out.shape),) * 2,
            scratch_shapes=[
                pltpu.VMEM((2 * rows, 2 * lane), jnp.float32),
                pltpu.VMEM((shards * PAD, LANES), jnp.float32),
            ],
        ),
        cost_estimate=cost(2.5),
        name=f"class_sums{chunk}",
    )(near, place, power_place, meta, noise, cosv, sinv, view, view, *given)


def spans(rows):
    return [(at, min(LANES, rows - at)) for at in range(0, rows, LANES)]


def encode(value, out, at):
    rows = value.shape[0]
    codes = jnp.zeros((PAD, LANES), jnp.float32)
    for i, (start, size) in enumerate(spans(rows)):
        x = value[start : start + size]
        top = jnp.maximum(jnp.max(jnp.abs(x), axis=1, keepdims=True), 1e-30)
        code = jnp.floor(jnp.log(top) / UNIT) + 1.0
        scaled = x * (jnp.exp(-code * UNIT) * 32767.0)
        scaled = jnp.clip(jnp.round(scaled), -32767.0, 32767.0)
        out[at + start : at + start + size, :] = scaled.astype(jnp.int32).astype(jnp.int16)
        eye = iota((size, LANES), 0) == iota((size, LANES), 1)
        row = jnp.sum(jnp.where(eye, code, 0.0), axis=0, keepdims=True)
        codes = jnp.where(iota((PAD, LANES), 0) == i, row, codes)
    for f in range(out.shape[1] // LANES):
        out[at + rows : at + rows + PAD, f * LANES : (f + 1) * LANES] = codes.astype(
            jnp.int32
        ).astype(jnp.int16)


def decode(ref, at, rows):
    codes = ref[at + rows : at + rows + PAD, :LANES].astype(jnp.int32).astype(jnp.float32)
    parts = []
    for i, (start, size) in enumerate(spans(rows)):
        eye = iota((size, LANES), 0) == iota((size, LANES), 1)
        row = jnp.broadcast_to(codes[i : i + 1], (size, LANES))
        code = jnp.sum(jnp.where(eye, row, 0.0), axis=1, keepdims=True)
        x = ref[at + start : at + start + size, :].astype(jnp.int32).astype(jnp.float32)
        parts.append(x * (jnp.exp(code * UNIT) * (1.0 / 32767.0)))
    return jnp.concatenate(parts, axis=0)


def shard_kernel(bit_ref, keep_ref, get_ref, own_ref, code_ref, *, coded):
    parts, rows, _ = own_ref.shape
    if coded:
        for p in range(2 * parts):
            keep_ref[p] = keep_ref[p] + decode(get_ref.at[p], 0, rows)
    bit = bit_ref[0]
    for p in range(parts):
        mine, other = bit * parts + p, (1 - bit) * parts + p
        if coded:
            encode(keep_ref[other], code_ref.at[p], 0)
            own_ref[p] = keep_ref[mine]
        else:
            encode(keep_ref[other] + get_ref[other], code_ref.at[p], 0)
            own_ref[p] = keep_ref[mine] + get_ref[mine]


def split_shards(bit, keep, get, name):
    parts, rows, width = keep.shape
    parts = parts // 2
    own = jax.ShapeDtypeStruct((parts, rows, width), jnp.float32)
    code = jax.ShapeDtypeStruct((parts, rows + PAD, width), jnp.int16)
    return pl.pallas_call(
        functools.partial(shard_kernel, coded=get.dtype == jnp.int16),
        out_shape=(own, code),
        grid=(1,),
        in_specs=[
            pl.BlockSpec(memory_space=pltpu.SMEM),
            whole(keep.shape),
            whole(get.shape),
        ],
        out_specs=(whole(own.shape), whole(code.shape)),
        cost_estimate=cost(1.5),
        name=name,
    )(bit, keep, get)


def cycle_kernel(bit_ref, keep_ref, get_ref, own_ref, code_ref, total, other, *, classes, cycles):
    rows = keep_ref.shape[0]
    total[...] = keep_ref[...] + decode(get_ref, 0, rows)
    bit = bit_ref[0]
    half = cycles // 2
    for k in range(classes):
        mine = pl.ds(pl.multiple_of(k * cycles + bit * half, 8), half)
        theirs = pl.ds(pl.multiple_of(k * cycles + (1 - bit) * half, 8), half)
        own_ref[k * half : (k + 1) * half, :] = total[mine, :]
        other[k * half : (k + 1) * half, :] = total[theirs, :]
    if rows > classes * cycles:
        own_ref[classes * half :, :] = total[classes * cycles :, :]
        other[classes * half :, :] = total[classes * cycles :, :]
    encode(other[...], code_ref, 0)


def split_cycles(bit, keep, get, classes, cycles, name):
    rows, width = keep.shape
    left = rows - classes * cycles // 2
    own = jax.ShapeDtypeStruct((left, width), jnp.float32)
    code = jax.ShapeDtypeStruct((left + PAD, width), jnp.int16)
    return pl.pallas_call(
        functools.partial(cycle_kernel, classes=classes, cycles=cycles),
        out_shape=(own, code),
        grid=(1,),
        in_specs=[
            pl.BlockSpec(memory_space=pltpu.SMEM),
            whole(keep.shape),
            whole(get.shape),
        ],
        out_specs=(whole(own.shape), whole(code.shape)),
        scratch_shapes=[
            pltpu.VMEM((rows, width), jnp.float32),
            pltpu.VMEM((left, width), jnp.float32),
        ],
        cost_estimate=cost(1),
        name=name,
    )(bit, keep, get)


def final_kernel(dom_ref, *refs):
    keeps, gets, out = refs[:CHUNKS], refs[CHUNKS : 2 * CHUNKS], refs[2 * CHUNKS]
    classes, cycles, width = out.shape
    rows = classes * cycles
    lane = width // 2 // CHUNKS
    sums = [k[...] + decode(g, 0, k.shape[0]) for k, g in zip(keeps, gets)]
    r = iota((cycles, LANES), 0)
    pick = iota((cycles, LANES), 1) == dom_ref[0] * cycles + r
    for k in range(classes):
        row = jnp.broadcast_to(sums[0][rows + k : rows + k + 1, :LANES], pick.shape)
        denom = jnp.sum(jnp.where(pick, row, 0.0), axis=1, keepdims=True) + 1.0
        for chunk in range(CHUNKS):
            numer = sums[chunk][k * cycles : (k + 1) * cycles, :] / denom
            out[k, :, chunk * lane : (chunk + 1) * lane] = numer[:, :lane]
            out[k, :, width // 2 + chunk * lane : width // 2 + (chunk + 1) * lane] = numer[:, lane:]


def finish(dom, keeps, gets, classes, cycles, width):
    out = (classes, cycles, width)
    return pl.pallas_call(
        final_kernel,
        out_shape=jax.ShapeDtypeStruct(out, jnp.float32),
        grid=(1,),
        in_specs=[pl.BlockSpec(memory_space=pltpu.SMEM)]
        + [whole(v.shape) for v in (*keeps, *gets)],
        out_specs=whole(out),
        cost_estimate=cost(1),
        name="finish",
    )(dom, *keeps, *gets)


def decoded(keep, get):
    rows = keep.shape[0]
    code = get[rows:, :LANES].astype(jnp.float32).reshape(-1)[:rows]
    scale = jnp.exp(code * UNIT) * (1.0 / 32767.0)
    return keep + get[:rows].astype(jnp.float32) * scale[:, None]


def per_device(spectra, ctf, noise_power, references, owner, sub_class, rotation):
    count, cycles, width = spectra.shape
    half = width // 2
    k_local = references.shape[0]
    turns_all = width
    domains, shards = lax.axis_size("dom"), lax.axis_size("cls")
    dom, cls = lax.axis_index("dom"), lax.axis_index("cls")
    far = domains // GROUP
    slice_cycles = cycles // domains
    mine = cycles // GROUP
    near = (dom & (GROUP - 1)).reshape(1)
    lane = half // CHUNKS
    rows = count * mine
    noise = noise_power.reshape(1, cycles)

    shard, inside = owner[:, 0], sub_class
    ints = jnp.stack([rotation >> 4, rotation & 15, shard, inside], axis=-1).astype(jnp.bfloat16)
    meta = jnp.concatenate([ctf, ints], axis=-1)
    meta = jnp.pad(meta, ((0, 0), (0, 2 * lane - meta.shape[1])))
    view = spectra.reshape(count, far, GROUP, slice_cycles, width)
    if slice_cycles % 16:
        view = jnp.moveaxis(view, 2, 0).reshape(GROUP, rows, width)
    sent = [pieces(near, view, meta, rows, mask) for mask in range(1, GROUP)]
    got = [
        [swap(sent[m - 1][c], "dom", m, f"raw_{c}_{m}") for m in range(1, GROUP)]
        for c in range(CHUNKS)
    ]

    held, mask = references, 2
    own_side, other_side = references, None
    while mask < shards:
        new = swap(held, "cls", mask, f"refs_{mask}")
        other_side = new if other_side is None else jnp.concatenate([other_side, new], axis=0)
        held = jnp.concatenate([held, new], axis=0) if 2 * mask < shards else held
        mask *= 2
    table = rotation_table(half, turns_all)
    before = score(
        spectra, ctf, noise, own_side, swap(own_side, "cls", 1, "refs_near"), table, None, "score_near"
    )
    far_refs = swap(other_side, "cls", 1, "refs_far")
    log_evidence = score(spectra, ctf, noise, other_side, far_refs, table, before, "score_far")
    log_evidence = log_evidence[:, 0]

    metas = jnp.concatenate([meta] + [piece[rows:] for piece in got[0]], axis=0)
    ints = metas[:, cycles : cycles + 4].astype(jnp.int32)
    turn = ints[:, 0] * 16 + ints[:, 1]
    block = ((ints[:, 2] ^ cls) & 1) * (shards // 2) + (ints[:, 2] >> 1)
    angle_at = jnp.arange(half, dtype=jnp.int32) * turn[:, None] % turns_all
    angle = angle_at.astype(jnp.float32) * (2.0 * math.pi / turns_all)
    cosv, sinv = jnp.cos(angle), jnp.sin(angle)

    folded = []
    for chunk in range(CHUNKS):
        here = slice(chunk * lane, (chunk + 1) * lane)
        size = k_local * mine + (PAD if chunk == 0 else 0)
        place = block * size + ints[:, 3] * mine
        power_place = block * PAD + ints[:, 3]
        keep, give = class_sums(
            near, view, chunk, got[chunk], place, power_place, metas, noise,
            cosv[:, here], sinv[:, here], mine, shards // 2 * size, shards, chunk == 0,
        )
        get = swap(give, "cls", 1, f"core_{chunk}")
        shape = (shards // 2, size, 2 * lane)
        keep, get = keep.reshape(shape), get.reshape(shape)
        mask = shards // 2
        while mask >= 2:
            bit = ((cls // mask) & 1).reshape(1)
            keep, code = split_shards(bit, keep, get, f"shards_{chunk}_{mask}")
            get = swap(code, "cls", mask, f"shard_{chunk}_{mask}")
            mask //= 2
        folded.append((keep[0], get[0]))

    ends = []
    span = mine
    for chunk, (keep, get) in enumerate(folded):
        span, mask = mine, domains // 2
        while mask >= GROUP and span % 32 == 0:
            bit = ((dom // mask) & 1).reshape(1)
            keep, code = split_cycles(bit, keep, get, k_local, span, f"cycles_{chunk}_{mask}")
            get = swap(code, "dom", mask, f"cycle_{chunk}_{mask}")
            span, mask = span // 2, mask // 2
        ends.append((keep, get))
    keeps, gets = zip(*ends)
    if mask < GROUP:
        new_refs = finish(dom.reshape(1), keeps, gets, k_local, slice_cycles, width)
        return (new_refs, log_evidence)

    numers = []
    for chunk, (keep, get) in enumerate(ends):
        total = decoded(keep, get)
        numer = total[: k_local * span].reshape(k_local, span, 2 * lane)
        power = total[k_local * span :]
        at, left = mask, span
        while at >= GROUP:
            bit = (dom // at) & 1
            left = left // 2
            own = lax.dynamic_slice_in_dim(numer, bit * left, left, 1)
            other = lax.dynamic_slice_in_dim(numer, (1 - bit) * left, left, 1)
            numer = own + swap(other, "dom", at, f"cycle_{chunk}_{at}")
            if chunk == 0:
                power = power + swap(power, "dom", at, f"power_{at}")
            at //= 2
        if chunk == 0:
            denom = lax.dynamic_slice_in_dim(power[:k_local, :LANES], dom * left, left, 1)
        numers.append(numer)
    numer = jnp.concatenate([p[..., :lane] for p in numers] + [p[..., lane:] for p in numers], axis=-1)
    return (numer / (denom + 1.0)[:, :, None], log_evidence)


def solution(mesh):
    return jax.shard_map(
        per_device,
        mesh=mesh,
        in_specs=(
            P(("dom", "cls"), None, None),
            P(("dom", "cls"), None),
            P(),
            P("cls", None, None),
            P(("dom", "cls"), None),
            P(("dom", "cls")),
            P(("dom", "cls")),
        ),
        out_specs=(P("cls", "dom", None), P(("dom", "cls"))),
        check_vma=False,
    )
```

```python
import functools
import math

import jax
import jax.numpy as jnp
from jax import lax
from jax.experimental import pallas as pl
from jax.experimental.pallas import tpu as pltpu
from jax.sharding import PartitionSpec as P


CHUNKS = 2
GROUP = 4
FAR_CALLS = 1
LANES = 128
PAD = 16
STEPS = 64.0
UNIT = math.log(2.0) / STEPS


def table_kernel(out_ref):
    width, turns_all = out_ref.shape
    half = width // 2
    step = 64
    for at in range(0, half, step):
        turns = (iota((step, turns_all), 0) + at) * iota((step, turns_all), 1) & (turns_all - 1)
        angle = turns.astype(jnp.float32) * (2.0 * math.pi / turns_all)
        out_ref[at : at + step, :] = jnp.cos(angle).astype(jnp.bfloat16)
        out_ref[half + at : half + at + step, :] = (-jnp.sin(angle)).astype(jnp.bfloat16)


def rotation_table(width):
    return pl.pallas_call(
        table_kernel,
        out_shape=pltpu.VMEM((width, width), jnp.bfloat16),
        out_specs=HERE,
        cost_estimate=cost(2),
        compiler_params=room(((width, width), 4)),
        name="table",
    )()


def held_near(*values):
    return [pltpu.with_memory_space_constraint(v, pltpu.VMEM) for v in values]


def held_far(*values):
    return [pltpu.with_memory_space_constraint(v, pltpu.HBM) for v in values]


def swap(value, axis, mask):
    size = lax.axis_size(axis)
    return lax.ppermute(value, axis, [(i, i ^ mask) for i in range(size)])


def iota(shape, axis):
    return lax.broadcasted_iota(jnp.int32, shape, axis)


HERE = pl.BlockSpec(memory_space=pltpu.VMEM)
SCALARS = pl.BlockSpec(memory_space=pltpu.SMEM)
THERE = pl.BlockSpec(memory_space=pltpu.HBM)


def room(*arrays):
    size = sum(math.prod(shape) * bits for shape, bits in arrays)
    return pltpu.CompilerParams(vmem_limit_bytes=size + (8 << 20))


def cost(us):
    return pl.CostEstimate(flops=0, transcendentals=0, bytes_accessed=int(us * 3.6e6))


def score_kernel(
    image_ref, ctf_ref, noise_ref, first_ref, second_ref, table_ref, *refs, merge, start
):
    before = refs[:2] if merge else None
    row_ref = refs[2] if merge else None
    outs = refs[3:4] if merge else refs[:2]
    low_ref, image, image_sum, staged, classes, cross, sem = refs[4 if merge else 2 :]
    count, cycles, width = low_ref.shape
    fetch = pltpu.make_async_copy(image_ref.at[pl.ds(start, count), :cycles, :], low_ref, sem)
    fetch.start()
    tiles = width // LANES
    pairs = tiles // 2
    kinds = cross.shape[0] // count
    part = first_ref.shape[0]
    ctf = ctf_ref[start : start + count, :].astype(jnp.float32)
    weight = ctf / noise_ref[...]
    power = ctf * weight
    eye = iota((cycles, LANES), 0) == iota((cycles, LANES), 1)
    fetch.wait()
    for n in range(count):
        row = jnp.broadcast_to(weight[n : n + 1, :], (cycles, LANES))
        column = jnp.sum(jnp.where(eye, row, 0.0), axis=1, keepdims=True)
        low = low_ref[n].astype(jnp.float32)
        weighted = (column * low).astype(jnp.bfloat16).astype(jnp.float32)
        for f in range(tiles):
            image[f, n * cycles : (n + 1) * cycles, :] = weighted[:, f * LANES : (f + 1) * LANES]
        for f in range(pairs):
            re = weighted[:, f * LANES : (f + 1) * LANES]
            im = weighted[:, (f + pairs) * LANES : (f + pairs + 1) * LANES]
            image_sum[f, n * cycles : (n + 1) * cycles, :] = re + im
    for at, ref in ((0, first_ref), (part, second_ref)):
        for f in range(tiles):
            staged[f, at : at + part, :] = ref[:, f * LANES : (f + 1) * LANES].astype(jnp.float32)
    blocks = kinds // 8
    zero = jnp.zeros((8, LANES), jnp.float32)
    norms = []
    for b in range(blocks):
        square = jnp.zeros((cycles, 8, LANES), jnp.float32)
        for f in range(pairs):
            rows = pl.ds(b * 8 * cycles, 8 * cycles)
            re = jnp.swapaxes(staged[f, rows, :].reshape(8, cycles, LANES), 0, 1)
            im = jnp.swapaxes(staged[f + pairs, rows, :].reshape(8, cycles, LANES), 0, 1)
            classes[3 * f, :, b * 8 : b * 8 + 8, :] = re
            classes[3 * f + 1, :, b * 8 : b * 8 + 8, :] = re - im
            classes[3 * f + 2, :, b * 8 : b * 8 + 8, :] = re + im
            square = square + (re * re + im * im)
        norm = zero
        for r in range(cycles):
            total = jnp.sum(square[r], axis=1, keepdims=True)
            norm = jnp.where(iota((8, LANES), 1) == r, total, norm)
        norms.append(norm)
    group = 2
    for f in range(pairs):

        def particles(g, _):
            def cycle(r, sums):
                new = list(sums)
                for i in range(group):
                    row = pl.ds((g * group + i) * cycles + r, 8, stride=0)
                    a_sum, a_im, a_re = image_sum[f, row, :], image[f + pairs, row, :], image[f, row, :]
                    for b in range(blocks):
                        at = slice(b * 8, b * 8 + 8)
                        j = 3 * (i * blocks + b)
                        new[j] = new[j] + classes[3 * f, r, at, :] * a_sum
                        new[j + 1] = new[j + 1] + classes[3 * f + 1, r, at, :] * a_im
                        new[j + 2] = new[j + 2] + classes[3 * f + 2, r, at, :] * a_re
                return tuple(new)

            sums = lax.fori_loop(0, cycles, cycle, (zero,) * (3 * group * blocks), unroll=4)
            for i in range(group):
                for b in range(blocks):
                    s1, s2, s3 = sums[3 * (i * blocks + b) : 3 * (i * blocks + b) + 3]
                    at = pl.ds(pl.multiple_of((g * group + i) * kinds + b * 8, 8), 8)
                    cross[at, f * LANES : (f + 1) * LANES] = s1 - s2
                    cross[at, (f + pairs) * LANES : (f + pairs + 1) * LANES] = s1 - s3
            return 0

        lax.fori_loop(0, count // group, particles, 0)
    scores = jnp.dot(
        cross[...].astype(jnp.bfloat16), table_ref[...], preferred_element_type=jnp.float32
    )
    cross[...] = scores
    inner = iota((8, LANES), 1) < cycles
    row = row_ref[...] if merge else None
    for n in range(count):
            mine = []
            for b in range(blocks):
                powers = jnp.where(inner, jnp.broadcast_to(power[n : n + 1, :], (8, LANES)), 0.0)
                energy = jnp.sum(powers * norms[b], axis=1, keepdims=True)
                at = n * kinds + b * 8
                mine.append(cross[at : at + 8, :] - 0.5 * energy)
            mine = jnp.concatenate(mine, axis=0)
            top = jnp.max(mine, axis=(0, 1), keepdims=True)
            if merge:
                top_before, total_before = before[0][start + n : start + n + 1, :], before[1][start + n : start + n + 1, :]
                top = jnp.maximum(top, jnp.max(top_before, axis=1, keepdims=True))
            total = jnp.sum(jnp.exp(mine - top), axis=(0, 1), keepdims=True)
            if merge:
                total = total + (total_before * jnp.exp(top_before - top))[:, :1]
                here = iota(row.shape, 1) == start + n
                row = jnp.where(here, jnp.broadcast_to(top + jnp.log(total), row.shape), row)
            else:
                outs[0][n : n + 1, :] = jnp.broadcast_to(top, (1, LANES))
                outs[1][n : n + 1, :] = jnp.broadcast_to(total, (1, LANES))
    if merge:
        outs[0][...] = row


def score(spectra, ctf, noise, first, second, table, before, start, count):
    width = spectra.shape[2]
    cycles = first.shape[1]
    kinds = 2 * first.shape[0]
    merge = before is not None
    each = pltpu.VMEM((count, LANES), jnp.float32)
    row = jax.ShapeDtypeStruct((1, ctf.shape[0]), jnp.float32)
    part = (kinds // 2 * cycles, width)
    outs = pl.pallas_call(
        functools.partial(score_kernel, merge=merge, start=start),
        out_shape=row if merge else (each, each),
        in_specs=[THERE] + [HERE] * (8 if merge else 5),
        out_specs=HERE if merge else (HERE, HERE),
        scratch_shapes=[
            pltpu.VMEM((count, cycles, width), spectra.dtype),
            pltpu.VMEM((width // LANES, count * cycles, LANES), jnp.float32),
            pltpu.VMEM((width // LANES // 2, count * cycles, LANES), jnp.float32),
            pltpu.VMEM((width // LANES, kinds * cycles, LANES), jnp.float32),
            pltpu.VMEM((width // LANES // 2 * 3, cycles, kinds, LANES), jnp.float32),
            pltpu.VMEM((count * kinds, width), jnp.float32),
            pltpu.SemaphoreType.DMA,
        ],
        cost_estimate=cost(8),
        compiler_params=room(
            ((count * cycles, width), 10),
            ((kinds * cycles, width), 12),
            ((count * kinds, width), 8),
            (table.shape, 2),
        ),
    )(
        *held_far(spectra), ctf, noise, *held_near(first.reshape(part), second.reshape(part), table),
        *(before or ()),
    )
    return outs


def part_of(view_ref, top, near):
    if view_ref.shape[0] == 2:
        return view_ref.at[top, near]
    return view_ref.at[:, top, near]


def column(row):
    size = row.shape[1]
    eye = iota((size, size), 0) == iota((size, size), 1)
    return jnp.sum(jnp.where(eye, jnp.broadcast_to(row, (size, size)), 0.0), axis=1, keepdims=True)


def pieces_kernel(near_ref, top_ref, view_ref, *refs, chunk):
    outs, sems = refs[-GROUP:-1], refs[-1]
    if chunk == 0:
        ctf_ref, owner_ref, sub_ref, turn_ref, meta_ref = refs[:5]
        outs = refs[5 : 5 + GROUP - 1]
        ctf_here, owner_here, sub_here, turn_here, small, sems = refs[5 + GROUP - 1 :]
        fetches = [
            pltpu.make_async_copy(there, here, small.at[i])
            for i, (there, here) in enumerate(
                ((ctf_ref, ctf_here), (owner_ref, owner_here), (sub_ref, sub_here), (turn_ref, turn_here))
            )
        ]
        for fetch in fetches:
            fetch.start()
    count = view_ref.shape[2] if view_ref.shape[0] == 2 else view_ref.shape[0]
    copies = [
        pltpu.make_async_copy(
            part_of(view_ref, top_ref[0] ^ (1 - chunk), near_ref[0] ^ (i + 1)),
            out.at[pl.ds(0, count)],
            sems.at[i],
        )
        for i, out in enumerate(outs)
    ]
    for copy in copies:
        copy.start()
    if chunk == 0:
        for fetch in fetches:
            fetch.wait()
        cycles = ctf_ref.shape[1]
        turn = turn_here[...]
        shape = (count, meta_ref.shape[1] - cycles)
        at = iota(shape, 1)
        rest = jnp.where(at == 0, column((turn >> 4).astype(jnp.float32)), 0.0)
        rest = jnp.where(at == 1, column((turn & 15).astype(jnp.float32)), rest)
        rest = jnp.where(at == 2, column(owner_here[...].astype(jnp.float32)), rest)
        rest = jnp.where(at == 3, column(sub_here[...].astype(jnp.float32)), rest)
        meta_ref[:, :cycles] = ctf_here[...]
        meta_ref[:, cycles:] = rest.astype(jnp.bfloat16)
        for out in outs:
            out[count, :, :] = jnp.zeros(out.shape[1:], out.dtype)
            out[count, :, : meta_ref.shape[1]] = meta_ref[...]
    for copy in copies:
        copy.wait()


def pieces(near, top, view, chunk, others):
    count, width = view.shape[2] if view.shape[0] == 2 else view.shape[0], view.shape[-1]
    out = pltpu.VMEM((count + (chunk == 0), PAD, width), view.dtype)
    shapes = [out] * (GROUP - 1)
    scratch = [pltpu.SemaphoreType.DMA((GROUP - 1,))]
    if chunk == 0:
        ctf = others[0]
        shapes = [pltpu.VMEM((count, 2 * ctf.shape[1]), view.dtype)] + shapes
        scratch = [
            pltpu.VMEM(ctf.shape, ctf.dtype),
            pltpu.VMEM((1, count), jnp.int32),
            pltpu.VMEM((1, count), jnp.int32),
            pltpu.VMEM((1, count), jnp.int32),
            pltpu.SemaphoreType.DMA((4,)),
        ] + scratch
    return pl.pallas_call(
        functools.partial(pieces_kernel, chunk=chunk),
        out_shape=shapes,
        in_specs=[SCALARS] * 2 + [THERE] * (1 + len(others)),
        out_specs=[HERE] * len(shapes),
        scratch_shapes=scratch,
        cost_estimate=cost(1.5),
        compiler_params=room(((count * PAD, width), 2 * GROUP)),
    )(near, top, *held_far(view, *others))


def sums_kernel(
    near_ref, top_ref, cls_ref, *refs, slice_cycles, far, chunk, shards,
):
    if chunk == 0:
        meta_ref, refs = refs[0], refs[1:]
    noise_ref, view_ref, refs = refs[0], refs[1], refs[2:]
    given, refs = refs[: GROUP - 1], refs[GROUP - 1 :]
    if chunk == 0:
        keep_ref, give_ref = refs[:2]
        shared, refs = refs[2:6], refs[6:]
        total, powers, own, plan, metas, cos_ref, sin_ref, place_ref, sems = refs
    else:
        shared, refs = refs[:4], refs[4:]
        keep_ref, give_ref, total, own, metas, cos_ref, sin_ref, place_ref, sems = refs
    cycles, half = PAD, cos_ref.shape[1]
    side = top_ref[0] ^ (1 - chunk)
    fetch = pltpu.make_async_copy(part_of(view_ref, side, near_ref[0]), own, sems.at[0])
    fetch.start()
    particles = cos_ref.shape[0]
    count = particles // GROUP
    width = 2 * half
    size = keep_ref.shape[0] // (shards // 2)
    if chunk == 0:
        metas[:count] = meta_ref[...]
        for g, piece in enumerate(given):
            metas[(g + 1) * count : (g + 2) * count] = piece[count, :, : metas.shape[1]]
        ints = metas[:, LANES : LANES + LANES].astype(jnp.float32).astype(jnp.int32)
        turn = ints[:, 0:1] * 16 + ints[:, 1:2]
        shard, inside = ints[:, 2:3], ints[:, 3:4]
        block = ((shard ^ cls_ref[0]) & 1) * (shards // 2) + (shard >> 1)
        lane_at = iota((particles, LANES), 1)
        places = jnp.where(lane_at == 0, block * size + inside * cycles, block * PAD + inside)
        plan[...] = jnp.where(lane_at == 2, block * (size - PAD) + inside * cycles, places)
        schedule = pltpu.make_async_copy(plan, place_ref, sems.at[1])
        schedule.start()
        total[...] = jnp.zeros_like(total)
        powers[...] = jnp.zeros_like(powers)
        turns = iota((particles, half), 1) * turn & (width - 1)
        angle = turns.astype(jnp.float32) * (2.0 * math.pi / width)
        cos_ref[...] = jnp.cos(angle)
        sin_ref[...] = jnp.sin(angle)
        saves = [
            pltpu.make_async_copy(here, there, sems.at[2 + i])
            for i, (here, there) in enumerate(zip((plan, metas, cos_ref, sin_ref), shared))
        ]
        for save in saves:
            save.start()
    else:
        loads = [
            pltpu.make_async_copy(there, here, sems.at[1 + i])
            for i, (here, there) in enumerate(zip((place_ref, metas, cos_ref, sin_ref), shared))
        ]
        for load in loads:
            load.start()
        total[...] = jnp.zeros_like(total)
    r = iota((cycles, LANES), 0)
    domain = (side * (far // 2) + r // slice_cycles) * GROUP + near_ref[0]
    pick = iota((cycles, LANES), 1) == domain * slice_cycles + r % slice_cycles
    batch = 2
    fetch.wait()
    if chunk == 0:
        schedule.wait()
    else:
        for load in loads:
            load.wait()
    place_at = 0 if chunk == 0 else 2

    def one(n, source):
        ctf = metas[n : n + 1, :LANES].astype(jnp.float32)
        weight_row = ctf / noise_ref[...]
        weight = jnp.sum(
            jnp.where(pick, jnp.broadcast_to(weight_row, pick.shape), 0.0), axis=1, keepdims=True
        )
        x = source[n % count].astype(jnp.float32)
        x_re, x_im = x[:, :half], x[:, half:]
        cosv, sinv = cos_ref[n : n + 1, :], sin_ref[n : n + 1, :]
        re = weight * (x_re * cosv - x_im * sinv)
        im = weight * (x_re * sinv + x_im * cosv)
        return re, im, ctf * weight_row

    for g in range(GROUP):
        source = own if g == 0 else given[g - 1]
        for start in range(g * count, (g + 1) * count, batch):
            done = [one(n, source) for n in range(start, start + batch)]
            for n, (re, im, power) in zip(range(start, start + batch), done):
                at = pl.ds(pl.multiple_of(place_ref[n, place_at], PAD), cycles)
                total[at, :half] += re
                total[at, half:] += im
                if chunk == 0:
                    powers[pl.ds(place_ref[n, 1], 1), :] += power
    if chunk == 0:
        blocks = powers.shape[0] // PAD
        for b in range(blocks):
            at = slice((b + 1) * size - PAD, (b + 1) * size)
            total[at, :LANES] = powers[b * PAD : (b + 1) * PAD]
    rows = keep_ref.shape[0]
    keep_ref[...] = total[:rows]
    give_ref[...] = total[rows:]
    if chunk == 0:
        for save in saves:
            save.wait()


def class_sums(scalars, view, chunk, given, meta, noise, shared, slice_cycles, far, rows, shards):
    width = view.shape[-1]
    first = chunk == 0
    count = view.shape[2] if view.shape[0] == 2 else view.shape[0]
    particles = count * GROUP
    out = pltpu.VMEM((rows, width), jnp.float32)
    kinds = [
        ((particles, LANES), jnp.int32),
        ((particles, 2 * LANES), view.dtype),
        ((particles, width // 2), jnp.float32),
        ((particles, width // 2), jnp.float32),
    ]
    held = [pltpu.VMEM(shape, dtype) for shape, dtype in kinds]
    shapes = [out, out] + ([pltpu.HBM(shape, dtype) for shape, dtype in kinds] if first else [])
    own = pltpu.VMEM((count, PAD, width), view.dtype)
    scratch = [pltpu.VMEM((2 * rows, width), jnp.float32)]
    if first:
        scratch += [pltpu.VMEM((shards * PAD, LANES), jnp.float32), own, *held]
    else:
        scratch += [own, *held[1:]]
    ins = [meta] if first else []
    return pl.pallas_call(
        functools.partial(
            sums_kernel, slice_cycles=slice_cycles, far=far, chunk=chunk, shards=shards
        ),
        out_shape=shapes,
        in_specs=[SCALARS] * 3 + [HERE] * len(ins) + [HERE, THERE] + [HERE] * (GROUP - 1)
        + [THERE] * len(shared),
        out_specs=[HERE, HERE] + [THERE] * (len(shapes) - 2),
        scratch_shapes=scratch
        + [pltpu.SMEM((particles, LANES), jnp.int32), pltpu.SemaphoreType.DMA((6,))],
        cost_estimate=cost(2.5),
        compiler_params=room(((2 * rows, width), 8), ((particles * PAD, width), 4)),
    )(
        *scalars, *held_near(*ins), noise, *held_far(view), *held_near(*given), *held_far(*shared)
    )


def spans(rows):
    return [(at, min(LANES, rows - at)) for at in range(0, rows, LANES)]


def encode(value, out, at):
    rows = value.shape[0]
    codes = jnp.zeros((PAD, LANES), jnp.float32)
    for i, (start, size) in enumerate(spans(rows)):
        x = value[start : start + size]
        top = jnp.maximum(jnp.max(jnp.abs(x), axis=1, keepdims=True), 1e-30)
        code = jnp.floor(jnp.log(top) / UNIT) + 1.0
        scaled = x * (jnp.exp(-code * UNIT) * 32767.0)
        scaled = jnp.clip(jnp.round(scaled), -32767.0, 32767.0)
        out[at + start : at + start + size, :] = scaled.astype(jnp.int32).astype(jnp.int16)
        eye = iota((size, LANES), 0) == iota((size, LANES), 1)
        row = jnp.sum(jnp.where(eye, code, 0.0), axis=0, keepdims=True)
        codes = jnp.where(iota((PAD, LANES), 0) == i, row, codes)
    for f in range(out.shape[1] // LANES):
        out[at + rows : at + rows + PAD, f * LANES : (f + 1) * LANES] = codes.astype(
            jnp.int32
        ).astype(jnp.int16)


def decode(ref, at, rows):
    codes = ref[at + rows : at + rows + PAD, :LANES].astype(jnp.int32).astype(jnp.float32)
    parts = []
    for i, (start, size) in enumerate(spans(rows)):
        eye = iota((size, LANES), 0) == iota((size, LANES), 1)
        row = jnp.broadcast_to(codes[i : i + 1], (size, LANES))
        code = jnp.sum(jnp.where(eye, row, 0.0), axis=1, keepdims=True)
        x = ref[at + start : at + start + size, :].astype(jnp.int32).astype(jnp.float32)
        parts.append(x * (jnp.exp(code * UNIT) * (1.0 / 32767.0)))
    return jnp.concatenate(parts, axis=0)


def shard_kernel(bit_ref, keep_ref, get_ref, own_ref, code_ref, *, coded):
    parts, rows, _ = own_ref.shape
    if coded:
        for p in range(2 * parts):
            keep_ref[p] = keep_ref[p] + decode(get_ref.at[p], 0, rows)
    bit = bit_ref[0]
    for p in range(parts):
        mine, other = bit * parts + p, (1 - bit) * parts + p
        if coded:
            encode(keep_ref[other], code_ref.at[p], 0)
            own_ref[p] = keep_ref[mine]
        else:
            encode(keep_ref[other] + get_ref[other], code_ref.at[p], 0)
            own_ref[p] = keep_ref[mine] + get_ref[mine]


def split_shards(bit, keep, get):
    parts, rows, width = keep.shape
    parts = parts // 2
    own = pltpu.VMEM((parts, rows, width), jnp.float32)
    code = pltpu.VMEM((parts, rows + PAD, width), jnp.int16)
    return pl.pallas_call(
        functools.partial(shard_kernel, coded=get.dtype == jnp.int16),
        out_shape=(own, code),
        in_specs=[SCALARS, HERE, HERE],
        out_specs=(HERE, HERE),
        cost_estimate=cost(1.5),
        compiler_params=room((keep.shape, 16)),
    )(bit, *held_near(keep, get))


def ahead_kernel(keep_ref, get_ref, power_ref, code_ref):
    rows = keep_ref.shape[0]
    total = keep_ref[...] + decode(get_ref, 0, rows)
    power_ref[...] = total[rows - PAD :, :LANES]
    encode(total, code_ref, 0)


def ahead(keep, get):
    rows, width = keep.shape
    return pl.pallas_call(
        ahead_kernel,
        out_shape=(
            pltpu.VMEM((PAD, LANES), jnp.float32),
            pltpu.VMEM((rows + PAD, width), jnp.int16),
        ),
        in_specs=[HERE, HERE],
        out_specs=(HERE, HERE),
        cost_estimate=cost(1),
        compiler_params=room((keep.shape, 16)),
        name="ahead",
    )(*held_near(keep, get))


def final_kernel(dom_ref, keep_ref, get_ref, power_ref, came_ref, out):
    classes, cycles, _ = out.shape
    rows = classes * cycles
    came = decode(came_ref, 0, rows + PAD)
    sums = keep_ref[...] + decode(get_ref, 0, rows) + came[:rows]
    powers = power_ref[...] + came[rows:, :LANES]
    r = iota((cycles, LANES), 0)
    pick = iota((cycles, LANES), 1) == dom_ref[0] * cycles + r
    for k in range(classes):
        row = jnp.broadcast_to(powers[k : k + 1], pick.shape)
        denom = jnp.sum(jnp.where(pick, row, 0.0), axis=1, keepdims=True) + 1.0
        out[k] = sums[k * cycles : (k + 1) * cycles, :] / denom


def finish(dom, keep, get, power, came, classes, cycles, width):
    out = (classes, cycles, width)
    return pl.pallas_call(
        final_kernel,
        out_shape=jax.ShapeDtypeStruct(out, jnp.float32),
        in_specs=[SCALARS] + [HERE] * 4,
        out_specs=HERE,
        cost_estimate=cost(1),
        compiler_params=room((out, 16)),
        name="finish",
    )(dom, *held_near(keep, get, power, came))


def decoded(keep, get):
    rows = keep.shape[0]
    code = get[rows:, :LANES].astype(jnp.float32).reshape(-1)[:rows]
    scale = jnp.exp(code * UNIT) * (1.0 / 32767.0)
    return keep + get[:rows].astype(jnp.float32) * scale[:, None]


def per_device(spectra, ctf, noise_power, references, owner, sub_class, rotation):
    count, cycles, width = spectra.shape
    k_local = references.shape[0]
    turns_all = width
    domains, shards = lax.axis_size("dom"), lax.axis_size("cls")
    dom, cls = lax.axis_index("dom"), lax.axis_index("cls")
    far = domains // GROUP
    slice_cycles = cycles // domains
    near = (dom & (GROUP - 1)).reshape(1)
    top = (dom // (domains // 2)).reshape(1)
    noise = noise_power.reshape(1, cycles)

    if slice_cycles == PAD:
        view = spectra.reshape(count, 2, GROUP, PAD, width)
    else:
        view = spectra.reshape(count, 2, far // 2, GROUP, slice_cycles, width)
        view = view.transpose(1, 3, 0, 2, 4, 5).reshape(2, GROUP, count, PAD, width)
    rows_of = [v.reshape(1, count) for v in (owner, sub_class, rotation)]
    meta, *sent_0 = pieces(near, top, view, 0, (ctf, *rows_of))
    sent = (sent_0, pieces(near, top, view, 1, ()))
    got = [[swap(sent[c][m - 1], "dom", m) for m in range(1, GROUP)] for c in range(CHUNKS)]

    held, mask = references, 2
    own_side, other_side = references, None
    while mask < shards:
        new = swap(held, "cls", mask)
        other_side = new if other_side is None else jnp.concatenate([other_side, new], axis=0)
        held = jnp.concatenate([held, new], axis=0) if 2 * mask < shards else held
        mask *= 2
    table = rotation_table(turns_all)
    near_refs = swap(own_side, "cls", 1)
    before = score(spectra, ctf, noise, own_side, near_refs, table, None, 0, count)
    far_refs = swap(other_side, "cls", 1)
    size = count // FAR_CALLS
    row = jnp.zeros((1, count), jnp.float32)
    for i in range(FAR_CALLS):
        row = score(
            spectra, ctf, noise, other_side, far_refs, table, (*before, row), i * size, size,
        )
    log_evidence = row.reshape(count)

    scalars = (near, top, cls.reshape(1))
    ends, shared = [], []
    for chunk in range(CHUNKS):
        size = k_local * PAD + (PAD if chunk == 0 else 0)
        keep, give, *more = class_sums(
            scalars, view, chunk, got[chunk], meta, noise, shared, slice_cycles, far,
            shards // 2 * size, shards,
        )
        shared = more
        get = swap(give, "cls", 1)
        shape = (shards // 2, size, width)
        keep, get = keep.reshape(shape), get.reshape(shape)
        mask = shards // 2
        while mask >= 2:
            bit = ((cls // mask) & 1).reshape(1)
            keep, code = split_shards(bit, keep, get)
            get = swap(code, "cls", mask)
            mask //= 2
        ends.append((keep[0], get[0]))
    power, code = ahead(*ends[0])
    came = swap(code, "dom", domains // 2)
    if far == 2:
        new_refs = finish(dom.reshape(1), *ends[1], power, came, k_local, slice_cycles, width)
        return (new_refs, log_evidence)

    came = decoded(jnp.zeros((came.shape[0] - PAD, width), jnp.float32), came)
    numer = decoded(*ends[1]) + came[: k_local * PAD]
    numer = numer.reshape(k_local, PAD, width)
    power = power + came[k_local * PAD :, :LANES]
    left, mask = PAD, domains // 4
    while mask >= GROUP:
        bit = (dom // mask) & 1
        left = left // 2
        own = lax.dynamic_slice_in_dim(numer, bit * left, left, 1)
        other = lax.dynamic_slice_in_dim(numer, (1 - bit) * left, left, 1)
        numer = own + swap(other, "dom", mask)
        power = power + swap(power, "dom", mask)
        mask //= 2
    denom = lax.dynamic_slice_in_dim(power[:k_local], dom * left, left, 1)
    return (numer / (denom + 1.0)[:, :, None], log_evidence)


def solution(mesh):
    return jax.shard_map(
        per_device,
        mesh=mesh,
        in_specs=(
            P(("dom", "cls"), None, None),
            P(("dom", "cls"), None),
            P(),
            P("cls", None, None),
            P(("dom", "cls"), None),
            P(("dom", "cls")),
            P(("dom", "cls")),
        ),
        out_specs=(P("cls", "dom", None), P(("dom", "cls"))),
        check_vma=False,
    )
```

```python
import functools
import math

import jax
import jax.numpy as jnp
from jax import lax
from jax.experimental import pallas as pl
from jax.experimental.pallas import tpu as pltpu
from jax.sharding import PartitionSpec as P


CHUNKS = 2
GROUP = 4
FAR_CALLS = 1
SPLITS = 4
LANES = 128
PAD = 16
STEPS = 64.0
UNIT = math.log(2.0) / STEPS


def table_kernel(out_ref):
    width, turns_all = out_ref.shape
    half = width // 2
    quarter = half // 2
    step = 32
    for at in range(0, quarter, step):
        shape = (step, turns_all)
        turns = (iota(shape, 0) + at) * iota(shape, 1) & (turns_all - 1)
        angle = turns.astype(jnp.float32) * (2.0 * math.pi / turns_all)
        cosv, sinv = jnp.cos(angle), jnp.sin(angle)
        odd, back = (iota(shape, 1) & 1) == 1, (iota(shape, 1) & 2) == 2
        cos_on, sin_on = jnp.where(odd, -sinv, cosv), jnp.where(odd, cosv, sinv)
        cos_on, sin_on = jnp.where(back, -cos_on, cos_on), jnp.where(back, -sin_on, sin_on)
        out_ref[at : at + step, :] = cosv.astype(jnp.bfloat16)
        out_ref[quarter + at : quarter + at + step, :] = cos_on.astype(jnp.bfloat16)
        out_ref[half + at : half + at + step, :] = (-sinv).astype(jnp.bfloat16)
        at = half + quarter + at
        out_ref[at : at + step, :] = (-sin_on).astype(jnp.bfloat16)


def rotation_table(width):
    return pl.pallas_call(
        table_kernel,
        out_shape=pltpu.VMEM((width, width), jnp.bfloat16),
        out_specs=HERE,
        cost_estimate=cost(2),
        compiler_params=room(((width, width), 4)),
        name="table",
    )()


def held_near(*values):
    return [pltpu.with_memory_space_constraint(v, pltpu.VMEM) for v in values]


def held_far(*values):
    return [pltpu.with_memory_space_constraint(v, pltpu.HBM) for v in values]


def swap(value, axis, mask):
    size = lax.axis_size(axis)
    return lax.ppermute(value, axis, [(i, i ^ mask) for i in range(size)])


def iota(shape, axis):
    return lax.broadcasted_iota(jnp.int32, shape, axis)


HERE = pl.BlockSpec(memory_space=pltpu.VMEM)
SCALARS = pl.BlockSpec(memory_space=pltpu.SMEM)
THERE = pl.BlockSpec(memory_space=pltpu.HBM)


def room(*arrays):
    size = sum(math.prod(shape) * bits for shape, bits in arrays)
    return pltpu.CompilerParams(vmem_limit_bytes=size + (8 << 20))


def cost(us):
    return pl.CostEstimate(flops=0, transcendentals=0, bytes_accessed=int(us * 3.6e6))


def score_kernel(
    image_ref, ctf_ref, noise_ref, first_ref, second_ref, table_ref, *refs, merge, start
):
    before = refs[:2] if merge else None
    row_ref = refs[2] if merge else None
    outs = refs[3:4] if merge else refs[:2]
    low_ref, image, image_sum, staged, classes, cross, sem = refs[4 if merge else 2 :]
    count, cycles, width = low_ref.shape
    fetch = pltpu.make_async_copy(image_ref.at[pl.ds(start, count), :cycles, :], low_ref, sem)
    fetch.start()
    tiles = width // LANES
    pairs = tiles // 2
    kinds = cross.shape[0] // count
    part = first_ref.shape[0]
    ctf = ctf_ref[start : start + count, :].astype(jnp.float32)
    weight = ctf / noise_ref[...]
    power = ctf * weight
    eye = iota((cycles, LANES), 0) == iota((cycles, LANES), 1)
    for at, ref in ((0, first_ref), (part, second_ref)):
        for f in range(tiles):
            staged[f, at : at + part, :] = ref[:, f * LANES : (f + 1) * LANES].astype(jnp.float32)
    blocks = kinds // 8
    zero = jnp.zeros((8, LANES), jnp.float32)
    norms = []
    for b in range(blocks):
        square = jnp.zeros((cycles, 8, LANES), jnp.float32)
        for f in range(pairs):
            rows = pl.ds(b * 8 * cycles, 8 * cycles)
            re = jnp.swapaxes(staged[f, rows, :].reshape(8, cycles, LANES), 0, 1)
            im = jnp.swapaxes(staged[f + pairs, rows, :].reshape(8, cycles, LANES), 0, 1)
            classes[3 * f, :, b * 8 : b * 8 + 8, :] = re
            classes[3 * f + 1, :, b * 8 : b * 8 + 8, :] = re - im
            classes[3 * f + 2, :, b * 8 : b * 8 + 8, :] = re + im
            square = square + (re * re + im * im)
        norm = zero
        for r in range(cycles):
            total = jnp.sum(square[r], axis=1, keepdims=True)
            norm = jnp.where(iota((8, LANES), 1) == r, total, norm)
        norms.append(norm)
    fetch.wait()
    for n in range(count):
        row = jnp.broadcast_to(weight[n : n + 1, :], (cycles, LANES))
        column = jnp.sum(jnp.where(eye, row, 0.0), axis=1, keepdims=True)
        low = low_ref[n].astype(jnp.float32)
        weighted = (column * low).astype(jnp.bfloat16).astype(jnp.float32)
        for f in range(tiles):
            image[f, n * cycles : (n + 1) * cycles, :] = weighted[:, f * LANES : (f + 1) * LANES]
        for f in range(pairs):
            re = weighted[:, f * LANES : (f + 1) * LANES]
            im = weighted[:, (f + pairs) * LANES : (f + pairs + 1) * LANES]
            image_sum[f, n * cycles : (n + 1) * cycles, :] = re + im
    group = 2
    for f in range(pairs):

        def particles(g, _):
            def cycle(r, sums):
                new = list(sums)
                for i in range(group):
                    row = pl.ds((g * group + i) * cycles + r, 8, stride=0)
                    a_sum, a_im, a_re = image_sum[f, row, :], image[f + pairs, row, :], image[f, row, :]
                    for b in range(blocks):
                        at = slice(b * 8, b * 8 + 8)
                        j = 3 * (i * blocks + b)
                        new[j] = new[j] + classes[3 * f, r, at, :] * a_sum
                        new[j + 1] = new[j + 1] + classes[3 * f + 1, r, at, :] * a_im
                        new[j + 2] = new[j + 2] + classes[3 * f + 2, r, at, :] * a_re
                return tuple(new)

            sums = lax.fori_loop(0, cycles, cycle, (zero,) * (3 * group * blocks), unroll=4)
            for i in range(group):
                for b in range(blocks):
                    s1, s2, s3 = sums[3 * (i * blocks + b) : 3 * (i * blocks + b) + 3]
                    at = pl.ds(pl.multiple_of((g * group + i) * kinds + b * 8, 8), 8)
                    cross[at, f * LANES : (f + 1) * LANES] = s1 - s2
                    cross[at, (f + pairs) * LANES : (f + pairs + 1) * LANES] = s1 - s3
            return 0

        lax.fori_loop(0, count // group, particles, 0)
    scores = jnp.dot(
        cross[...].astype(jnp.bfloat16), table_ref[...], preferred_element_type=jnp.float32
    )
    cross[...] = scores
    inner = iota((8, LANES), 1) < cycles
    row = row_ref[...] if merge else None
    for n in range(count):
            mine = []
            for b in range(blocks):
                powers = jnp.where(inner, jnp.broadcast_to(power[n : n + 1, :], (8, LANES)), 0.0)
                energy = jnp.sum(powers * norms[b], axis=1, keepdims=True)
                at = n * kinds + b * 8
                mine.append(cross[at : at + 8, :] - 0.5 * energy)
            mine = jnp.concatenate(mine, axis=0)
            top = jnp.max(mine, axis=(0, 1), keepdims=True)
            if merge:
                top_before, total_before = before[0][start + n : start + n + 1, :], before[1][start + n : start + n + 1, :]
                top = jnp.maximum(top, jnp.max(top_before, axis=1, keepdims=True))
            total = jnp.sum(jnp.exp(mine - top), axis=(0, 1), keepdims=True)
            if merge:
                total = total + (total_before * jnp.exp(top_before - top))[:, :1]
                here = iota(row.shape, 1) == start + n
                row = jnp.where(here, jnp.broadcast_to(top + jnp.log(total), row.shape), row)
            else:
                outs[0][n : n + 1, :] = jnp.broadcast_to(top, (1, LANES))
                outs[1][n : n + 1, :] = jnp.broadcast_to(total, (1, LANES))
    if merge:
        outs[0][...] = row


def score(spectra, ctf, noise, first, second, table, before, start, count):
    width = spectra.shape[2]
    cycles = first.shape[1]
    kinds = 2 * first.shape[0]
    merge = before is not None
    each = pltpu.VMEM((count, LANES), jnp.float32)
    row = jax.ShapeDtypeStruct((1, ctf.shape[0]), jnp.float32)
    part = (kinds // 2 * cycles, width)
    outs = pl.pallas_call(
        functools.partial(score_kernel, merge=merge, start=start),
        out_shape=row if merge else (each, each),
        in_specs=[THERE] + [HERE] * (8 if merge else 5),
        out_specs=HERE if merge else (HERE, HERE),
        scratch_shapes=[
            pltpu.VMEM((count, cycles, width), spectra.dtype),
            pltpu.VMEM((width // LANES, count * cycles, LANES), jnp.float32),
            pltpu.VMEM((width // LANES // 2, count * cycles, LANES), jnp.float32),
            pltpu.VMEM((width // LANES, kinds * cycles, LANES), jnp.float32),
            pltpu.VMEM((width // LANES // 2 * 3, cycles, kinds, LANES), jnp.float32),
            pltpu.VMEM((count * kinds, width), jnp.float32),
            pltpu.SemaphoreType.DMA,
        ],
        cost_estimate=cost(8),
        compiler_params=room(
            ((count * cycles, width), 10),
            ((kinds * cycles, width), 12),
            ((count * kinds, width), 8),
            (table.shape, 2),
        ),
    )(
        *held_far(spectra), ctf, noise, *held_near(first.reshape(part), second.reshape(part), table),
        *(before or ()),
    )
    return outs


def part_of(view_ref, top, near):
    if view_ref.shape[0] == 2:
        return view_ref.at[top, near]
    return view_ref.at[:, top, near]


def column(row):
    size = row.shape[1]
    eye = iota((size, size), 0) == iota((size, size), 1)
    return jnp.sum(jnp.where(eye, jnp.broadcast_to(row, (size, size)), 0.0), axis=1, keepdims=True)


def pieces_kernel(near_ref, top_ref, view_ref, *refs, chunk):
    outs, sems = refs[-GROUP:-1], refs[-1]
    if chunk == 0:
        ctf_ref, owner_ref, sub_ref, turn_ref, meta_ref = refs[:5]
        outs = refs[5 : 5 + GROUP - 1]
        ctf_here, owner_here, sub_here, turn_here, small, sems = refs[5 + GROUP - 1 :]
        fetches = [
            pltpu.make_async_copy(there, here, small.at[i])
            for i, (there, here) in enumerate(
                ((ctf_ref, ctf_here), (owner_ref, owner_here), (sub_ref, sub_here), (turn_ref, turn_here))
            )
        ]
        for fetch in fetches:
            fetch.start()
    count = view_ref.shape[2] if view_ref.shape[0] == 2 else view_ref.shape[0]
    part = count // SPLITS
    copies = [
        pltpu.make_async_copy(
            part_of(view_ref, top_ref[0] ^ (1 - chunk), near_ref[0] ^ (i + 1)).at[
                pl.ds(j * part, part)
            ],
            out.at[pl.ds(j * part, part)],
            sems.at[i * SPLITS + j],
        )
        for i, out in enumerate(outs)
        for j in range(SPLITS)
    ]
    for copy in copies:
        copy.start()
    if chunk == 0:
        for fetch in fetches:
            fetch.wait()
        cycles = ctf_ref.shape[1]
        turn = turn_here[...]
        shape = (count, meta_ref.shape[1] - cycles)
        at = iota(shape, 1)
        rest = jnp.where(at == 0, column((turn >> 4).astype(jnp.float32)), 0.0)
        rest = jnp.where(at == 1, column((turn & 15).astype(jnp.float32)), rest)
        rest = jnp.where(at == 2, column(owner_here[...].astype(jnp.float32)), rest)
        rest = jnp.where(at == 3, column(sub_here[...].astype(jnp.float32)), rest)
        meta_ref[:, :cycles] = ctf_here[...]
        meta_ref[:, cycles:] = rest.astype(jnp.bfloat16)
        for out in outs:
            out[count, :, :] = jnp.zeros(out.shape[1:], out.dtype)
            out[count, :, : meta_ref.shape[1]] = meta_ref[...]
    for copy in copies:
        copy.wait()


def pieces(near, top, view, chunk, others):
    count, width = view.shape[2] if view.shape[0] == 2 else view.shape[0], view.shape[-1]
    out = pltpu.VMEM((count + (chunk == 0), PAD, width), view.dtype)
    shapes = [out] * (GROUP - 1)
    scratch = [pltpu.SemaphoreType.DMA(((GROUP - 1) * SPLITS,))]
    if chunk == 0:
        ctf = others[0]
        shapes = [pltpu.VMEM((count, 2 * ctf.shape[1]), view.dtype)] + shapes
        scratch = [
            pltpu.VMEM(ctf.shape, ctf.dtype),
            pltpu.VMEM((1, count), jnp.int32),
            pltpu.VMEM((1, count), jnp.int32),
            pltpu.VMEM((1, count), jnp.int32),
            pltpu.SemaphoreType.DMA((4,)),
        ] + scratch
    return pl.pallas_call(
        functools.partial(pieces_kernel, chunk=chunk),
        out_shape=shapes,
        in_specs=[SCALARS] * 2 + [THERE] * (1 + len(others)),
        out_specs=[HERE] * len(shapes),
        scratch_shapes=scratch,
        cost_estimate=cost(1.5),
        compiler_params=room(((count * PAD, width), 2 * GROUP)),
    )(near, top, *held_far(view, *others))


def sums_kernel(
    near_ref, top_ref, cls_ref, *refs, slice_cycles, far, chunk, shards,
):
    if chunk == 0:
        meta_ref, refs = refs[0], refs[1:]
    noise_ref, view_ref, refs = refs[0], refs[1], refs[2:]
    given, refs = refs[: GROUP - 1], refs[GROUP - 1 :]
    if chunk == 0:
        keep_ref, give_ref = refs[:2]
        shared, refs = refs[2:6], refs[6:]
        total, own, powers, plan, metas, cos_ref, sin_ref, place_ref, sems = refs
    else:
        plan, metas, cos_ref, sin_ref = refs[:4]
        keep_ref, give_ref, total, own, place_ref, sems = refs[4:]
    cycles, half = PAD, cos_ref.shape[1]
    side = top_ref[0] ^ (1 - chunk)
    particles = cos_ref.shape[0]
    count = particles // GROUP
    width = 2 * half
    size = keep_ref.shape[0] // (shards // 2)
    fetch = pltpu.make_async_copy(part_of(view_ref, side, near_ref[0]), own, sems.at[5])
    fetch.start()
    schedule = pltpu.make_async_copy(plan, place_ref, sems.at[0])
    if chunk == 0:
        metas[:count] = meta_ref[...]
        for g, piece in enumerate(given):
            metas[(g + 1) * count : (g + 2) * count] = piece[count, :, : metas.shape[1]]
        ints = metas[:, LANES : LANES + LANES].astype(jnp.float32).astype(jnp.int32)
        turn = ints[:, 0:1] * 16 + ints[:, 1:2]
        shard, inside = ints[:, 2:3], ints[:, 3:4]
        block = ((shard ^ cls_ref[0]) & 1) * (shards // 2) + (shard >> 1)
        here = iota((particles, LANES), 0) == iota((particles, LANES), 1)

        def in_row(values):
            return jnp.sum(jnp.where(here, values.astype(jnp.float32), 0.0), axis=0, keepdims=True)

        rows = (
            in_row(block * size + inside * cycles),
            in_row(block * PAD + inside),
            in_row(block * (size - PAD) + inside * cycles),
        )
        at = iota(plan.shape, 0)
        places = jnp.where(at == 0, rows[0], jnp.where(at == 1, rows[1], rows[2]))
        plan[...] = places.astype(jnp.int32)
        schedule.start()
        total[...] = jnp.zeros_like(total)
        powers[...] = jnp.zeros_like(powers)
        turns = iota((particles, half), 1) * turn & (width - 1)
        angle = turns.astype(jnp.float32) * (2.0 * math.pi / width)
        cos_ref[...] = jnp.cos(angle)
        sin_ref[...] = jnp.sin(angle)
        saves = [
            pltpu.make_async_copy(here, there, sems.at[1 + i])
            for i, (here, there) in enumerate(zip((plan, metas, cos_ref, sin_ref), shared))
        ]
        for save in saves:
            save.start()
    else:
        schedule.start()
        total[...] = jnp.zeros_like(total)
    r = iota((cycles, LANES), 0)
    domain = (side * (far // 2) + r // slice_cycles) * GROUP + near_ref[0]
    pick = iota((cycles, LANES), 1) == domain * slice_cycles + r % slice_cycles
    batch = 2
    schedule.wait()
    place_at = 0 if chunk == 0 else 2

    def one(n, source):
        ctf = metas[n : n + 1, :LANES].astype(jnp.float32)
        weight_row = ctf / noise_ref[...]
        weight = jnp.sum(
            jnp.where(pick, jnp.broadcast_to(weight_row, pick.shape), 0.0), axis=1, keepdims=True
        )
        x = source[n % count].astype(jnp.float32)
        x_re, x_im = x[:, :half], x[:, half:]
        cosv, sinv = cos_ref[n : n + 1, :], sin_ref[n : n + 1, :]
        re = weight * (x_re * cosv - x_im * sinv)
        im = weight * (x_re * sinv + x_im * cosv)
        return re, im, ctf * weight_row

    for g in (*range(1, GROUP), 0):
        source = given[g - 1] if g else own
        if g == 0:
            fetch.wait()
        for start in range(g * count, (g + 1) * count, batch):
            done = [one(n, source) for n in range(start, start + batch)]
            for n, (re, im, power) in zip(range(start, start + batch), done):
                at = pl.ds(pl.multiple_of(place_ref[place_at, n], PAD), cycles)
                total[at, :half] += re
                total[at, half:] += im
                if chunk == 0:
                    powers[pl.ds(place_ref[1, n], 1), :] += power
    if chunk == 0:
        blocks = powers.shape[0] // PAD
        for b in range(blocks):
            at = slice((b + 1) * size - PAD, (b + 1) * size)
            total[at, :LANES] = powers[b * PAD : (b + 1) * PAD]
    rows = keep_ref.shape[0]
    keep_ref[...] = total[:rows]
    give_ref[...] = total[rows:]
    if chunk == 0:
        for save in saves:
            save.wait()


def class_sums(scalars, view, chunk, given, meta, noise, shared, slice_cycles, far, rows, shards):
    width = view.shape[-1]
    count = view.shape[2] if view.shape[0] == 2 else view.shape[0]
    first = chunk == 0
    particles = count * GROUP
    out = pltpu.VMEM((rows, width), jnp.float32)
    kinds = [
        ((8, LANES), jnp.int32),
        ((particles, 2 * LANES), given[0].dtype),
        ((particles, width // 2), jnp.float32),
        ((particles, width // 2), jnp.float32),
    ]
    shapes = [out, out] + ([pltpu.HBM(shape, dtype) for shape, dtype in kinds] if first else [])
    scratch = [
        pltpu.VMEM((2 * rows, width), jnp.float32),
        pltpu.VMEM((count, PAD, width), view.dtype),
    ]
    if first:
        scratch += [pltpu.VMEM((shards * PAD, LANES), jnp.float32)]
        scratch += [pltpu.VMEM(shape, dtype) for shape, dtype in kinds]
    ins = [meta] if first else []
    return pl.pallas_call(
        functools.partial(
            sums_kernel, slice_cycles=slice_cycles, far=far, chunk=chunk, shards=shards
        ),
        out_shape=shapes,
        in_specs=[SCALARS] * 3 + [HERE] * (len(ins) + 1) + [THERE]
        + [HERE] * (GROUP - 1 + len(shared)),
        out_specs=[HERE, HERE] + [THERE] * (len(shapes) - 2),
        scratch_shapes=scratch
        + [pltpu.SMEM((8, LANES), jnp.int32), pltpu.SemaphoreType.DMA((6,))],
        cost_estimate=cost(2.5),
        compiler_params=room(((2 * rows, width), 8), ((particles * PAD, width), 4)),
    )(*scalars, *held_near(*ins), noise, *held_far(view), *held_near(*given, *shared))


def spans(rows):
    return [(at, min(LANES, rows - at)) for at in range(0, rows, LANES)]


def encode(value, out, at):
    rows = value.shape[0]
    codes = jnp.zeros((PAD, LANES), jnp.float32)
    for i, (start, size) in enumerate(spans(rows)):
        x = value[start : start + size]
        top = jnp.maximum(jnp.max(jnp.abs(x), axis=1, keepdims=True), 1e-30)
        code = jnp.floor(jnp.log(top) / UNIT) + 1.0
        scaled = x * (jnp.exp(-code * UNIT) * 32767.0)
        scaled = jnp.clip(jnp.round(scaled), -32767.0, 32767.0)
        out[at + start : at + start + size, :] = scaled.astype(jnp.int32).astype(jnp.int16)
        eye = iota((size, LANES), 0) == iota((size, LANES), 1)
        row = jnp.sum(jnp.where(eye, code, 0.0), axis=0, keepdims=True)
        codes = jnp.where(iota((PAD, LANES), 0) == i, row, codes)
    for f in range(out.shape[1] // LANES):
        out[at + rows : at + rows + PAD, f * LANES : (f + 1) * LANES] = codes.astype(
            jnp.int32
        ).astype(jnp.int16)


def decode(ref, at, rows):
    codes = ref[at + rows : at + rows + PAD, :LANES].astype(jnp.int32).astype(jnp.float32)
    parts = []
    for i, (start, size) in enumerate(spans(rows)):
        eye = iota((size, LANES), 0) == iota((size, LANES), 1)
        row = jnp.broadcast_to(codes[i : i + 1], (size, LANES))
        code = jnp.sum(jnp.where(eye, row, 0.0), axis=1, keepdims=True)
        x = ref[at + start : at + start + size, :].astype(jnp.int32).astype(jnp.float32)
        parts.append(x * (jnp.exp(code * UNIT) * (1.0 / 32767.0)))
    return jnp.concatenate(parts, axis=0)


def shard_kernel(bit_ref, keep_ref, get_ref, own_ref, code_ref, *, coded):
    parts, rows, _ = own_ref.shape
    if coded:
        for p in range(2 * parts):
            keep_ref[p] = keep_ref[p] + decode(get_ref.at[p], 0, rows)
    bit = bit_ref[0]
    for p in range(parts):
        mine, other = bit * parts + p, (1 - bit) * parts + p
        if coded:
            encode(keep_ref[other], code_ref.at[p], 0)
            own_ref[p] = keep_ref[mine]
        else:
            encode(keep_ref[other] + get_ref[other], code_ref.at[p], 0)
            own_ref[p] = keep_ref[mine] + get_ref[mine]


def split_shards(bit, keep, get):
    parts, rows, width = keep.shape
    parts = parts // 2
    own = pltpu.VMEM((parts, rows, width), jnp.float32)
    code = pltpu.VMEM((parts, rows + PAD, width), jnp.int16)
    return pl.pallas_call(
        functools.partial(shard_kernel, coded=get.dtype == jnp.int16),
        out_shape=(own, code),
        in_specs=[SCALARS, HERE, HERE],
        out_specs=(HERE, HERE),
        cost_estimate=cost(1.5),
        compiler_params=room((keep.shape, 16)),
    )(bit, *held_near(keep, get))


def ahead_kernel(keep_ref, get_ref, power_ref, code_ref):
    rows = keep_ref.shape[0]
    total = keep_ref[...] + decode(get_ref, 0, rows)
    power_ref[...] = total[rows - PAD :, :LANES]
    encode(total, code_ref, 0)


def ahead(keep, get):
    rows, width = keep.shape
    return pl.pallas_call(
        ahead_kernel,
        out_shape=(
            pltpu.VMEM((PAD, LANES), jnp.float32),
            pltpu.VMEM((rows + PAD, width), jnp.int16),
        ),
        in_specs=[HERE, HERE],
        out_specs=(HERE, HERE),
        cost_estimate=cost(1),
        compiler_params=room((keep.shape, 16)),
        name="ahead",
    )(*held_near(keep, get))


def final_kernel(dom_ref, keep_ref, get_ref, power_ref, came_ref, out):
    classes, cycles, _ = out.shape
    rows = classes * cycles
    came = decode(came_ref, 0, rows + PAD)
    sums = keep_ref[...] + decode(get_ref, 0, rows) + came[:rows]
    powers = power_ref[...] + came[rows:, :LANES]
    r = iota((cycles, LANES), 0)
    pick = iota((cycles, LANES), 1) == dom_ref[0] * cycles + r
    for k in range(classes):
        row = jnp.broadcast_to(powers[k : k + 1], pick.shape)
        denom = jnp.sum(jnp.where(pick, row, 0.0), axis=1, keepdims=True) + 1.0
        out[k] = sums[k * cycles : (k + 1) * cycles, :] / denom


def finish(dom, keep, get, power, came, classes, cycles, width):
    out = (classes, cycles, width)
    return pl.pallas_call(
        final_kernel,
        out_shape=jax.ShapeDtypeStruct(out, jnp.float32),
        in_specs=[SCALARS] + [HERE] * 4,
        out_specs=HERE,
        cost_estimate=cost(1),
        compiler_params=room((out, 16)),
        name="finish",
    )(dom, *held_near(keep, get, power, came))


def decoded(keep, get):
    rows = keep.shape[0]
    code = get[rows:, :LANES].astype(jnp.float32).reshape(-1)[:rows]
    scale = jnp.exp(code * UNIT) * (1.0 / 32767.0)
    return keep + get[:rows].astype(jnp.float32) * scale[:, None]


def per_device(spectra, ctf, noise_power, references, owner, sub_class, rotation):
    count, cycles, width = spectra.shape
    k_local = references.shape[0]
    turns_all = width
    domains, shards = lax.axis_size("dom"), lax.axis_size("cls")
    dom, cls = lax.axis_index("dom"), lax.axis_index("cls")
    far = domains // GROUP
    slice_cycles = cycles // domains
    near = (dom & (GROUP - 1)).reshape(1)
    top = (dom // (domains // 2)).reshape(1)
    noise = noise_power.reshape(1, cycles)

    if slice_cycles == PAD:
        view = spectra.reshape(count, 2, GROUP, PAD, width)
    else:
        view = spectra.reshape(count, 2, far // 2, GROUP, slice_cycles, width)
        view = view.transpose(1, 3, 0, 2, 4, 5).reshape(2, GROUP, count, PAD, width)
    rows_of = [v.reshape(1, count) for v in (owner, sub_class, rotation)]
    meta, *sent_0 = pieces(near, top, view, 0, (ctf, *rows_of))
    sent = (sent_0, pieces(near, top, view, 1, ()))
    got = [[swap(sent[c][m - 1], "dom", m) for m in range(1, GROUP)] for c in range(CHUNKS)]

    held, mask = references, 2
    own_side, other_side = references, None
    while mask < shards:
        new = swap(held, "cls", mask)
        other_side = new if other_side is None else jnp.concatenate([other_side, new], axis=0)
        held = jnp.concatenate([held, new], axis=0) if 2 * mask < shards else held
        mask *= 2
    table = rotation_table(turns_all)
    near_refs = swap(own_side, "cls", 1)
    before = score(spectra, ctf, noise, own_side, near_refs, table, None, 0, count)
    far_refs = swap(other_side, "cls", 1)
    size = count // FAR_CALLS
    row = jnp.zeros((1, count), jnp.float32)
    for i in range(FAR_CALLS):
        row = score(
            spectra, ctf, noise, other_side, far_refs, table, (*before, row), i * size, size,
        )
    log_evidence = row.reshape(count)

    scalars = (near, top, cls.reshape(1))
    ends, shared = [], []
    for chunk in range(CHUNKS):
        size = k_local * PAD + (PAD if chunk == 0 else 0)
        keep, give, *more = class_sums(
            scalars, view, chunk, got[chunk], meta, noise, shared, slice_cycles, far,
            shards // 2 * size, shards,
        )
        shared = more
        get = swap(give, "cls", 1)
        shape = (shards // 2, size, width)
        keep, get = keep.reshape(shape), get.reshape(shape)
        mask = shards // 2
        while mask >= 2:
            bit = ((cls // mask) & 1).reshape(1)
            keep, code = split_shards(bit, keep, get)
            get = swap(code, "cls", mask)
            mask //= 2
        ends.append((keep[0], get[0]))
    power, code = ahead(*ends[0])
    came = swap(code, "dom", domains // 2)
    if far == 2:
        new_refs = finish(dom.reshape(1), *ends[1], power, came, k_local, slice_cycles, width)
        return (new_refs, log_evidence)

    came = decoded(jnp.zeros((came.shape[0] - PAD, width), jnp.float32), came)
    numer = decoded(*ends[1]) + came[: k_local * PAD]
    numer = numer.reshape(k_local, PAD, width)
    power = power + came[k_local * PAD :, :LANES]
    left, mask = PAD, domains // 4
    while mask >= GROUP:
        bit = (dom // mask) & 1
        left = left // 2
        own = lax.dynamic_slice_in_dim(numer, bit * left, left, 1)
        other = lax.dynamic_slice_in_dim(numer, (1 - bit) * left, left, 1)
        numer = own + swap(other, "dom", mask)
        power = power + swap(power, "dom", mask)
        mask //= 2
    denom = lax.dynamic_slice_in_dim(power[:k_local], dom * left, left, 1)
    return (numer / (denom + 1.0)[:, :, None], log_evidence)


def solution(mesh):
    return jax.shard_map(
        per_device,
        mesh=mesh,
        in_specs=(
            P(("dom", "cls"), None, None),
            P(("dom", "cls"), None),
            P(),
            P("cls", None, None),
            P(("dom", "cls"), None),
            P(("dom", "cls")),
            P(("dom", "cls")),
        ),
        out_specs=(P("cls", "dom", None), P(("dom", "cls"))),
        check_vma=False,
    )
```

```python
import functools
import math

import jax
import jax.numpy as jnp
from jax import lax
from jax.experimental import pallas as pl
from jax.experimental.pallas import tpu as pltpu
from jax.sharding import PartitionSpec as P


CHUNKS = 2
GROUP = 4
NEAR_CALLS = 2
SPLITS = 4
LANES = 128
PAD = 16
STEPS = 64.0
UNIT = math.log(2.0) / STEPS


def table_kernel(image_ref, out_ref, low_ref, sems):
    width, turns_all = out_ref.shape
    count, cycles, _ = low_ref.shape
    part = count // SPLITS
    copies = [
        pltpu.make_async_copy(
            image_ref.at[pl.ds(i * part, part), :cycles, :], low_ref.at[pl.ds(i * part, part)], sems.at[i]
        )
        for i in range(SPLITS)
    ]
    for copy in copies:
        copy.start()
    half = width // 2
    quarter = half // 2
    step = 32
    for at in range(0, quarter, step):
        shape = (step, turns_all)
        turns = (iota(shape, 0) + at) * iota(shape, 1) & (turns_all - 1)
        angle = turns.astype(jnp.float32) * (2.0 * math.pi / turns_all)
        cosv, sinv = jnp.cos(angle), jnp.sin(angle)
        odd, back = (iota(shape, 1) & 1) == 1, (iota(shape, 1) & 2) == 2
        cos_on, sin_on = jnp.where(odd, -sinv, cosv), jnp.where(odd, cosv, sinv)
        cos_on, sin_on = jnp.where(back, -cos_on, cos_on), jnp.where(back, -sin_on, sin_on)
        out_ref[at : at + step, :] = cosv.astype(jnp.bfloat16)
        out_ref[quarter + at : quarter + at + step, :] = cos_on.astype(jnp.bfloat16)
        out_ref[half + at : half + at + step, :] = (-sinv).astype(jnp.bfloat16)
        at = half + quarter + at
        out_ref[at : at + step, :] = (-sin_on).astype(jnp.bfloat16)
    for copy in copies:
        copy.wait()


def rotation_table(spectra, cycles):
    count, _, width = spectra.shape
    return pl.pallas_call(
        table_kernel,
        out_shape=(
            pltpu.VMEM((width, width), jnp.bfloat16),
            pltpu.VMEM((count, cycles, width), spectra.dtype),
        ),
        in_specs=[THERE],
        out_specs=(HERE, HERE),
        scratch_shapes=[pltpu.SemaphoreType.DMA((SPLITS,))],
        cost_estimate=cost(2),
        compiler_params=room(((width, width), 4)),
        name="table",
    )(*held_far(spectra))


def held_near(*values):
    return [pltpu.with_memory_space_constraint(v, pltpu.VMEM) for v in values]


def held_far(*values):
    return [pltpu.with_memory_space_constraint(v, pltpu.HBM) for v in values]


def swap(value, axis, mask):
    size = lax.axis_size(axis)
    return lax.ppermute(value, axis, [(i, i ^ mask) for i in range(size)])


def iota(shape, axis):
    return lax.broadcasted_iota(jnp.int32, shape, axis)


HERE = pl.BlockSpec(memory_space=pltpu.VMEM)
SCALARS = pl.BlockSpec(memory_space=pltpu.SMEM)
THERE = pl.BlockSpec(memory_space=pltpu.HBM)


def room(*arrays):
    size = sum(math.prod(shape) * bits for shape, bits in arrays)
    return pltpu.CompilerParams(vmem_limit_bytes=size + (8 << 20))


def cost(us):
    return pl.CostEstimate(flops=0, transcendentals=0, bytes_accessed=int(us * 3.6e6))


def score_kernel(
    low_ref, ctf_ref, noise_ref, first_ref, second_ref, table_ref, *refs, merge, start
):
    before, refs = refs[:merge], refs[merge:]
    outs, refs = refs[: 1 if merge else 2], refs[1 if merge else 2 :]
    image, image_sum, staged, classes, cross = refs
    _, cycles, width = low_ref.shape
    tiles = width // LANES
    pairs = tiles // 2
    count = image.shape[1] // cycles
    kinds = cross.shape[0] // count
    part = first_ref.shape[0]
    ctf = ctf_ref[start : start + count, :].astype(jnp.float32)
    weight = ctf / noise_ref[...]
    power = ctf * weight
    eye = iota((cycles, LANES), 0) == iota((cycles, LANES), 1)
    for at, ref in ((0, first_ref), (part, second_ref)):
        for f in range(tiles):
            staged[f, at : at + part, :] = ref[:, f * LANES : (f + 1) * LANES].astype(jnp.float32)
    blocks = kinds // 8
    zero = jnp.zeros((8, LANES), jnp.float32)
    norms = []
    for b in range(blocks):
        square = jnp.zeros((cycles, 8, LANES), jnp.float32)
        for f in range(pairs):
            rows = pl.ds(b * 8 * cycles, 8 * cycles)
            re = jnp.swapaxes(staged[f, rows, :].reshape(8, cycles, LANES), 0, 1)
            im = jnp.swapaxes(staged[f + pairs, rows, :].reshape(8, cycles, LANES), 0, 1)
            classes[3 * f, :, b * 8 : b * 8 + 8, :] = re
            classes[3 * f + 1, :, b * 8 : b * 8 + 8, :] = re - im
            classes[3 * f + 2, :, b * 8 : b * 8 + 8, :] = re + im
            square = square + (re * re + im * im)
        norm = zero
        for r in range(cycles):
            total = jnp.sum(square[r], axis=1, keepdims=True)
            norm = jnp.where(iota((8, LANES), 1) == r, total, norm)
        norms.append(norm)
    for n in range(count):
        row = jnp.broadcast_to(weight[n : n + 1, :], (cycles, LANES))
        column = jnp.sum(jnp.where(eye, row, 0.0), axis=1, keepdims=True)
        low = low_ref[start + n].astype(jnp.float32)
        weighted = (column * low).astype(jnp.bfloat16).astype(jnp.float32)
        for f in range(tiles):
            image[f, n * cycles : (n + 1) * cycles, :] = weighted[:, f * LANES : (f + 1) * LANES]
        for f in range(pairs):
            re = weighted[:, f * LANES : (f + 1) * LANES]
            im = weighted[:, (f + pairs) * LANES : (f + pairs + 1) * LANES]
            image_sum[f, n * cycles : (n + 1) * cycles, :] = re + im
    group = 2
    for f in range(pairs):

        def particles(g, _):
            def cycle(r, sums):
                new = list(sums)
                for i in range(group):
                    row = pl.ds((g * group + i) * cycles + r, 8, stride=0)
                    a_sum, a_im, a_re = image_sum[f, row, :], image[f + pairs, row, :], image[f, row, :]
                    for b in range(blocks):
                        at = slice(b * 8, b * 8 + 8)
                        j = 3 * (i * blocks + b)
                        new[j] = new[j] + classes[3 * f, r, at, :] * a_sum
                        new[j + 1] = new[j + 1] + classes[3 * f + 1, r, at, :] * a_im
                        new[j + 2] = new[j + 2] + classes[3 * f + 2, r, at, :] * a_re
                return tuple(new)

            sums = lax.fori_loop(0, cycles, cycle, (zero,) * (3 * group * blocks), unroll=4)
            for i in range(group):
                for b in range(blocks):
                    s1, s2, s3 = sums[3 * (i * blocks + b) : 3 * (i * blocks + b) + 3]
                    at = pl.ds(pl.multiple_of((g * group + i) * kinds + b * 8, 8), 8)
                    cross[at, f * LANES : (f + 1) * LANES] = s1 - s2
                    cross[at, (f + pairs) * LANES : (f + pairs + 1) * LANES] = s1 - s3
            return 0

        lax.fori_loop(0, count // group, particles, 0)
    scores = jnp.dot(
        cross[...].astype(jnp.bfloat16), table_ref[...], preferred_element_type=jnp.float32
    )
    cross[...] = scores
    inner = iota((8, LANES), 1) < cycles
    row = jnp.zeros(outs[0].shape, jnp.float32)
    for n in range(count):
            mine = []
            for b in range(blocks):
                powers = jnp.where(inner, jnp.broadcast_to(power[n : n + 1, :], (8, LANES)), 0.0)
                energy = jnp.sum(powers * norms[b], axis=1, keepdims=True)
                at = n * kinds + b * 8
                mine.append(cross[at : at + 8, :] - 0.5 * energy)
            mine = jnp.concatenate(mine, axis=0)
            top = jnp.max(mine, axis=(0, 1), keepdims=True)
            if merge:
                per = count // (merge // 2)
                pair, i = before[n // per * 2 : n // per * 2 + 2], n % per
                top_before, total_before = pair[0][i : i + 1, :], pair[1][i : i + 1, :]
                top = jnp.maximum(top, jnp.max(top_before, axis=1, keepdims=True))
            total = jnp.sum(jnp.exp(mine - top), axis=(0, 1), keepdims=True)
            if merge:
                total = total + (total_before * jnp.exp(top_before - top))[:, :1]
                here = iota(row.shape, 1) == start + n
                row = jnp.where(here, jnp.broadcast_to(top + jnp.log(total), row.shape), row)
            else:
                outs[0][n : n + 1, :] = jnp.broadcast_to(top, (1, LANES))
                outs[1][n : n + 1, :] = jnp.broadcast_to(total, (1, LANES))
    if merge:
        outs[0][...] = row


def score(low, ctf, noise, first, second, table, before, start, count):
    _, cycles, width = low.shape
    kinds = 2 * first.shape[0]
    merge = len(before)
    each = pltpu.VMEM((count, LANES), jnp.float32)
    row = jax.ShapeDtypeStruct((1, count), jnp.float32)
    part = (kinds // 2 * cycles, width)
    return pl.pallas_call(
        functools.partial(score_kernel, merge=merge, start=start),
        out_shape=row if merge else (each, each),
        in_specs=[HERE] * (6 + merge),
        out_specs=HERE if merge else (HERE, HERE),
        scratch_shapes=[
            pltpu.VMEM((width // LANES, count * cycles, LANES), jnp.float32),
            pltpu.VMEM((width // LANES // 2, count * cycles, LANES), jnp.float32),
            pltpu.VMEM((width // LANES, kinds * cycles, LANES), jnp.float32),
            pltpu.VMEM((width // LANES // 2 * 3, cycles, kinds, LANES), jnp.float32),
            pltpu.VMEM((count * kinds, width), jnp.float32),
        ],
        cost_estimate=cost(count / 2),
        compiler_params=room(
            ((count * cycles, width), 8),
            ((kinds * cycles, width), 12),
            ((count * kinds, width), 8),
            (table.shape, 2),
        ),
    )(
        *held_near(low), ctf, noise, *held_near(first.reshape(part), second.reshape(part), table),
        *before,
    )


def part_of(view_ref, top, near):
    if view_ref.shape[0] == 2:
        return view_ref.at[top, near]
    return view_ref.at[:, top, near]


def column(row):
    size = row.shape[1]
    eye = iota((size, size), 0) == iota((size, size), 1)
    return jnp.sum(jnp.where(eye, jnp.broadcast_to(row, (size, size)), 0.0), axis=1, keepdims=True)


def pieces_kernel(near_ref, top_ref, view_ref, *refs, chunk):
    outs, sems = refs[-GROUP:-1], refs[-1]
    if chunk == 0:
        ctf_ref, owner_ref, sub_ref, turn_ref, meta_ref = refs[:5]
        outs = refs[5 : 5 + GROUP - 1]
        ctf_here, owner_here, sub_here, turn_here, small, sems = refs[5 + GROUP - 1 :]
        fetches = [
            pltpu.make_async_copy(there, here, small.at[i])
            for i, (there, here) in enumerate(
                ((ctf_ref, ctf_here), (owner_ref, owner_here), (sub_ref, sub_here), (turn_ref, turn_here))
            )
        ]
        for fetch in fetches:
            fetch.start()
    count = view_ref.shape[2] if view_ref.shape[0] == 2 else view_ref.shape[0]
    part = count // SPLITS
    copies = [
        pltpu.make_async_copy(
            part_of(view_ref, top_ref[0] ^ (1 - chunk), near_ref[0] ^ (i + 1)).at[
                pl.ds(j * part, part)
            ],
            out.at[pl.ds(j * part, part)],
            sems.at[i * SPLITS + j],
        )
        for i, out in enumerate(outs)
        for j in range(SPLITS)
    ]
    for copy in copies:
        copy.start()
    if chunk == 0:
        for fetch in fetches:
            fetch.wait()
        cycles = ctf_ref.shape[1]
        turn = turn_here[...]
        shape = (count, meta_ref.shape[1] - cycles)
        at = iota(shape, 1)
        rest = jnp.where(at == 0, column((turn >> 4).astype(jnp.float32)), 0.0)
        rest = jnp.where(at == 1, column((turn & 15).astype(jnp.float32)), rest)
        rest = jnp.where(at == 2, column(owner_here[...].astype(jnp.float32)), rest)
        rest = jnp.where(at == 3, column(sub_here[...].astype(jnp.float32)), rest)
        meta_ref[:, :cycles] = ctf_here[...]
        meta_ref[:, cycles:] = rest.astype(jnp.bfloat16)
        for out in outs:
            out[count, :, :] = jnp.zeros(out.shape[1:], out.dtype)
            out[count, :, : meta_ref.shape[1]] = meta_ref[...]
    for copy in copies:
        copy.wait()


def pieces(near, top, view, chunk, others):
    count, width = view.shape[2] if view.shape[0] == 2 else view.shape[0], view.shape[-1]
    out = pltpu.VMEM((count + (chunk == 0), PAD, width), view.dtype)
    shapes = [out] * (GROUP - 1)
    scratch = [pltpu.SemaphoreType.DMA(((GROUP - 1) * SPLITS,))]
    if chunk == 0:
        ctf = others[0]
        shapes = [pltpu.VMEM((count, 2 * ctf.shape[1]), view.dtype)] + shapes
        scratch = [
            pltpu.VMEM(ctf.shape, ctf.dtype),
            pltpu.VMEM((1, count), jnp.int32),
            pltpu.VMEM((1, count), jnp.int32),
            pltpu.VMEM((1, count), jnp.int32),
            pltpu.SemaphoreType.DMA((4,)),
        ] + scratch
    return pl.pallas_call(
        functools.partial(pieces_kernel, chunk=chunk),
        out_shape=shapes,
        in_specs=[SCALARS] * 2 + [THERE] * (1 + len(others)),
        out_specs=[HERE] * len(shapes),
        scratch_shapes=scratch,
        cost_estimate=cost(1.5),
        compiler_params=room(((count * PAD, width), 2 * GROUP)),
    )(near, top, *held_far(view, *others))


def sums_kernel(
    near_ref, top_ref, cls_ref, *refs, slice_cycles, far, chunk, shards,
):
    if chunk == 0:
        meta_ref, refs = refs[0], refs[1:]
    noise_ref, view_ref, refs = refs[0], refs[1], refs[2:]
    given, refs = refs[: GROUP - 1], refs[GROUP - 1 :]
    if chunk == 0:
        keep_ref, give_ref = refs[:2]
        shared, refs = refs[2:6], refs[6:]
        total, own, powers, plan, metas, cos_ref, sin_ref, place_ref, sems = refs
    else:
        plan, metas, cos_ref, sin_ref = refs[:4]
        keep_ref, give_ref, total, own, place_ref, sems = refs[4:]
    cycles, half = PAD, cos_ref.shape[1]
    side = top_ref[0] ^ (1 - chunk)
    particles = cos_ref.shape[0]
    count = particles // GROUP
    width = 2 * half
    size = keep_ref.shape[0] // (shards // 2)
    part = count // SPLITS
    fetches = [
        pltpu.make_async_copy(
            part_of(view_ref, side, near_ref[0]).at[pl.ds(i * part, part)],
            own.at[pl.ds(i * part, part)],
            sems.at[5 + i],
        )
        for i in range(SPLITS)
    ]
    for fetch in fetches:
        fetch.start()
    schedule = pltpu.make_async_copy(plan, place_ref, sems.at[0])
    if chunk == 0:
        metas[:count] = meta_ref[...]
        for g, piece in enumerate(given):
            metas[(g + 1) * count : (g + 2) * count] = piece[count, :, : metas.shape[1]]
        ints = metas[:, LANES : LANES + LANES].astype(jnp.float32).astype(jnp.int32)
        turn = ints[:, 0:1] * 16 + ints[:, 1:2]
        shard, inside = ints[:, 2:3], ints[:, 3:4]
        block = ((shard ^ cls_ref[0]) & 1) * (shards // 2) + (shard >> 1)
        here = iota((particles, LANES), 0) == iota((particles, LANES), 1)

        def in_row(values):
            return jnp.sum(jnp.where(here, values.astype(jnp.float32), 0.0), axis=0, keepdims=True)

        rows = (
            in_row(block * size + inside * cycles),
            in_row(block * PAD + inside),
            in_row(block * (size - PAD) + inside * cycles),
        )
        at = iota(plan.shape, 0)
        places = jnp.where(at == 0, rows[0], jnp.where(at == 1, rows[1], rows[2]))
        plan[...] = places.astype(jnp.int32)
        schedule.start()
        total[...] = jnp.zeros_like(total)
        powers[...] = jnp.zeros_like(powers)
        turns = iota((particles, half), 1) * turn & (width - 1)
        angle = turns.astype(jnp.float32) * (2.0 * math.pi / width)
        cos_ref[...] = jnp.cos(angle)
        sin_ref[...] = jnp.sin(angle)
        saves = [
            pltpu.make_async_copy(here, there, sems.at[1 + i])
            for i, (here, there) in enumerate(zip((plan, metas, cos_ref, sin_ref), shared))
        ]
        for save in saves:
            save.start()
    else:
        schedule.start()
        total[...] = jnp.zeros_like(total)
    r = iota((cycles, LANES), 0)
    domain = (side * (far // 2) + r // slice_cycles) * GROUP + near_ref[0]
    pick = iota((cycles, LANES), 1) == domain * slice_cycles + r % slice_cycles
    batch = 2
    schedule.wait()
    place_at = 0 if chunk == 0 else 2

    def one(n, source):
        ctf = metas[n : n + 1, :LANES].astype(jnp.float32)
        weight_row = ctf / noise_ref[...]
        weight = jnp.sum(
            jnp.where(pick, jnp.broadcast_to(weight_row, pick.shape), 0.0), axis=1, keepdims=True
        )
        x = source[n % count].astype(jnp.float32)
        x_re, x_im = x[:, :half], x[:, half:]
        cosv, sinv = cos_ref[n : n + 1, :], sin_ref[n : n + 1, :]
        re = weight * (x_re * cosv - x_im * sinv)
        im = weight * (x_re * sinv + x_im * cosv)
        return re, im, ctf * weight_row

    for g in (*range(1, GROUP), 0):
        source = given[g - 1] if g else own
        if g == 0:
            for fetch in fetches:
                fetch.wait()
        for start in range(g * count, (g + 1) * count, batch):
            done = [one(n, source) for n in range(start, start + batch)]
            for n, (re, im, power) in zip(range(start, start + batch), done):
                at = pl.ds(pl.multiple_of(place_ref[place_at, n], PAD), cycles)
                total[at, :half] += re
                total[at, half:] += im
                if chunk == 0:
                    powers[pl.ds(place_ref[1, n], 1), :] += power
    if chunk == 0:
        blocks = powers.shape[0] // PAD
        for b in range(blocks):
            at = slice((b + 1) * size - PAD, (b + 1) * size)
            total[at, :LANES] = powers[b * PAD : (b + 1) * PAD]
    rows = keep_ref.shape[0]
    keep_ref[...] = total[:rows]
    give_ref[...] = total[rows:]
    if chunk == 0:
        for save in saves:
            save.wait()


def class_sums(scalars, view, chunk, given, meta, noise, shared, slice_cycles, far, rows, shards):
    width = view.shape[-1]
    count = view.shape[2] if view.shape[0] == 2 else view.shape[0]
    first = chunk == 0
    particles = count * GROUP
    out = pltpu.VMEM((rows, width), jnp.float32)
    kinds = [
        ((8, LANES), jnp.int32),
        ((particles, 2 * LANES), given[0].dtype),
        ((particles, width // 2), jnp.float32),
        ((particles, width // 2), jnp.float32),
    ]
    shapes = [out, out] + ([pltpu.HBM(shape, dtype) for shape, dtype in kinds] if first else [])
    scratch = [
        pltpu.VMEM((2 * rows, width), jnp.float32),
        pltpu.VMEM((count, PAD, width), view.dtype),
    ]
    if first:
        scratch += [pltpu.VMEM((shards * PAD, LANES), jnp.float32)]
        scratch += [pltpu.VMEM(shape, dtype) for shape, dtype in kinds]
    ins = [meta] if first else []
    return pl.pallas_call(
        functools.partial(
            sums_kernel, slice_cycles=slice_cycles, far=far, chunk=chunk, shards=shards
        ),
        out_shape=shapes,
        in_specs=[SCALARS] * 3 + [HERE] * (len(ins) + 1) + [THERE]
        + [HERE] * (GROUP - 1 + len(shared)),
        out_specs=[HERE, HERE] + [THERE] * (len(shapes) - 2),
        scratch_shapes=scratch
        + [pltpu.SMEM((8, LANES), jnp.int32), pltpu.SemaphoreType.DMA((5 + SPLITS,))],
        cost_estimate=cost(2.5),
        compiler_params=room(((2 * rows, width), 8), ((particles * PAD, width), 4)),
    )(*scalars, *held_near(*ins), noise, *held_far(view), *held_near(*given, *shared))


def spans(rows):
    return [(at, min(LANES, rows - at)) for at in range(0, rows, LANES)]


def encode(value, out, rows):
    codes = jnp.zeros((PAD, LANES), jnp.float32)
    blocks = spans(rows)
    for i, (start, size) in enumerate(blocks):
        x = value[start : start + size]
        scaled, code = coded(x)
        out[start : start + size, :] = scaled
        eye = iota((size, LANES), 0) == iota((size, LANES), 1)
        row = jnp.sum(jnp.where(eye, code, 0.0), axis=0, keepdims=True)
        codes = jnp.where(iota((PAD, LANES), 0) == i, row, codes)
    out[rows:, :] = jnp.zeros((PAD, out.shape[1]), jnp.int16)
    if value.shape[0] > rows:
        scaled, code = coded(value[rows:, :LANES])
        out[rows:, :LANES] = scaled
        eye = iota((PAD, LANES), 0) == iota((PAD, LANES), 1)
        row = jnp.sum(jnp.where(eye, code, 0.0), axis=0, keepdims=True)
        codes = jnp.where(iota((PAD, LANES), 0) == len(blocks), row, codes)
    out[rows:, LANES : 2 * LANES] = codes.astype(jnp.int32).astype(jnp.int16)


def coded(x):
    top = jnp.maximum(jnp.max(jnp.abs(x), axis=1, keepdims=True), 1e-30)
    code = jnp.floor(jnp.log(top) / UNIT) + 1.0
    scaled = jnp.round(x * (jnp.exp(-code * UNIT) * 32767.0))
    return jnp.clip(scaled, -32767.0, 32767.0).astype(jnp.int32).astype(jnp.int16), code


def decode(ref):
    rows = ref.shape[0] - PAD
    codes = ref[rows:, LANES : 2 * LANES].astype(jnp.int32).astype(jnp.float32)
    parts = []
    for i, (start, size) in enumerate(spans(rows)):
        parts.append(ref[start : start + size, :].astype(jnp.int32).astype(jnp.float32) * scale(codes, i, size))
    return jnp.concatenate(parts, axis=0)


def decode_power(ref):
    rows = ref.shape[0] - PAD
    codes = ref[rows:, LANES : 2 * LANES].astype(jnp.int32).astype(jnp.float32)
    x = ref[rows:, :LANES].astype(jnp.int32).astype(jnp.float32)
    return x * scale(codes, len(spans(rows)), PAD)


def scale(codes, i, size):
    eye = iota((size, LANES), 0) == iota((size, LANES), 1)
    row = jnp.broadcast_to(codes[i : i + 1], (size, LANES))
    code = jnp.sum(jnp.where(eye, row, 0.0), axis=1, keepdims=True)
    return jnp.exp(code * UNIT) * (1.0 / 32767.0)


def shard_kernel(bit_ref, keep_ref, get_ref, own_ref, code_ref, *, was_coded):
    parts, rows, _ = own_ref.shape
    full = code_ref.shape[1] - PAD
    if was_coded:
        for p in range(2 * parts):
            keep_ref[p, :full] = keep_ref[p, :full] + decode(get_ref.at[p])
            if rows > full:
                keep_ref[p, full:, :LANES] = keep_ref[p, full:, :LANES] + decode_power(get_ref.at[p])
    bit = bit_ref[0]
    for p in range(parts):
        mine, other = bit * parts + p, (1 - bit) * parts + p
        if was_coded:
            encode(keep_ref[other], code_ref.at[p], full)
            own_ref[p] = keep_ref[mine]
        else:
            encode(keep_ref[other] + get_ref[other], code_ref.at[p], full)
            own_ref[p] = keep_ref[mine] + get_ref[mine]


def split_shards(bit, keep, get, full):
    parts, rows, width = keep.shape
    parts = parts // 2
    own = pltpu.VMEM((parts, rows, width), jnp.float32)
    code = pltpu.VMEM((parts, full + PAD, width), jnp.int16)
    return pl.pallas_call(
        functools.partial(shard_kernel, was_coded=get.dtype == jnp.int16),
        out_shape=(own, code),
        in_specs=[SCALARS, HERE, HERE],
        out_specs=(HERE, HERE),
        cost_estimate=cost(1.5),
        compiler_params=room((keep.shape, 16)),
    )(bit, *held_near(keep, get))


def ahead_kernel(keep_ref, get_ref, power_ref, code_ref, total):
    full = keep_ref.shape[0] - PAD
    total[:full] = keep_ref[:full] + decode(get_ref)
    total[full:, :] = jnp.zeros((PAD, total.shape[1]), jnp.float32)
    total[full:, :LANES] = keep_ref[full:, :LANES] + decode_power(get_ref)
    power_ref[...] = total[full:, :LANES]
    encode(total, code_ref, full)


def ahead(keep, get):
    rows, width = keep.shape
    return pl.pallas_call(
        ahead_kernel,
        out_shape=(
            pltpu.VMEM((PAD, LANES), jnp.float32),
            pltpu.VMEM((rows, width), jnp.int16),
        ),
        in_specs=[HERE, HERE],
        out_specs=(HERE, HERE),
        scratch_shapes=[pltpu.VMEM((rows, width), jnp.float32)],
        cost_estimate=cost(1),
        compiler_params=room((keep.shape, 20)),
        name="ahead",
    )(*held_near(keep, get))


def final_kernel(dom_ref, keep_ref, get_ref, power_ref, came_ref, out):
    classes, cycles, _ = out.shape
    sums = keep_ref[...] + decode(get_ref) + decode(came_ref)
    powers = power_ref[...] + decode_power(came_ref)
    r = iota((cycles, LANES), 0)
    pick = iota((cycles, LANES), 1) == dom_ref[0] * cycles + r
    for k in range(classes):
        row = jnp.broadcast_to(powers[k : k + 1], pick.shape)
        denom = jnp.sum(jnp.where(pick, row, 0.0), axis=1, keepdims=True) + 1.0
        out[k] = sums[k * cycles : (k + 1) * cycles, :] / denom


def finish(dom, keep, get, power, came, classes, cycles, width):
    out = (classes, cycles, width)
    return pl.pallas_call(
        final_kernel,
        out_shape=jax.ShapeDtypeStruct(out, jnp.float32),
        in_specs=[SCALARS] + [HERE] * 4,
        out_specs=HERE,
        cost_estimate=cost(1),
        compiler_params=room((out, 16)),
        name="finish",
    )(dom, *held_near(keep, get, power, came))


def decoded(get):
    rows = get.shape[0] - PAD
    codes = get[rows:, LANES : 2 * LANES].astype(jnp.float32)
    values = get.astype(jnp.float32)
    scales = jnp.exp(codes * UNIT) * (1.0 / 32767.0)
    blocks = len(spans(rows))
    full = values[:rows] * scales[:blocks].reshape(-1)[:rows, None]
    return full, values[rows:, :LANES] * scales[blocks, :PAD, None]


def per_device(spectra, ctf, noise_power, references, owner, sub_class, rotation):
    count, cycles, width = spectra.shape
    k_local = references.shape[0]
    domains, shards = lax.axis_size("dom"), lax.axis_size("cls")
    dom, cls = lax.axis_index("dom"), lax.axis_index("cls")
    far = domains // GROUP
    slice_cycles = cycles // domains
    near = (dom & (GROUP - 1)).reshape(1)
    top = (dom // (domains // 2)).reshape(1)
    noise = noise_power.reshape(1, cycles)

    if slice_cycles == PAD:
        view = spectra.reshape(count, 2, GROUP, PAD, width)
    else:
        view = spectra.reshape(count, 2, far // 2, GROUP, slice_cycles, width)
        view = view.transpose(1, 3, 0, 2, 4, 5).reshape(2, GROUP, count, PAD, width)
    rows_of = [v.reshape(1, count) for v in (owner, sub_class, rotation)]
    meta, *sent_0 = pieces(near, top, view, 0, (ctf, *rows_of))
    sent = (sent_0, pieces(near, top, view, 1, ()))
    got = [[swap(sent[c][m - 1], "dom", m) for m in range(1, GROUP)] for c in range(CHUNKS)]

    held, mask = references, 2
    own_side, other_side = references, None
    while mask < shards:
        new = swap(held, "cls", mask)
        other_side = new if other_side is None else jnp.concatenate([other_side, new], axis=0)
        held = jnp.concatenate([held, new], axis=0) if 2 * mask < shards else held
        mask *= 2
    table, low = rotation_table(spectra, references.shape[1])
    near_refs = swap(own_side, "cls", 1)
    per = count // NEAR_CALLS
    before = []
    for i in range(NEAR_CALLS):
        before += score(low, ctf, noise, own_side, near_refs, table, (), i * per, per)
    far_refs = swap(other_side, "cls", 1)
    row = score(low, ctf, noise, other_side, far_refs, table, before, 0, count)
    log_evidence = row.reshape(count)

    scalars = (near, top, cls.reshape(1))
    ends, shared = [], []
    for chunk in range(CHUNKS):
        size = k_local * PAD + (PAD if chunk == 0 else 0)
        keep, give, *more = class_sums(
            scalars, view, chunk, got[chunk], meta, noise, shared, slice_cycles, far,
            shards // 2 * size, shards,
        )
        shared = more
        get = swap(give, "cls", 1)
        shape = (shards // 2, size, width)
        keep, get = keep.reshape(shape), get.reshape(shape)
        mask = shards // 2
        while mask >= 2:
            bit = ((cls // mask) & 1).reshape(1)
            keep, code = split_shards(bit, keep, get, k_local * PAD)
            get = swap(code, "cls", mask)
            mask //= 2
        ends.append((keep[0], get[0]))
    power, code = ahead(*ends[0])
    came = swap(code, "dom", domains // 2)
    if far == 2:
        new_refs = finish(dom.reshape(1), *ends[1], power, came, k_local, slice_cycles, width)
        return (new_refs, log_evidence)

    came, came_power = decoded(came)
    keep, get = ends[1]
    numer = (keep + decoded(get)[0] + came).reshape(k_local, PAD, width)
    power = power + came_power
    left, mask = PAD, domains // 4
    while mask >= GROUP:
        bit = (dom // mask) & 1
        left = left // 2
        own = lax.dynamic_slice_in_dim(numer, bit * left, left, 1)
        other = lax.dynamic_slice_in_dim(numer, (1 - bit) * left, left, 1)
        numer = own + swap(other, "dom", mask)
        power = power + swap(power, "dom", mask)
        mask //= 2
    denom = lax.dynamic_slice_in_dim(power[:k_local], dom * left, left, 1)
    return (numer / (denom + 1.0)[:, :, None], log_evidence)


def solution(mesh):
    return jax.shard_map(
        per_device,
        mesh=mesh,
        in_specs=(
            P(("dom", "cls"), None, None),
            P(("dom", "cls"), None),
            P(),
            P("cls", None, None),
            P(("dom", "cls"), None),
            P(("dom", "cls")),
            P(("dom", "cls")),
        ),
        out_specs=(P("cls", "dom", None), P(("dom", "cls"))),
        check_vma=False,
    )
```

```python
import functools
import math

import jax
import jax.numpy as jnp
from jax import lax
from jax.experimental import pallas as pl
from jax.experimental.pallas import tpu as pltpu
from jax.sharding import PartitionSpec as P


CHUNKS = 2
GROUP = 4
NEAR_CALLS = 2
SPLITS = 4
LANES = 128
PAD = 16
STEPS = 64.0
UNIT = math.log(2.0) / STEPS


def table_kernel(image_ref, out_ref, low_ref, sems):
    width, turns_all = out_ref.shape
    count, cycles, _ = low_ref.shape
    part = count // SPLITS
    copies = [
        pltpu.make_async_copy(
            image_ref.at[pl.ds(i * part, part), :cycles, :], low_ref.at[pl.ds(i * part, part)], sems.at[i]
        )
        for i in range(SPLITS)
    ]
    for copy in copies:
        copy.start()
    half = width // 2
    quarter = half // 2
    step = 32
    for at in range(0, quarter, step):
        shape = (step, turns_all)
        turns = (iota(shape, 0) + at) * iota(shape, 1) & (turns_all - 1)
        angle = turns.astype(jnp.float32) * (2.0 * math.pi / turns_all)
        cosv, sinv = jnp.cos(angle), jnp.sin(angle)
        odd, back = (iota(shape, 1) & 1) == 1, (iota(shape, 1) & 2) == 2
        cos_on, sin_on = jnp.where(odd, -sinv, cosv), jnp.where(odd, cosv, sinv)
        cos_on, sin_on = jnp.where(back, -cos_on, cos_on), jnp.where(back, -sin_on, sin_on)
        out_ref[at : at + step, :] = cosv.astype(jnp.bfloat16)
        out_ref[quarter + at : quarter + at + step, :] = cos_on.astype(jnp.bfloat16)
        out_ref[half + at : half + at + step, :] = (-sinv).astype(jnp.bfloat16)
        at = half + quarter + at
        out_ref[at : at + step, :] = (-sin_on).astype(jnp.bfloat16)
    for copy in copies:
        copy.wait()


def rotation_table(spectra, cycles):
    count, _, width = spectra.shape
    return pl.pallas_call(
        table_kernel,
        out_shape=(
            pltpu.VMEM((width, width), jnp.bfloat16),
            pltpu.VMEM((count, cycles, width), spectra.dtype),
        ),
        in_specs=[THERE],
        out_specs=(HERE, HERE),
        scratch_shapes=[pltpu.SemaphoreType.DMA((SPLITS,))],
        cost_estimate=cost(2),
        compiler_params=room(((width, width), 4)),
        name="table",
    )(*held_far(spectra))


def held_near(*values):
    return [pltpu.with_memory_space_constraint(v, pltpu.VMEM) for v in values]


def held_far(*values):
    return [pltpu.with_memory_space_constraint(v, pltpu.HBM) for v in values]


def swap(value, axis, mask):
    size = lax.axis_size(axis)
    return lax.ppermute(value, axis, [(i, i ^ mask) for i in range(size)])


def iota(shape, axis):
    return lax.broadcasted_iota(jnp.int32, shape, axis)


HERE = pl.BlockSpec(memory_space=pltpu.VMEM)
SCALARS = pl.BlockSpec(memory_space=pltpu.SMEM)
THERE = pl.BlockSpec(memory_space=pltpu.HBM)


def room(*arrays):
    size = sum(math.prod(shape) * bits for shape, bits in arrays)
    return pltpu.CompilerParams(vmem_limit_bytes=size + (8 << 20))


def cost(us):
    return pl.CostEstimate(flops=0, transcendentals=0, bytes_accessed=int(us * 3.6e6))


def score_kernel(
    low_ref, ctf_ref, noise_ref, first_ref, second_ref, table_ref, *refs, merge, start
):
    before, refs = refs[:merge], refs[merge:]
    outs, refs = refs[: 1 if merge else 2], refs[1 if merge else 2 :]
    image, image_sum, staged, classes, cross = refs
    _, cycles, width = low_ref.shape
    tiles = width // LANES
    pairs = tiles // 2
    count = image.shape[1] // cycles
    kinds = cross.shape[0] // count
    part = first_ref.shape[0]
    ctf = ctf_ref[start : start + count, :].astype(jnp.float32)
    weight = ctf / noise_ref[...]
    power = ctf * weight
    eye = iota((cycles, LANES), 0) == iota((cycles, LANES), 1)
    for at, ref in ((0, first_ref), (part, second_ref)):
        for f in range(tiles):
            staged[f, at : at + part, :] = ref[:, f * LANES : (f + 1) * LANES].astype(jnp.float32)
    blocks = kinds // 8
    zero = jnp.zeros((8, LANES), jnp.float32)
    norms = []
    for b in range(blocks):
        square = jnp.zeros((cycles, 8, LANES), jnp.float32)
        for f in range(pairs):
            rows = pl.ds(b * 8 * cycles, 8 * cycles)
            re = jnp.swapaxes(staged[f, rows, :].reshape(8, cycles, LANES), 0, 1)
            im = jnp.swapaxes(staged[f + pairs, rows, :].reshape(8, cycles, LANES), 0, 1)
            classes[3 * f, :, b * 8 : b * 8 + 8, :] = re
            classes[3 * f + 1, :, b * 8 : b * 8 + 8, :] = re - im
            classes[3 * f + 2, :, b * 8 : b * 8 + 8, :] = re + im
            square = square + (re * re + im * im)
        norm = zero
        for r in range(cycles):
            total = jnp.sum(square[r], axis=1, keepdims=True)
            norm = jnp.where(iota((8, LANES), 1) == r, total, norm)
        norms.append(norm)
    for n in range(count):
        row = jnp.broadcast_to(weight[n : n + 1, :], (cycles, LANES))
        column = jnp.sum(jnp.where(eye, row, 0.0), axis=1, keepdims=True)
        low = low_ref[start + n].astype(jnp.float32)
        weighted = (column * low).astype(jnp.bfloat16).astype(jnp.float32)
        for f in range(tiles):
            image[f, n * cycles : (n + 1) * cycles, :] = weighted[:, f * LANES : (f + 1) * LANES]
        for f in range(pairs):
            re = weighted[:, f * LANES : (f + 1) * LANES]
            im = weighted[:, (f + pairs) * LANES : (f + pairs + 1) * LANES]
            image_sum[f, n * cycles : (n + 1) * cycles, :] = re + im
    group = 2
    for f in range(pairs):

        def particles(g, _):
            def cycle(r, sums):
                new = list(sums)
                for i in range(group):
                    row = pl.ds((g * group + i) * cycles + r, 8, stride=0)
                    a_sum, a_im, a_re = image_sum[f, row, :], image[f + pairs, row, :], image[f, row, :]
                    for b in range(blocks):
                        at = slice(b * 8, b * 8 + 8)
                        j = 3 * (i * blocks + b)
                        new[j] = new[j] + classes[3 * f, r, at, :] * a_sum
                        new[j + 1] = new[j + 1] + classes[3 * f + 1, r, at, :] * a_im
                        new[j + 2] = new[j + 2] + classes[3 * f + 2, r, at, :] * a_re
                return tuple(new)

            sums = lax.fori_loop(0, cycles, cycle, (zero,) * (3 * group * blocks), unroll=4)
            for i in range(group):
                for b in range(blocks):
                    s1, s2, s3 = sums[3 * (i * blocks + b) : 3 * (i * blocks + b) + 3]
                    at = pl.ds(pl.multiple_of((g * group + i) * kinds + b * 8, 8), 8)
                    cross[at, f * LANES : (f + 1) * LANES] = s1 - s2
                    cross[at, (f + pairs) * LANES : (f + pairs + 1) * LANES] = s1 - s3
            return 0

        lax.fori_loop(0, count // group, particles, 0)
    scores = jnp.dot(
        cross[...].astype(jnp.bfloat16), table_ref[...], preferred_element_type=jnp.float32
    )
    cross[...] = scores
    inner = iota((8, LANES), 1) < cycles
    row = jnp.zeros(outs[0].shape, jnp.float32)
    for n in range(count):
            mine = []
            for b in range(blocks):
                powers = jnp.where(inner, jnp.broadcast_to(power[n : n + 1, :], (8, LANES)), 0.0)
                energy = jnp.sum(powers * norms[b], axis=1, keepdims=True)
                at = n * kinds + b * 8
                mine.append(cross[at : at + 8, :] - 0.5 * energy)
            mine = jnp.concatenate(mine, axis=0)
            top = jnp.max(mine, axis=(0, 1), keepdims=True)
            if merge:
                per = count // (merge // 2)
                pair, i = before[n // per * 2 : n // per * 2 + 2], n % per
                top_before, total_before = pair[0][i : i + 1, :], pair[1][i : i + 1, :]
                top = jnp.maximum(top, jnp.max(top_before, axis=1, keepdims=True))
            total = jnp.sum(jnp.exp(mine - top), axis=(0, 1), keepdims=True)
            if merge:
                total = total + (total_before * jnp.exp(top_before - top))[:, :1]
                here = iota(row.shape, 1) == start + n
                row = jnp.where(here, jnp.broadcast_to(top + jnp.log(total), row.shape), row)
            else:
                outs[0][n : n + 1, :] = jnp.broadcast_to(top, (1, LANES))
                outs[1][n : n + 1, :] = jnp.broadcast_to(total, (1, LANES))
    if merge:
        outs[0][...] = row


def score(low, ctf, noise, first, second, table, before, start, count):
    _, cycles, width = low.shape
    kinds = 2 * first.shape[0]
    merge = len(before)
    each = pltpu.VMEM((count, LANES), jnp.float32)
    row = jax.ShapeDtypeStruct((1, count), jnp.float32)
    part = (kinds // 2 * cycles, width)
    return pl.pallas_call(
        functools.partial(score_kernel, merge=merge, start=start),
        out_shape=row if merge else (each, each),
        in_specs=[HERE] * (6 + merge),
        out_specs=HERE if merge else (HERE, HERE),
        scratch_shapes=[
            pltpu.VMEM((width // LANES, count * cycles, LANES), jnp.float32),
            pltpu.VMEM((width // LANES // 2, count * cycles, LANES), jnp.float32),
            pltpu.VMEM((width // LANES, kinds * cycles, LANES), jnp.float32),
            pltpu.VMEM((width // LANES // 2 * 3, cycles, kinds, LANES), jnp.float32),
            pltpu.VMEM((count * kinds, width), jnp.float32),
        ],
        cost_estimate=cost(count / 2),
        compiler_params=room(
            ((count * cycles, width), 8),
            ((kinds * cycles, width), 12),
            ((count * kinds, width), 8),
            (table.shape, 2),
        ),
    )(
        *held_near(low), ctf, noise, *held_near(first.reshape(part), second.reshape(part), table),
        *before,
    )


def part_of(view_ref, top, near):
    if view_ref.shape[0] == 2:
        return view_ref.at[top, near]
    return view_ref.at[:, top, near]


def column(row):
    size = row.shape[1]
    eye = iota((size, size), 0) == iota((size, size), 1)
    return jnp.sum(jnp.where(eye, jnp.broadcast_to(row, (size, size)), 0.0), axis=1, keepdims=True)


def pieces_kernel(near_ref, top_ref, view_ref, *refs, chunk):
    outs, sems = refs[:-1], refs[-1]
    if chunk == 0:
        ctf_ref, owner_ref, sub_ref, turn_ref, meta_ref = refs[:5]
        outs = refs[5 : 5 + GROUP - 1]
        ctf_here, owner_here, sub_here, turn_here, small, sems = refs[5 + GROUP - 1 :]
        fetches = [
            pltpu.make_async_copy(there, here, small.at[i])
            for i, (there, here) in enumerate(
                ((ctf_ref, ctf_here), (owner_ref, owner_here), (sub_ref, sub_here), (turn_ref, turn_here))
            )
        ]
        for fetch in fetches:
            fetch.start()
    count = view_ref.shape[2] if view_ref.shape[0] == 2 else view_ref.shape[0]
    part = count // SPLITS
    first = 1 if chunk == 0 else 0
    copies = [
        pltpu.make_async_copy(
            part_of(view_ref, top_ref[0] ^ (1 - chunk), near_ref[0] ^ (i + first)).at[
                pl.ds(j * part, part)
            ],
            out.at[pl.ds(j * part, part)],
            sems.at[i * SPLITS + j],
        )
        for i, out in enumerate(outs)
        for j in range(SPLITS)
    ]
    for copy in copies:
        copy.start()
    if chunk == 0:
        for fetch in fetches:
            fetch.wait()
        cycles = ctf_ref.shape[1]
        turn = turn_here[...]
        shape = (count, meta_ref.shape[1] - cycles)
        at = iota(shape, 1)
        rest = jnp.where(at == 0, column((turn >> 4).astype(jnp.float32)), 0.0)
        rest = jnp.where(at == 1, column((turn & 15).astype(jnp.float32)), rest)
        rest = jnp.where(at == 2, column(owner_here[...].astype(jnp.float32)), rest)
        rest = jnp.where(at == 3, column(sub_here[...].astype(jnp.float32)), rest)
        meta_ref[:, :cycles] = ctf_here[...]
        meta_ref[:, cycles:] = rest.astype(jnp.bfloat16)
        for out in outs:
            out[count, :, :] = jnp.zeros(out.shape[1:], out.dtype)
            out[count, :, : meta_ref.shape[1]] = meta_ref[...]
    for copy in copies:
        copy.wait()


def pieces(near, top, view, chunk, others):
    count, width = view.shape[2] if view.shape[0] == 2 else view.shape[0], view.shape[-1]
    out = pltpu.VMEM((count + (chunk == 0), PAD, width), view.dtype)
    shapes, specs = [out] * (GROUP - 1), [HERE] * (GROUP - 1)
    scratch = [pltpu.SemaphoreType.DMA((GROUP * SPLITS,))]
    if chunk == 1:
        shapes = [pltpu.HBM((count, PAD, width), view.dtype)] + shapes
        specs = [THERE] + specs
    if chunk == 0:
        ctf = others[0]
        shapes = [pltpu.VMEM((count, 2 * ctf.shape[1]), view.dtype)] + shapes
        specs = [HERE] + specs
        scratch = [
            pltpu.VMEM(ctf.shape, ctf.dtype),
            pltpu.VMEM((1, count), jnp.int32),
            pltpu.VMEM((1, count), jnp.int32),
            pltpu.VMEM((1, count), jnp.int32),
            pltpu.SemaphoreType.DMA((4,)),
        ] + scratch
    return pl.pallas_call(
        functools.partial(pieces_kernel, chunk=chunk),
        out_shape=shapes,
        in_specs=[SCALARS] * 2 + [THERE] * (1 + len(others)),
        out_specs=specs,
        scratch_shapes=scratch,
        cost_estimate=cost(1.5),
        compiler_params=room(((count * PAD, width), 2 * GROUP)),
    )(near, top, *held_far(view, *others))


def sums_kernel(
    near_ref, top_ref, cls_ref, *refs, slice_cycles, far, chunk, shards,
):
    if chunk == 0:
        meta_ref, refs = refs[0], refs[1:]
    noise_ref, view_ref, refs = refs[0], refs[1], refs[2:]
    given, refs = refs[: GROUP - 1], refs[GROUP - 1 :]
    if chunk == 0:
        keep_ref, give_ref = refs[:2]
        shared, refs = refs[2:6], refs[6:]
        total, own, powers, plan, metas, cos_ref, sin_ref, place_ref, sems = refs
    else:
        plan, metas, cos_ref, sin_ref, own = refs[:5]
        keep_ref, give_ref, total, place_ref, sems = refs[5:]
    cycles, half = PAD, cos_ref.shape[1]
    side = top_ref[0] ^ (1 - chunk)
    particles = cos_ref.shape[0]
    count = particles // GROUP
    width = 2 * half
    size = keep_ref.shape[0] // (shards // 2)
    part = count // SPLITS
    fetches = [
        pltpu.make_async_copy(
            part_of(view_ref, side, near_ref[0]).at[pl.ds(i * part, part)],
            own.at[pl.ds(i * part, part)],
            sems.at[5 + i],
        )
        for i in range(SPLITS if chunk == 0 else 0)
    ]
    for fetch in fetches:
        fetch.start()
    schedule = pltpu.make_async_copy(plan, place_ref, sems.at[0])
    if chunk == 0:
        metas[:count] = meta_ref[...]
        for g, piece in enumerate(given):
            metas[(g + 1) * count : (g + 2) * count] = piece[count, :, : metas.shape[1]]
        ints = metas[:, LANES : LANES + LANES].astype(jnp.float32).astype(jnp.int32)
        turn = ints[:, 0:1] * 16 + ints[:, 1:2]
        shard, inside = ints[:, 2:3], ints[:, 3:4]
        block = ((shard ^ cls_ref[0]) & 1) * (shards // 2) + (shard >> 1)
        here = iota((particles, LANES), 0) == iota((particles, LANES), 1)

        def in_row(values):
            return jnp.sum(jnp.where(here, values.astype(jnp.float32), 0.0), axis=0, keepdims=True)

        rows = (
            in_row(block * size + inside * cycles),
            in_row(block * PAD + inside),
            in_row(block * (size - PAD) + inside * cycles),
        )
        at = iota(plan.shape, 0)
        places = jnp.where(at == 0, rows[0], jnp.where(at == 1, rows[1], rows[2]))
        plan[...] = places.astype(jnp.int32)
        schedule.start()
        total[...] = jnp.zeros_like(total)
        powers[...] = jnp.zeros_like(powers)
        turns = iota((particles, half), 1) * turn & (width - 1)
        angle = turns.astype(jnp.float32) * (2.0 * math.pi / width)
        cos_ref[...] = jnp.cos(angle)
        sin_ref[...] = jnp.sin(angle)
        saves = [
            pltpu.make_async_copy(here, there, sems.at[1 + i])
            for i, (here, there) in enumerate(zip((plan, metas, cos_ref, sin_ref), shared))
        ]
        for save in saves:
            save.start()
    else:
        schedule.start()
        total[...] = jnp.zeros_like(total)
    r = iota((cycles, LANES), 0)
    domain = (side * (far // 2) + r // slice_cycles) * GROUP + near_ref[0]
    pick = iota((cycles, LANES), 1) == domain * slice_cycles + r % slice_cycles
    batch = 2
    schedule.wait()
    place_at = 0 if chunk == 0 else 2

    def one(n, source):
        ctf = metas[n : n + 1, :LANES].astype(jnp.float32)
        weight_row = ctf / noise_ref[...]
        weight = jnp.sum(
            jnp.where(pick, jnp.broadcast_to(weight_row, pick.shape), 0.0), axis=1, keepdims=True
        )
        x = source[n % count].astype(jnp.float32)
        x_re, x_im = x[:, :half], x[:, half:]
        cosv, sinv = cos_ref[n : n + 1, :], sin_ref[n : n + 1, :]
        re = weight * (x_re * cosv - x_im * sinv)
        im = weight * (x_re * sinv + x_im * cosv)
        return re, im, ctf * weight_row

    for g in (*range(1, GROUP), 0):
        source = given[g - 1] if g else own
        if g == 0:
            for fetch in fetches:
                fetch.wait()
        for start in range(g * count, (g + 1) * count, batch):
            done = [one(n, source) for n in range(start, start + batch)]
            for n, (re, im, power) in zip(range(start, start + batch), done):
                at = pl.ds(pl.multiple_of(place_ref[place_at, n], PAD), cycles)
                total[at, :half] += re
                total[at, half:] += im
                if chunk == 0:
                    powers[pl.ds(place_ref[1, n], 1), :] += power
    if chunk == 0:
        blocks = powers.shape[0] // PAD
        for b in range(blocks):
            at = slice((b + 1) * size - PAD, (b + 1) * size)
            total[at, :LANES] = powers[b * PAD : (b + 1) * PAD]
    rows = keep_ref.shape[0]
    keep_ref[...] = total[:rows]
    give_ref[...] = total[rows:]
    if chunk == 0:
        for save in saves:
            save.wait()


def class_sums(scalars, view, chunk, given, meta, noise, shared, slice_cycles, far, rows, shards):
    width = view.shape[-1]
    count = view.shape[2] if view.shape[0] == 2 else view.shape[0]
    first = chunk == 0
    particles = count * GROUP
    out = pltpu.VMEM((rows, width), jnp.float32)
    kinds = [
        ((8, LANES), jnp.int32),
        ((particles, 2 * LANES), given[0].dtype),
        ((particles, width // 2), jnp.float32),
        ((particles, width // 2), jnp.float32),
    ]
    shapes = [out, out] + ([pltpu.HBM(shape, dtype) for shape, dtype in kinds] if first else [])
    scratch = [pltpu.VMEM((2 * rows, width), jnp.float32)]
    if first:
        scratch += [pltpu.VMEM((count, PAD, width), view.dtype)]
        scratch += [pltpu.VMEM((shards * PAD, LANES), jnp.float32)]
        scratch += [pltpu.VMEM(shape, dtype) for shape, dtype in kinds]
    ins = [meta] if first else []
    return pl.pallas_call(
        functools.partial(
            sums_kernel, slice_cycles=slice_cycles, far=far, chunk=chunk, shards=shards
        ),
        out_shape=shapes,
        in_specs=[SCALARS] * 3 + [HERE] * (len(ins) + 1) + [THERE]
        + [HERE] * (GROUP - 1 + len(shared)),
        out_specs=[HERE, HERE] + [THERE] * (len(shapes) - 2),
        scratch_shapes=scratch
        + [pltpu.SMEM((8, LANES), jnp.int32), pltpu.SemaphoreType.DMA((5 + SPLITS,))],
        cost_estimate=cost(2.5),
        compiler_params=room(((2 * rows, width), 8), ((particles * PAD, width), 4)),
    )(*scalars, *held_near(*ins), noise, *held_far(view), *held_near(*given, *shared))


def spans(rows):
    return [(at, min(LANES, rows - at)) for at in range(0, rows, LANES)]


def encode(value, out, rows):
    codes = jnp.zeros((PAD, LANES), jnp.float32)
    blocks = spans(rows)
    for i, (start, size) in enumerate(blocks):
        x = value[start : start + size]
        scaled, code = coded(x)
        out[start : start + size, :] = scaled
        eye = iota((size, LANES), 0) == iota((size, LANES), 1)
        row = jnp.sum(jnp.where(eye, code, 0.0), axis=0, keepdims=True)
        codes = jnp.where(iota((PAD, LANES), 0) == i, row, codes)
    out[rows:, :] = jnp.zeros((PAD, out.shape[1]), jnp.int16)
    if value.shape[0] > rows:
        scaled, code = coded(value[rows:, :LANES])
        out[rows:, :LANES] = scaled
        eye = iota((PAD, LANES), 0) == iota((PAD, LANES), 1)
        row = jnp.sum(jnp.where(eye, code, 0.0), axis=0, keepdims=True)
        codes = jnp.where(iota((PAD, LANES), 0) == len(blocks), row, codes)
    out[rows:, LANES : 2 * LANES] = codes.astype(jnp.int32).astype(jnp.int16)


def coded(x):
    top = jnp.maximum(jnp.max(jnp.abs(x), axis=1, keepdims=True), 1e-30)
    code = jnp.floor(jnp.log(top) / UNIT) + 1.0
    scaled = jnp.round(x * (jnp.exp(-code * UNIT) * 32767.0))
    return jnp.clip(scaled, -32767.0, 32767.0).astype(jnp.int32).astype(jnp.int16), code


def decode(ref):
    rows = ref.shape[0] - PAD
    codes = ref[rows:, LANES : 2 * LANES].astype(jnp.int32).astype(jnp.float32)
    parts = []
    for i, (start, size) in enumerate(spans(rows)):
        parts.append(ref[start : start + size, :].astype(jnp.int32).astype(jnp.float32) * scale(codes, i, size))
    return jnp.concatenate(parts, axis=0)


def decode_power(ref):
    rows = ref.shape[0] - PAD
    codes = ref[rows:, LANES : 2 * LANES].astype(jnp.int32).astype(jnp.float32)
    x = ref[rows:, :LANES].astype(jnp.int32).astype(jnp.float32)
    return x * scale(codes, len(spans(rows)), PAD)


def scale(codes, i, size):
    eye = iota((size, LANES), 0) == iota((size, LANES), 1)
    row = jnp.broadcast_to(codes[i : i + 1], (size, LANES))
    code = jnp.sum(jnp.where(eye, row, 0.0), axis=1, keepdims=True)
    return jnp.exp(code * UNIT) * (1.0 / 32767.0)


def shard_kernel(bit_ref, keep_ref, get_ref, own_ref, code_ref, *, was_coded):
    parts, rows, _ = own_ref.shape
    full = code_ref.shape[1] - PAD
    if was_coded:
        for p in range(2 * parts):
            keep_ref[p, :full] = keep_ref[p, :full] + decode(get_ref.at[p])
            if rows > full:
                keep_ref[p, full:, :LANES] = keep_ref[p, full:, :LANES] + decode_power(get_ref.at[p])
    bit = bit_ref[0]
    for p in range(parts):
        mine, other = bit * parts + p, (1 - bit) * parts + p
        if was_coded:
            encode(keep_ref[other], code_ref.at[p], full)
            own_ref[p] = keep_ref[mine]
        else:
            encode(keep_ref[other] + get_ref[other], code_ref.at[p], full)
            own_ref[p] = keep_ref[mine] + get_ref[mine]


def split_shards(bit, keep, get, full):
    parts, rows, width = keep.shape
    parts = parts // 2
    own = pltpu.VMEM((parts, rows, width), jnp.float32)
    code = pltpu.VMEM((parts, full + PAD, width), jnp.int16)
    return pl.pallas_call(
        functools.partial(shard_kernel, was_coded=get.dtype == jnp.int16),
        out_shape=(own, code),
        in_specs=[SCALARS, HERE, HERE],
        out_specs=(HERE, HERE),
        cost_estimate=cost(1.5),
        compiler_params=room((keep.shape, 16)),
    )(bit, *held_near(keep, get))


def ahead_kernel(keep_ref, get_ref, power_ref, code_ref, total):
    full = keep_ref.shape[0] - PAD
    total[:full] = keep_ref[:full] + decode(get_ref)
    total[full:, :] = jnp.zeros((PAD, total.shape[1]), jnp.float32)
    total[full:, :LANES] = keep_ref[full:, :LANES] + decode_power(get_ref)
    power_ref[...] = total[full:, :LANES]
    encode(total, code_ref, full)


def ahead(keep, get):
    rows, width = keep.shape
    return pl.pallas_call(
        ahead_kernel,
        out_shape=(
            pltpu.VMEM((PAD, LANES), jnp.float32),
            pltpu.VMEM((rows, width), jnp.int16),
        ),
        in_specs=[HERE, HERE],
        out_specs=(HERE, HERE),
        scratch_shapes=[pltpu.VMEM((rows, width), jnp.float32)],
        cost_estimate=cost(1),
        compiler_params=room((keep.shape, 20)),
        name="ahead",
    )(*held_near(keep, get))


def final_kernel(dom_ref, keep_ref, get_ref, power_ref, came_ref, out):
    classes, cycles, _ = out.shape
    sums = keep_ref[...] + decode(get_ref) + decode(came_ref)
    powers = power_ref[...] + decode_power(came_ref)
    r = iota((cycles, LANES), 0)
    pick = iota((cycles, LANES), 1) == dom_ref[0] * cycles + r
    for k in range(classes):
        row = jnp.broadcast_to(powers[k : k + 1], pick.shape)
        denom = jnp.sum(jnp.where(pick, row, 0.0), axis=1, keepdims=True) + 1.0
        out[k] = sums[k * cycles : (k + 1) * cycles, :] / denom


def finish(dom, keep, get, power, came, classes, cycles, width):
    out = (classes, cycles, width)
    return pl.pallas_call(
        final_kernel,
        out_shape=jax.ShapeDtypeStruct(out, jnp.float32),
        in_specs=[SCALARS] + [HERE] * 4,
        out_specs=HERE,
        cost_estimate=cost(1),
        compiler_params=room((out, 16)),
        name="finish",
    )(dom, *held_near(keep, get, power, came))


def decoded(get):
    rows = get.shape[0] - PAD
    codes = get[rows:, LANES : 2 * LANES].astype(jnp.float32)
    values = get.astype(jnp.float32)
    scales = jnp.exp(codes * UNIT) * (1.0 / 32767.0)
    blocks = len(spans(rows))
    full = values[:rows] * scales[:blocks].reshape(-1)[:rows, None]
    return full, values[rows:, :LANES] * scales[blocks, :PAD, None]


def per_device(spectra, ctf, noise_power, references, owner, sub_class, rotation):
    count, cycles, width = spectra.shape
    k_local = references.shape[0]
    domains, shards = lax.axis_size("dom"), lax.axis_size("cls")
    dom, cls = lax.axis_index("dom"), lax.axis_index("cls")
    far = domains // GROUP
    slice_cycles = cycles // domains
    near = (dom & (GROUP - 1)).reshape(1)
    top = (dom // (domains // 2)).reshape(1)
    noise = noise_power.reshape(1, cycles)

    if slice_cycles == PAD:
        view = spectra.reshape(count, 2, GROUP, PAD, width)
    else:
        view = spectra.reshape(count, 2, far // 2, GROUP, slice_cycles, width)
        view = view.transpose(1, 3, 0, 2, 4, 5).reshape(2, GROUP, count, PAD, width)
    rows_of = [v.reshape(1, count) for v in (owner, sub_class, rotation)]
    meta, *sent_0 = pieces(near, top, view, 0, (ctf, *rows_of))
    own_1, *sent_1 = pieces(near, top, view, 1, ())
    sent = (sent_0, sent_1)
    got = [[swap(sent[c][m - 1], "dom", m) for m in range(1, GROUP)] for c in range(CHUNKS)]

    held, mask = references, 2
    own_side, other_side = references, None
    while mask < shards:
        new = swap(held, "cls", mask)
        other_side = new if other_side is None else jnp.concatenate([other_side, new], axis=0)
        held = jnp.concatenate([held, new], axis=0) if 2 * mask < shards else held
        mask *= 2
    table, low = rotation_table(spectra, references.shape[1])
    near_refs = swap(own_side, "cls", 1)
    per = count // NEAR_CALLS
    before = []
    for i in range(NEAR_CALLS):
        before += score(low, ctf, noise, own_side, near_refs, table, (), i * per, per)
    far_refs = swap(other_side, "cls", 1)
    row = score(low, ctf, noise, other_side, far_refs, table, before, 0, count)
    log_evidence = row.reshape(count)

    scalars = (near, top, cls.reshape(1))
    ends, shared = [], []
    for chunk in range(CHUNKS):
        size = k_local * PAD + (PAD if chunk == 0 else 0)
        keep, give, *more = class_sums(
            scalars, view, chunk, got[chunk], meta, noise, shared, slice_cycles, far,
            shards // 2 * size, shards,
        )
        shared = [*more, own_1]
        get = swap(give, "cls", 1)
        shape = (shards // 2, size, width)
        keep, get = keep.reshape(shape), get.reshape(shape)
        mask = shards // 2
        while mask >= 2:
            bit = ((cls // mask) & 1).reshape(1)
            keep, code = split_shards(bit, keep, get, k_local * PAD)
            get = swap(code, "cls", mask)
            mask //= 2
        ends.append((keep[0], get[0]))
    power, code = ahead(*ends[0])
    came = swap(code, "dom", domains // 2)
    if far == 2:
        new_refs = finish(dom.reshape(1), *ends[1], power, came, k_local, slice_cycles, width)
        return (new_refs, log_evidence)

    came, came_power = decoded(came)
    keep, get = ends[1]
    numer = (keep + decoded(get)[0] + came).reshape(k_local, PAD, width)
    power = power + came_power
    left, mask = PAD, domains // 4
    while mask >= GROUP:
        bit = (dom // mask) & 1
        left = left // 2
        own = lax.dynamic_slice_in_dim(numer, bit * left, left, 1)
        other = lax.dynamic_slice_in_dim(numer, (1 - bit) * left, left, 1)
        numer = own + swap(other, "dom", mask)
        power = power + swap(power, "dom", mask)
        mask //= 2
    denom = lax.dynamic_slice_in_dim(power[:k_local], dom * left, left, 1)
    return (numer / (denom + 1.0)[:, :, None], log_evidence)


def solution(mesh):
    return jax.shard_map(
        per_device,
        mesh=mesh,
        in_specs=(
            P(("dom", "cls"), None, None),
            P(("dom", "cls"), None),
            P(),
            P("cls", None, None),
            P(("dom", "cls"), None),
            P(("dom", "cls")),
            P(("dom", "cls")),
        ),
        out_specs=(P("cls", "dom", None), P(("dom", "cls"))),
        check_vma=False,
    )
```

```python
import functools
import math

import jax
import jax.numpy as jnp
from jax import lax
from jax.experimental import pallas as pl
from jax.experimental.pallas import tpu as pltpu
from jax.sharding import PartitionSpec as P


CHUNKS = 2
GROUP = 4
NEAR_CALLS = 2
SPLITS = 4
LANES = 128
PAD = 16
STEPS = 64.0
UNIT = math.log(2.0) / STEPS


def table_kernel(image_ref, out_ref, low_ref, sems):
    width, turns_all = out_ref.shape
    count, cycles, _ = low_ref.shape
    part = count // SPLITS
    copies = [
        pltpu.make_async_copy(
            image_ref.at[pl.ds(i * part, part), :cycles, :], low_ref.at[pl.ds(i * part, part)], sems.at[i]
        )
        for i in range(SPLITS)
    ]
    for copy in copies:
        copy.start()
    half = width // 2
    quarter = half // 2
    step = 32
    for at in range(0, quarter, step):
        shape = (step, turns_all)
        turns = (iota(shape, 0) + at) * iota(shape, 1) & (turns_all - 1)
        angle = turns.astype(jnp.float32) * (2.0 * math.pi / turns_all)
        cosv, sinv = jnp.cos(angle), jnp.sin(angle)
        odd, back = (iota(shape, 1) & 1) == 1, (iota(shape, 1) & 2) == 2
        cos_on, sin_on = jnp.where(odd, -sinv, cosv), jnp.where(odd, cosv, sinv)
        cos_on, sin_on = jnp.where(back, -cos_on, cos_on), jnp.where(back, -sin_on, sin_on)
        out_ref[at : at + step, :] = cosv.astype(jnp.bfloat16)
        out_ref[quarter + at : quarter + at + step, :] = cos_on.astype(jnp.bfloat16)
        out_ref[half + at : half + at + step, :] = (-sinv).astype(jnp.bfloat16)
        at = half + quarter + at
        out_ref[at : at + step, :] = (-sin_on).astype(jnp.bfloat16)
    for copy in copies:
        copy.wait()


def rotation_table(spectra, cycles):
    count, _, width = spectra.shape
    return pl.pallas_call(
        table_kernel,
        out_shape=(
            pltpu.VMEM((width, width), jnp.bfloat16),
            pltpu.VMEM((count, cycles, width), spectra.dtype),
        ),
        in_specs=[THERE],
        out_specs=(HERE, HERE),
        scratch_shapes=[pltpu.SemaphoreType.DMA((SPLITS,))],
        cost_estimate=cost(2),
        compiler_params=room(((width, width), 4)),
        name="table",
    )(*held_far(spectra))


def held_near(*values):
    return [pltpu.with_memory_space_constraint(v, pltpu.VMEM) for v in values]


def held_far(*values):
    return [pltpu.with_memory_space_constraint(v, pltpu.HBM) for v in values]


def swap(value, axis, mask):
    size = lax.axis_size(axis)
    return lax.ppermute(value, axis, [(i, i ^ mask) for i in range(size)])


def iota(shape, axis):
    return lax.broadcasted_iota(jnp.int32, shape, axis)


HERE = pl.BlockSpec(memory_space=pltpu.VMEM)
SCALARS = pl.BlockSpec(memory_space=pltpu.SMEM)
THERE = pl.BlockSpec(memory_space=pltpu.HBM)


def room(*arrays):
    size = sum(math.prod(shape) * bits for shape, bits in arrays)
    return pltpu.CompilerParams(vmem_limit_bytes=size + (8 << 20))


def cost(us):
    return pl.CostEstimate(flops=0, transcendentals=0, bytes_accessed=int(us * 3.6e6))


def score_kernel(
    low_ref, ctf_ref, noise_ref, first_ref, second_ref, table_ref, *refs, merge, start
):
    before, refs = refs[:merge], refs[merge:]
    outs, refs = refs[: 1 if merge else 2], refs[1 if merge else 2 :]
    image, image_sum, staged, classes, cross = refs[:5]
    copies = []
    if merge:
        there, first_ref, sems = first_ref, refs[5], refs[6]
        part = there.shape[0] // SPLITS
        copies = [
            pltpu.make_async_copy(
                there.at[pl.ds(i * part, part)], first_ref.at[pl.ds(i * part, part)], sems.at[i]
            )
            for i in range(SPLITS)
        ]
    for copy in copies:
        copy.start()
    _, cycles, width = low_ref.shape
    tiles = width // LANES
    pairs = tiles // 2
    count = image.shape[1] // cycles
    kinds = cross.shape[0] // count
    part = first_ref.shape[0]
    ctf = ctf_ref[start : start + count, :].astype(jnp.float32)
    weight = ctf / noise_ref[...]
    power = ctf * weight
    eye = iota((cycles, LANES), 0) == iota((cycles, LANES), 1)
    for n in range(count):
        row = jnp.broadcast_to(weight[n : n + 1, :], (cycles, LANES))
        column = jnp.sum(jnp.where(eye, row, 0.0), axis=1, keepdims=True)
        low = low_ref[start + n].astype(jnp.float32)
        weighted = (column * low).astype(jnp.bfloat16).astype(jnp.float32)
        for f in range(tiles):
            image[f, n * cycles : (n + 1) * cycles, :] = weighted[:, f * LANES : (f + 1) * LANES]
        for f in range(pairs):
            re = weighted[:, f * LANES : (f + 1) * LANES]
            im = weighted[:, (f + pairs) * LANES : (f + pairs + 1) * LANES]
            image_sum[f, n * cycles : (n + 1) * cycles, :] = re + im
    for copy in copies:
        copy.wait()
    for at, ref in ((0, first_ref), (part, second_ref)):
        for f in range(tiles):
            staged[f, at : at + part, :] = ref[:, f * LANES : (f + 1) * LANES].astype(jnp.float32)
    blocks = kinds // 8
    zero = jnp.zeros((8, LANES), jnp.float32)
    norms = []
    for b in range(blocks):
        square = jnp.zeros((cycles, 8, LANES), jnp.float32)
        for f in range(pairs):
            rows = pl.ds(b * 8 * cycles, 8 * cycles)
            re = jnp.swapaxes(staged[f, rows, :].reshape(8, cycles, LANES), 0, 1)
            im = jnp.swapaxes(staged[f + pairs, rows, :].reshape(8, cycles, LANES), 0, 1)
            classes[3 * f, :, b * 8 : b * 8 + 8, :] = re
            classes[3 * f + 1, :, b * 8 : b * 8 + 8, :] = re - im
            classes[3 * f + 2, :, b * 8 : b * 8 + 8, :] = re + im
            square = square + (re * re + im * im)
        norm = zero
        for r in range(cycles):
            total = jnp.sum(square[r], axis=1, keepdims=True)
            norm = jnp.where(iota((8, LANES), 1) == r, total, norm)
        norms.append(norm)
    group = 2
    for f in range(pairs):

        def particles(g, _):
            def cycle(r, sums):
                new = list(sums)
                for i in range(group):
                    row = pl.ds((g * group + i) * cycles + r, 8, stride=0)
                    a_sum, a_im, a_re = image_sum[f, row, :], image[f + pairs, row, :], image[f, row, :]
                    for b in range(blocks):
                        at = slice(b * 8, b * 8 + 8)
                        j = 3 * (i * blocks + b)
                        new[j] = new[j] + classes[3 * f, r, at, :] * a_sum
                        new[j + 1] = new[j + 1] + classes[3 * f + 1, r, at, :] * a_im
                        new[j + 2] = new[j + 2] + classes[3 * f + 2, r, at, :] * a_re
                return tuple(new)

            sums = lax.fori_loop(0, cycles, cycle, (zero,) * (3 * group * blocks), unroll=4)
            for i in range(group):
                for b in range(blocks):
                    s1, s2, s3 = sums[3 * (i * blocks + b) : 3 * (i * blocks + b) + 3]
                    at = pl.ds(pl.multiple_of((g * group + i) * kinds + b * 8, 8), 8)
                    cross[at, f * LANES : (f + 1) * LANES] = s1 - s2
                    cross[at, (f + pairs) * LANES : (f + pairs + 1) * LANES] = s1 - s3
            return 0

        lax.fori_loop(0, count // group, particles, 0)
    scores = jnp.dot(
        cross[...].astype(jnp.bfloat16), table_ref[...], preferred_element_type=jnp.float32
    )
    cross[...] = scores
    inner = iota((8, LANES), 1) < cycles
    row = jnp.zeros(outs[0].shape, jnp.float32)
    for n in range(count):
            mine = []
            for b in range(blocks):
                powers = jnp.where(inner, jnp.broadcast_to(power[n : n + 1, :], (8, LANES)), 0.0)
                energy = jnp.sum(powers * norms[b], axis=1, keepdims=True)
                at = n * kinds + b * 8
                mine.append(cross[at : at + 8, :] - 0.5 * energy)
            mine = jnp.concatenate(mine, axis=0)
            top = jnp.max(mine, axis=(0, 1), keepdims=True)
            if merge:
                per = count // (merge // 2)
                pair, i = before[n // per * 2 : n // per * 2 + 2], n % per
                top_before, total_before = pair[0][i : i + 1, :], pair[1][i : i + 1, :]
                top = jnp.maximum(top, jnp.max(top_before, axis=1, keepdims=True))
            total = jnp.sum(jnp.exp(mine - top), axis=(0, 1), keepdims=True)
            if merge:
                total = total + (total_before * jnp.exp(top_before - top))[:, :1]
                here = iota(row.shape, 1) == start + n
                row = jnp.where(here, jnp.broadcast_to(top + jnp.log(total), row.shape), row)
            else:
                outs[0][n : n + 1, :] = jnp.broadcast_to(top, (1, LANES))
                outs[1][n : n + 1, :] = jnp.broadcast_to(total, (1, LANES))
    if merge:
        outs[0][...] = row


def score(low, ctf, noise, first, second, table, before, start, count):
    _, cycles, width = low.shape
    kinds = 2 * first.shape[0]
    merge = len(before)
    each = pltpu.VMEM((count, LANES), jnp.float32)
    row = jax.ShapeDtypeStruct((1, count), jnp.float32)
    part = (kinds // 2 * cycles, width)
    return pl.pallas_call(
        functools.partial(score_kernel, merge=merge, start=start),
        out_shape=row if merge else (each, each),
        in_specs=[HERE] * 3 + [THERE if merge else HERE] + [HERE] * (2 + merge),
        out_specs=HERE if merge else (HERE, HERE),
        scratch_shapes=[
            pltpu.VMEM((width // LANES, count * cycles, LANES), jnp.float32),
            pltpu.VMEM((width // LANES // 2, count * cycles, LANES), jnp.float32),
            pltpu.VMEM((width // LANES, kinds * cycles, LANES), jnp.float32),
            pltpu.VMEM((width // LANES // 2 * 3, cycles, kinds, LANES), jnp.float32),
            pltpu.VMEM((count * kinds, width), jnp.float32),
        ]
        + ([pltpu.VMEM(part, first.dtype), pltpu.SemaphoreType.DMA((SPLITS,))] if merge else []),
        cost_estimate=cost(count / 2),
        compiler_params=room(
            ((count * cycles, width), 8),
            ((kinds * cycles, width), 12),
            ((count * kinds, width), 8),
            (table.shape, 2),
        ),
    )(
        *held_near(low), ctf, noise, *(held_far if merge else held_near)(first.reshape(part)),
        *held_near(second.reshape(part), table),
        *before,
    )


def part_of(view_ref, top, near):
    if view_ref.shape[0] == 2:
        return view_ref.at[top, near]
    return view_ref.at[:, top, near]


def column(row):
    size = row.shape[1]
    eye = iota((size, size), 0) == iota((size, size), 1)
    return jnp.sum(jnp.where(eye, jnp.broadcast_to(row, (size, size)), 0.0), axis=1, keepdims=True)


def pieces_kernel(near_ref, top_ref, view_ref, *refs, chunk):
    outs, sems = refs[-GROUP:-1], refs[-1]
    if chunk == 0:
        ctf_ref, owner_ref, sub_ref, turn_ref, meta_ref = refs[:5]
        outs = refs[5 : 5 + GROUP - 1]
        ctf_here, owner_here, sub_here, turn_here, small, sems = refs[5 + GROUP - 1 :]
        fetches = [
            pltpu.make_async_copy(there, here, small.at[i])
            for i, (there, here) in enumerate(
                ((ctf_ref, ctf_here), (owner_ref, owner_here), (sub_ref, sub_here), (turn_ref, turn_here))
            )
        ]
        for fetch in fetches:
            fetch.start()
    count = view_ref.shape[2] if view_ref.shape[0] == 2 else view_ref.shape[0]
    part = count // SPLITS
    copies = [
        pltpu.make_async_copy(
            part_of(view_ref, top_ref[0] ^ (1 - chunk), near_ref[0] ^ (i + 1)).at[
                pl.ds(j * part, part)
            ],
            out.at[pl.ds(j * part, part)],
            sems.at[i * SPLITS + j],
        )
        for i, out in enumerate(outs)
        for j in range(SPLITS)
    ]
    for copy in copies:
        copy.start()
    if chunk == 0:
        for fetch in fetches:
            fetch.wait()
        cycles = ctf_ref.shape[1]
        turn = turn_here[...]
        shape = (count, meta_ref.shape[1] - cycles)
        at = iota(shape, 1)
        rest = jnp.where(at == 0, column((turn >> 4).astype(jnp.float32)), 0.0)
        rest = jnp.where(at == 1, column((turn & 15).astype(jnp.float32)), rest)
        rest = jnp.where(at == 2, column(owner_here[...].astype(jnp.float32)), rest)
        rest = jnp.where(at == 3, column(sub_here[...].astype(jnp.float32)), rest)
        meta_ref[:, :cycles] = ctf_here[...]
        meta_ref[:, cycles:] = rest.astype(jnp.bfloat16)
        for out in outs:
            out[count, :, :] = jnp.zeros(out.shape[1:], out.dtype)
            out[count, :, : meta_ref.shape[1]] = meta_ref[...]
    for copy in copies:
        copy.wait()


def pieces(near, top, view, chunk, others):
    count, width = view.shape[2] if view.shape[0] == 2 else view.shape[0], view.shape[-1]
    out = pltpu.VMEM((count + (chunk == 0), PAD, width), view.dtype)
    shapes = [out] * (GROUP - 1)
    scratch = [pltpu.SemaphoreType.DMA(((GROUP - 1) * SPLITS,))]
    if chunk == 0:
        ctf = others[0]
        shapes = [pltpu.VMEM((count, 2 * ctf.shape[1]), view.dtype)] + shapes
        scratch = [
            pltpu.VMEM(ctf.shape, ctf.dtype),
            pltpu.VMEM((1, count), jnp.int32),
            pltpu.VMEM((1, count), jnp.int32),
            pltpu.VMEM((1, count), jnp.int32),
            pltpu.SemaphoreType.DMA((4,)),
        ] + scratch
    return pl.pallas_call(
        functools.partial(pieces_kernel, chunk=chunk),
        out_shape=shapes,
        in_specs=[SCALARS] * 2 + [THERE] * (1 + len(others)),
        out_specs=[HERE] * len(shapes),
        scratch_shapes=scratch,
        cost_estimate=cost(1.5),
        compiler_params=room(((count * PAD, width), 2 * GROUP)),
    )(near, top, *held_far(view, *others))


def sums_kernel(
    near_ref, top_ref, cls_ref, *refs, slice_cycles, far, chunk, shards,
):
    if chunk == 0:
        meta_ref, refs = refs[0], refs[1:]
    noise_ref, view_ref, refs = refs[0], refs[1], refs[2:]
    given, refs = refs[: GROUP - 1], refs[GROUP - 1 :]
    if chunk == 0:
        keep_ref, give_ref = refs[:2]
        shared, refs = refs[2:6], refs[6:]
        total, own, powers, plan, metas, cos_ref, sin_ref, place_ref, sems = refs
    else:
        plan, metas, cos_ref, sin_ref = refs[:4]
        keep_ref, give_ref, total, own, place_ref, sems = refs[4:]
    cycles, half = PAD, cos_ref.shape[1]
    side = top_ref[0] ^ (1 - chunk)
    particles = cos_ref.shape[0]
    count = particles // GROUP
    width = 2 * half
    size = keep_ref.shape[0] // (shards // 2)
    part = count // SPLITS
    fetches = [
        pltpu.make_async_copy(
            part_of(view_ref, side, near_ref[0]).at[pl.ds(i * part, part)],
            own.at[pl.ds(i * part, part)],
            sems.at[5 + i],
        )
        for i in range(SPLITS)
    ]
    for fetch in fetches:
        fetch.start()
    schedule = pltpu.make_async_copy(plan, place_ref, sems.at[0])
    if chunk == 0:
        metas[:count] = meta_ref[...]
        for g, piece in enumerate(given):
            metas[(g + 1) * count : (g + 2) * count] = piece[count, :, : metas.shape[1]]
        ints = metas[:, LANES : LANES + LANES].astype(jnp.float32).astype(jnp.int32)
        turn = ints[:, 0:1] * 16 + ints[:, 1:2]
        shard, inside = ints[:, 2:3], ints[:, 3:4]
        block = ((shard ^ cls_ref[0]) & 1) * (shards // 2) + (shard >> 1)
        here = iota((particles, LANES), 0) == iota((particles, LANES), 1)

        def in_row(values):
            return jnp.sum(jnp.where(here, values.astype(jnp.float32), 0.0), axis=0, keepdims=True)

        rows = (
            in_row(block * size + inside * cycles),
            in_row(block * PAD + inside),
            in_row(block * (size - PAD) + inside * cycles),
        )
        at = iota(plan.shape, 0)
        places = jnp.where(at == 0, rows[0], jnp.where(at == 1, rows[1], rows[2]))
        plan[...] = places.astype(jnp.int32)
        schedule.start()
        total[...] = jnp.zeros_like(total)
        powers[...] = jnp.zeros_like(powers)
        turns = iota((particles, half), 1) * turn & (width - 1)
        angle = turns.astype(jnp.float32) * (2.0 * math.pi / width)
        cos_ref[...] = jnp.cos(angle)
        sin_ref[...] = jnp.sin(angle)
        saves = [
            pltpu.make_async_copy(here, there, sems.at[1 + i])
            for i, (here, there) in enumerate(zip((plan, metas, cos_ref, sin_ref), shared))
        ]
        for save in saves:
            save.start()
    else:
        schedule.start()
        total[...] = jnp.zeros_like(total)
    r = iota((cycles, LANES), 0)
    domain = (side * (far // 2) + r // slice_cycles) * GROUP + near_ref[0]
    pick = iota((cycles, LANES), 1) == domain * slice_cycles + r % slice_cycles
    batch = 2
    schedule.wait()
    place_at = 0 if chunk == 0 else 2

    def one(n, source):
        ctf = metas[n : n + 1, :LANES].astype(jnp.float32)
        weight_row = ctf / noise_ref[...]
        weight = jnp.sum(
            jnp.where(pick, jnp.broadcast_to(weight_row, pick.shape), 0.0), axis=1, keepdims=True
        )
        x = source[n % count].astype(jnp.float32)
        x_re, x_im = x[:, :half], x[:, half:]
        cosv, sinv = cos_ref[n : n + 1, :], sin_ref[n : n + 1, :]
        re = weight * (x_re * cosv - x_im * sinv)
        im = weight * (x_re * sinv + x_im * cosv)
        return re, im, ctf * weight_row

    for g in (*range(1, GROUP), 0):
        source = given[g - 1] if g else own
        if g == 0:
            for fetch in fetches:
                fetch.wait()
        for start in range(g * count, (g + 1) * count, batch):
            done = [one(n, source) for n in range(start, start + batch)]
            for n, (re, im, power) in zip(range(start, start + batch), done):
                at = pl.ds(pl.multiple_of(place_ref[place_at, n], PAD), cycles)
                total[at, :half] += re
                total[at, half:] += im
                if chunk == 0:
                    powers[pl.ds(place_ref[1, n], 1), :] += power
    if chunk == 0:
        blocks = powers.shape[0] // PAD
        for b in range(blocks):
            at = slice((b + 1) * size - PAD, (b + 1) * size)
            total[at, :LANES] = powers[b * PAD : (b + 1) * PAD]
    rows = keep_ref.shape[0]
    keep_ref[...] = total[:rows]
    give_ref[...] = total[rows:]
    if chunk == 0:
        for save in saves:
            save.wait()


def class_sums(scalars, view, chunk, given, meta, noise, shared, slice_cycles, far, rows, shards):
    width = view.shape[-1]
    count = view.shape[2] if view.shape[0] == 2 else view.shape[0]
    first = chunk == 0
    particles = count * GROUP
    out = pltpu.VMEM((rows, width), jnp.float32)
    kinds = [
        ((8, LANES), jnp.int32),
        ((particles, 2 * LANES), given[0].dtype),
        ((particles, width // 2), jnp.float32),
        ((particles, width // 2), jnp.float32),
    ]
    shapes = [out, out] + ([pltpu.HBM(shape, dtype) for shape, dtype in kinds] if first else [])
    scratch = [
        pltpu.VMEM((2 * rows, width), jnp.float32),
        pltpu.VMEM((count, PAD, width), view.dtype),
    ]
    if first:
        scratch += [pltpu.VMEM((shards * PAD, LANES), jnp.float32)]
        scratch += [pltpu.VMEM(shape, dtype) for shape, dtype in kinds]
    ins = [meta] if first else []
    return pl.pallas_call(
        functools.partial(
            sums_kernel, slice_cycles=slice_cycles, far=far, chunk=chunk, shards=shards
        ),
        out_shape=shapes,
        in_specs=[SCALARS] * 3 + [HERE] * (len(ins) + 1) + [THERE]
        + [HERE] * (GROUP - 1 + len(shared)),
        out_specs=[HERE, HERE] + [THERE] * (len(shapes) - 2),
        scratch_shapes=scratch
        + [pltpu.SMEM((8, LANES), jnp.int32), pltpu.SemaphoreType.DMA((5 + SPLITS,))],
        cost_estimate=cost(2.5),
        compiler_params=room(((2 * rows, width), 8), ((particles * PAD, width), 4)),
    )(*scalars, *held_near(*ins), noise, *held_far(view), *held_near(*given, *shared))


def spans(rows):
    return [(at, min(LANES, rows - at)) for at in range(0, rows, LANES)]


def encode(value, out, rows):
    codes = jnp.zeros((PAD, LANES), jnp.float32)
    blocks = spans(rows)
    for i, (start, size) in enumerate(blocks):
        x = value[start : start + size]
        scaled, code = coded(x)
        out[start : start + size, :] = scaled
        eye = iota((size, LANES), 0) == iota((size, LANES), 1)
        row = jnp.sum(jnp.where(eye, code, 0.0), axis=0, keepdims=True)
        codes = jnp.where(iota((PAD, LANES), 0) == i, row, codes)
    out[rows:, :] = jnp.zeros((PAD, out.shape[1]), jnp.int16)
    if value.shape[0] > rows:
        scaled, code = coded(value[rows:, :LANES])
        out[rows:, :LANES] = scaled
        eye = iota((PAD, LANES), 0) == iota((PAD, LANES), 1)
        row = jnp.sum(jnp.where(eye, code, 0.0), axis=0, keepdims=True)
        codes = jnp.where(iota((PAD, LANES), 0) == len(blocks), row, codes)
    out[rows:, LANES : 2 * LANES] = codes.astype(jnp.int32).astype(jnp.int16)


def coded(x):
    top = jnp.maximum(jnp.max(jnp.abs(x), axis=1, keepdims=True), 1e-30)
    code = jnp.floor(jnp.log(top) / UNIT) + 1.0
    scaled = jnp.round(x * (jnp.exp(-code * UNIT) * 32767.0))
    return jnp.clip(scaled, -32767.0, 32767.0).astype(jnp.int32).astype(jnp.int16), code


def decode(ref):
    rows = ref.shape[0] - PAD
    codes = ref[rows:, LANES : 2 * LANES].astype(jnp.int32).astype(jnp.float32)
    parts = []
    for i, (start, size) in enumerate(spans(rows)):
        parts.append(ref[start : start + size, :].astype(jnp.int32).astype(jnp.float32) * scale(codes, i, size))
    return jnp.concatenate(parts, axis=0)


def decode_power(ref):
    rows = ref.shape[0] - PAD
    codes = ref[rows:, LANES : 2 * LANES].astype(jnp.int32).astype(jnp.float32)
    x = ref[rows:, :LANES].astype(jnp.int32).astype(jnp.float32)
    return x * scale(codes, len(spans(rows)), PAD)


def scale(codes, i, size):
    eye = iota((size, LANES), 0) == iota((size, LANES), 1)
    row = jnp.broadcast_to(codes[i : i + 1], (size, LANES))
    code = jnp.sum(jnp.where(eye, row, 0.0), axis=1, keepdims=True)
    return jnp.exp(code * UNIT) * (1.0 / 32767.0)


def shard_kernel(bit_ref, keep_ref, get_ref, own_ref, code_ref, *, was_coded):
    parts, rows, _ = own_ref.shape
    full = code_ref.shape[1] - PAD
    if was_coded:
        for p in range(2 * parts):
            keep_ref[p, :full] = keep_ref[p, :full] + decode(get_ref.at[p])
            if rows > full:
                keep_ref[p, full:, :LANES] = keep_ref[p, full:, :LANES] + decode_power(get_ref.at[p])
    bit = bit_ref[0]
    for p in range(parts):
        mine, other = bit * parts + p, (1 - bit) * parts + p
        if was_coded:
            encode(keep_ref[other], code_ref.at[p], full)
            own_ref[p] = keep_ref[mine]
        else:
            encode(keep_ref[other] + get_ref[other], code_ref.at[p], full)
            own_ref[p] = keep_ref[mine] + get_ref[mine]


def split_shards(bit, keep, get, full):
    parts, rows, width = keep.shape
    parts = parts // 2
    own = pltpu.VMEM((parts, rows, width), jnp.float32)
    code = pltpu.VMEM((parts, full + PAD, width), jnp.int16)
    return pl.pallas_call(
        functools.partial(shard_kernel, was_coded=get.dtype == jnp.int16),
        out_shape=(own, code),
        in_specs=[SCALARS, HERE, HERE],
        out_specs=(HERE, HERE),
        cost_estimate=cost(1.5),
        compiler_params=room((keep.shape, 16)),
    )(bit, *held_near(keep, get))


def ahead_kernel(keep_ref, get_ref, power_ref, code_ref, total):
    full = keep_ref.shape[0] - PAD
    total[:full] = keep_ref[:full] + decode(get_ref)
    total[full:, :] = jnp.zeros((PAD, total.shape[1]), jnp.float32)
    total[full:, :LANES] = keep_ref[full:, :LANES] + decode_power(get_ref)
    power_ref[...] = total[full:, :LANES]
    encode(total, code_ref, full)


def ahead(keep, get):
    rows, width = keep.shape
    return pl.pallas_call(
        ahead_kernel,
        out_shape=(
            pltpu.VMEM((PAD, LANES), jnp.float32),
            pltpu.VMEM((rows, width), jnp.int16),
        ),
        in_specs=[HERE, HERE],
        out_specs=(HERE, HERE),
        scratch_shapes=[pltpu.VMEM((rows, width), jnp.float32)],
        cost_estimate=cost(1),
        compiler_params=room((keep.shape, 20)),
        name="ahead",
    )(*held_near(keep, get))


def final_kernel(dom_ref, keep_ref, get_ref, power_ref, came_ref, out):
    classes, cycles, _ = out.shape
    sums = keep_ref[...] + decode(get_ref) + decode(came_ref)
    powers = power_ref[...] + decode_power(came_ref)
    r = iota((cycles, LANES), 0)
    pick = iota((cycles, LANES), 1) == dom_ref[0] * cycles + r
    for k in range(classes):
        row = jnp.broadcast_to(powers[k : k + 1], pick.shape)
        denom = jnp.sum(jnp.where(pick, row, 0.0), axis=1, keepdims=True) + 1.0
        out[k] = sums[k * cycles : (k + 1) * cycles, :] / denom


def finish(dom, keep, get, power, came, classes, cycles, width):
    out = (classes, cycles, width)
    return pl.pallas_call(
        final_kernel,
        out_shape=jax.ShapeDtypeStruct(out, jnp.float32),
        in_specs=[SCALARS] + [HERE] * 4,
        out_specs=HERE,
        cost_estimate=cost(1),
        compiler_params=room((out, 16)),
        name="finish",
    )(dom, *held_near(keep, get, power, came))


def decoded(get):
    rows = get.shape[0] - PAD
    codes = get[rows:, LANES : 2 * LANES].astype(jnp.float32)
    values = get.astype(jnp.float32)
    scales = jnp.exp(codes * UNIT) * (1.0 / 32767.0)
    blocks = len(spans(rows))
    full = values[:rows] * scales[:blocks].reshape(-1)[:rows, None]
    return full, values[rows:, :LANES] * scales[blocks, :PAD, None]


def per_device(spectra, ctf, noise_power, references, owner, sub_class, rotation):
    count, cycles, width = spectra.shape
    k_local = references.shape[0]
    domains, shards = lax.axis_size("dom"), lax.axis_size("cls")
    dom, cls = lax.axis_index("dom"), lax.axis_index("cls")
    far = domains // GROUP
    slice_cycles = cycles // domains
    near = (dom & (GROUP - 1)).reshape(1)
    top = (dom // (domains // 2)).reshape(1)
    noise = noise_power.reshape(1, cycles)

    if slice_cycles == PAD:
        view = spectra.reshape(count, 2, GROUP, PAD, width)
    else:
        view = spectra.reshape(count, 2, far // 2, GROUP, slice_cycles, width)
        view = view.transpose(1, 3, 0, 2, 4, 5).reshape(2, GROUP, count, PAD, width)
    rows_of = [v.reshape(1, count) for v in (owner, sub_class, rotation)]
    meta, *sent_0 = pieces(near, top, view, 0, (ctf, *rows_of))
    sent = (sent_0, pieces(near, top, view, 1, ()))
    got = [[swap(sent[c][m - 1], "dom", m) for m in range(1, GROUP)] for c in range(CHUNKS)]

    held, mask = references, 2
    own_side, other_side = references, None
    while mask < shards:
        new = swap(held, "cls", mask)
        other_side = new if other_side is None else jnp.concatenate([other_side, new], axis=0)
        held = jnp.concatenate([held, new], axis=0) if 2 * mask < shards else held
        mask *= 2
    table, low = rotation_table(spectra, references.shape[1])
    near_refs = swap(own_side, "cls", 1)
    per = count // NEAR_CALLS
    before = []
    for i in range(NEAR_CALLS):
        before += score(low, ctf, noise, own_side, near_refs, table, (), i * per, per)
    far_refs = swap(other_side, "cls", 1)
    row = score(low, ctf, noise, other_side, far_refs, table, before, 0, count)
    log_evidence = row.reshape(count)

    scalars = (near, top, cls.reshape(1))
    ends, shared = [], []
    for chunk in range(CHUNKS):
        size = k_local * PAD + (PAD if chunk == 0 else 0)
        keep, give, *more = class_sums(
            scalars, view, chunk, got[chunk], meta, noise, shared, slice_cycles, far,
            shards // 2 * size, shards,
        )
        shared = more
        get = swap(give, "cls", 1)
        shape = (shards // 2, size, width)
        keep, get = keep.reshape(shape), get.reshape(shape)
        mask = shards // 2
        while mask >= 2:
            bit = ((cls // mask) & 1).reshape(1)
            keep, code = split_shards(bit, keep, get, k_local * PAD)
            get = swap(code, "cls", mask)
            mask //= 2
        ends.append((keep[0], get[0]))
    power, code = ahead(*ends[0])
    came = swap(code, "dom", domains // 2)
    if far == 2:
        new_refs = finish(dom.reshape(1), *ends[1], power, came, k_local, slice_cycles, width)
        return (new_refs, log_evidence)

    came, came_power = decoded(came)
    keep, get = ends[1]
    numer = (keep + decoded(get)[0] + came).reshape(k_local, PAD, width)
    power = power + came_power
    left, mask = PAD, domains // 4
    while mask >= GROUP:
        bit = (dom // mask) & 1
        left = left // 2
        own = lax.dynamic_slice_in_dim(numer, bit * left, left, 1)
        other = lax.dynamic_slice_in_dim(numer, (1 - bit) * left, left, 1)
        numer = own + swap(other, "dom", mask)
        power = power + swap(power, "dom", mask)
        mask //= 2
    denom = lax.dynamic_slice_in_dim(power[:k_local], dom * left, left, 1)
    return (numer / (denom + 1.0)[:, :, None], log_evidence)


def solution(mesh):
    return jax.shard_map(
        per_device,
        mesh=mesh,
        in_specs=(
            P(("dom", "cls"), None, None),
            P(("dom", "cls"), None),
            P(),
            P("cls", None, None),
            P(("dom", "cls"), None),
            P(("dom", "cls")),
            P(("dom", "cls")),
        ),
        out_specs=(P("cls", "dom", None), P(("dom", "cls"))),
        check_vma=False,
    )
```

```python
import functools
import math

import jax
import jax.numpy as jnp
from jax import lax
from jax.experimental import pallas as pl
from jax.experimental.pallas import tpu as pltpu
from jax.sharding import PartitionSpec as P


CHUNKS = 2
GROUP = 4
NEAR_CALLS = 2
SPLITS = 4
LANES = 128
PAD = 16
STEPS = 64.0
UNIT = math.log(2.0) / STEPS


def table_kernel(image_ref, out_ref, low_ref, sems):
    width, turns_all = out_ref.shape
    count, cycles, _ = low_ref.shape
    part = count // SPLITS
    copies = [
        pltpu.make_async_copy(
            image_ref.at[pl.ds(i * part, part), :cycles, :], low_ref.at[pl.ds(i * part, part)], sems.at[i]
        )
        for i in range(SPLITS)
    ]
    for copy in copies:
        copy.start()
    half = width // 2
    quarter = half // 2
    step = 32
    for at in range(0, quarter, step):
        shape = (step, turns_all)
        turns = (iota(shape, 0) + at) * iota(shape, 1) & (turns_all - 1)
        angle = turns.astype(jnp.float32) * (2.0 * math.pi / turns_all)
        cosv, sinv = jnp.cos(angle), jnp.sin(angle)
        odd, back = (iota(shape, 1) & 1) == 1, (iota(shape, 1) & 2) == 2
        cos_on, sin_on = jnp.where(odd, -sinv, cosv), jnp.where(odd, cosv, sinv)
        cos_on, sin_on = jnp.where(back, -cos_on, cos_on), jnp.where(back, -sin_on, sin_on)
        out_ref[at : at + step, :] = cosv.astype(jnp.bfloat16)
        out_ref[quarter + at : quarter + at + step, :] = cos_on.astype(jnp.bfloat16)
        out_ref[half + at : half + at + step, :] = (-sinv).astype(jnp.bfloat16)
        at = half + quarter + at
        out_ref[at : at + step, :] = (-sin_on).astype(jnp.bfloat16)
    for copy in copies:
        copy.wait()


def rotation_table(spectra, cycles):
    count, _, width = spectra.shape
    return pl.pallas_call(
        table_kernel,
        out_shape=(
            pltpu.VMEM((width, width), jnp.bfloat16),
            pltpu.VMEM((count, cycles, width), spectra.dtype),
        ),
        in_specs=[THERE],
        out_specs=(HERE, HERE),
        scratch_shapes=[pltpu.SemaphoreType.DMA((SPLITS,))],
        cost_estimate=cost(2),
        compiler_params=room(((width, width), 4)),
        name="table",
    )(*held_far(spectra))


def held_near(*values):
    return [pltpu.with_memory_space_constraint(v, pltpu.VMEM) for v in values]


def held_far(*values):
    return [pltpu.with_memory_space_constraint(v, pltpu.HBM) for v in values]


def swap(value, axis, mask):
    size = lax.axis_size(axis)
    return lax.ppermute(value, axis, [(i, i ^ mask) for i in range(size)])


def iota(shape, axis):
    return lax.broadcasted_iota(jnp.int32, shape, axis)


HERE = pl.BlockSpec(memory_space=pltpu.VMEM)
SCALARS = pl.BlockSpec(memory_space=pltpu.SMEM)
THERE = pl.BlockSpec(memory_space=pltpu.HBM)


def room(*arrays):
    size = sum(math.prod(shape) * bits for shape, bits in arrays)
    return pltpu.CompilerParams(vmem_limit_bytes=size + (8 << 20))


def cost(us):
    return pl.CostEstimate(flops=0, transcendentals=0, bytes_accessed=int(us * 3.6e6))


def score_kernel(
    low_ref, ctf_ref, noise_ref, first_ref, second_ref, table_ref, *refs, merge, start
):
    before, refs = refs[:merge], refs[merge:]
    outs, refs = refs[: 1 if merge else 2], refs[1 if merge else 2 :]
    image, image_sum, staged, classes, cross = refs[:5]
    copies = []
    if merge:
        there, first_ref, sems = first_ref, refs[5], refs[6]
        part = there.shape[0] // SPLITS
        copies = [
            pltpu.make_async_copy(
                there.at[pl.ds(i * part, part)], first_ref.at[pl.ds(i * part, part)], sems.at[i]
            )
            for i in range(SPLITS)
        ]
    for copy in copies:
        copy.start()
    _, cycles, width = low_ref.shape
    tiles = width // LANES
    pairs = tiles // 2
    count = image.shape[1] // cycles
    kinds = cross.shape[0] // count
    part = first_ref.shape[0]
    ctf = ctf_ref[start : start + count, :].astype(jnp.float32)
    weight = ctf / noise_ref[...]
    power = ctf * weight
    eye = iota((cycles, LANES), 0) == iota((cycles, LANES), 1)
    for n in range(count):
        row = jnp.broadcast_to(weight[n : n + 1, :], (cycles, LANES))
        column = jnp.sum(jnp.where(eye, row, 0.0), axis=1, keepdims=True)
        low = low_ref[start + n].astype(jnp.float32)
        weighted = (column * low).astype(jnp.bfloat16).astype(jnp.float32)
        for f in range(tiles):
            image[f, n * cycles : (n + 1) * cycles, :] = weighted[:, f * LANES : (f + 1) * LANES]
        for f in range(pairs):
            re = weighted[:, f * LANES : (f + 1) * LANES]
            im = weighted[:, (f + pairs) * LANES : (f + pairs + 1) * LANES]
            image_sum[f, n * cycles : (n + 1) * cycles, :] = re + im
    for copy in copies:
        copy.wait()
    for at, ref in ((0, first_ref), (part, second_ref)):
        for f in range(tiles):
            staged[f, at : at + part, :] = ref[:, f * LANES : (f + 1) * LANES].astype(jnp.float32)
    blocks = kinds // 8
    zero = jnp.zeros((8, LANES), jnp.float32)
    norms = []
    for b in range(blocks):
        square = jnp.zeros((cycles, 8, LANES), jnp.float32)
        for f in range(pairs):
            rows = pl.ds(b * 8 * cycles, 8 * cycles)
            re = jnp.swapaxes(staged[f, rows, :].reshape(8, cycles, LANES), 0, 1)
            im = jnp.swapaxes(staged[f + pairs, rows, :].reshape(8, cycles, LANES), 0, 1)
            classes[3 * f, :, b * 8 : b * 8 + 8, :] = re
            classes[3 * f + 1, :, b * 8 : b * 8 + 8, :] = re - im
            classes[3 * f + 2, :, b * 8 : b * 8 + 8, :] = re + im
            square = square + (re * re + im * im)
        norm = zero
        for r in range(cycles):
            total = jnp.sum(square[r], axis=1, keepdims=True)
            norm = jnp.where(iota((8, LANES), 1) == r, total, norm)
        norms.append(norm)
    group = 2
    for f in range(pairs):

        def particles(g, _):
            def cycle(r, sums):
                new = list(sums)
                for i in range(group):
                    row = pl.ds((g * group + i) * cycles + r, 8, stride=0)
                    a_sum, a_im, a_re = image_sum[f, row, :], image[f + pairs, row, :], image[f, row, :]
                    for b in range(blocks):
                        at = slice(b * 8, b * 8 + 8)
                        j = 3 * (i * blocks + b)
                        new[j] = new[j] + classes[3 * f, r, at, :] * a_sum
                        new[j + 1] = new[j + 1] + classes[3 * f + 1, r, at, :] * a_im
                        new[j + 2] = new[j + 2] + classes[3 * f + 2, r, at, :] * a_re
                return tuple(new)

            sums = lax.fori_loop(0, cycles, cycle, (zero,) * (3 * group * blocks), unroll=16)
            for i in range(group):
                for b in range(blocks):
                    s1, s2, s3 = sums[3 * (i * blocks + b) : 3 * (i * blocks + b) + 3]
                    at = pl.ds(pl.multiple_of((g * group + i) * kinds + b * 8, 8), 8)
                    cross[at, f * LANES : (f + 1) * LANES] = s1 - s2
                    cross[at, (f + pairs) * LANES : (f + pairs + 1) * LANES] = s1 - s3
            return 0

        lax.fori_loop(0, count // group, particles, 0)
    scores = jnp.dot(
        cross[...].astype(jnp.bfloat16), table_ref[...], preferred_element_type=jnp.float32
    )
    cross[...] = scores
    inner = iota((8, LANES), 1) < cycles
    tops, totals = [], []
    for n in range(count):
        powers = jnp.where(inner, jnp.broadcast_to(power[n : n + 1, :], (8, LANES)), 0.0)
        most = None
        for b in range(blocks):
            energy = jnp.sum(powers * norms[b], axis=1, keepdims=True)
            at = n * kinds + b * 8
            mine = cross[at : at + 8, :] - 0.5 * energy
            cross[at : at + 8, :] = mine
            most = mine if most is None else jnp.maximum(most, mine)
        tops.append(jnp.max(most, axis=(0, 1), keepdims=True))
    if merge:
        per = count // (merge // 2)
        old = [
            [before[n // per * 2 + i][n % per : n % per + 1, :1] for n in range(count)] for i in range(2)
        ]
        tops = [jnp.maximum(top, was) for top, was in zip(tops, old[0])]
    for n in range(count):
        mine = jnp.exp(cross[n * kinds : (n + 1) * kinds, :] - tops[n])
        part_sum = mine[:8]
        for b in range(1, blocks):
            part_sum = part_sum + mine[b * 8 : b * 8 + 8]
        totals.append(jnp.sum(part_sum, axis=(0, 1), keepdims=True))
    if not merge:
        for n in range(count):
            outs[0][n : n + 1, :] = jnp.broadcast_to(tops[n], (1, LANES))
            outs[1][n : n + 1, :] = jnp.broadcast_to(totals[n], (1, LANES))
        return
    row_top = jnp.zeros(outs[0].shape, jnp.float32)
    row_was, row_total, row_old = row_top, row_top, row_top
    for n in range(count):
        here = iota(row_top.shape, 1) == n
        row_top = jnp.where(here, tops[n], row_top)
        row_total = jnp.where(here, totals[n], row_total)
        row_was = jnp.where(here, old[0][n], row_was)
        row_old = jnp.where(here, old[1][n], row_old)
    outs[0][...] = row_top + jnp.log(row_total + row_old * jnp.exp(row_was - row_top))


def score(low, ctf, noise, first, second, table, before, start, count):
    _, cycles, width = low.shape
    kinds = 2 * first.shape[0]
    merge = len(before)
    each = pltpu.VMEM((count, LANES), jnp.float32)
    row = jax.ShapeDtypeStruct((1, count), jnp.float32)
    part = (kinds // 2 * cycles, width)
    return pl.pallas_call(
        functools.partial(score_kernel, merge=merge, start=start),
        out_shape=row if merge else (each, each),
        in_specs=[HERE] * 3 + [THERE if merge else HERE] + [HERE] * (2 + merge),
        out_specs=HERE if merge else (HERE, HERE),
        scratch_shapes=[
            pltpu.VMEM((width // LANES, count * cycles, LANES), jnp.float32),
            pltpu.VMEM((width // LANES // 2, count * cycles, LANES), jnp.float32),
            pltpu.VMEM((width // LANES, kinds * cycles, LANES), jnp.float32),
            pltpu.VMEM((width // LANES // 2 * 3, cycles, kinds, LANES), jnp.float32),
            pltpu.VMEM((count * kinds, width), jnp.float32),
        ]
        + ([pltpu.VMEM(part, first.dtype), pltpu.SemaphoreType.DMA((SPLITS,))] if merge else []),
        cost_estimate=cost(count / 2),
        compiler_params=room(
            ((count * cycles, width), 8),
            ((kinds * cycles, width), 12),
            ((count * kinds, width), 8),
            (table.shape, 2),
        ),
    )(
        *held_near(low), ctf, noise, *(held_far if merge else held_near)(first.reshape(part)),
        *held_near(second.reshape(part), table),
        *before,
    )


def part_of(view_ref, top, near):
    if view_ref.shape[0] == 2:
        return view_ref.at[top, near]
    return view_ref.at[:, top, near]


def column(row):
    size = row.shape[1]
    eye = iota((size, size), 0) == iota((size, size), 1)
    return jnp.sum(jnp.where(eye, jnp.broadcast_to(row, (size, size)), 0.0), axis=1, keepdims=True)


def pieces_kernel(near_ref, top_ref, view_ref, *refs, chunk):
    outs, sems = refs[-GROUP:-1], refs[-1]
    if chunk == 0:
        ctf_ref, owner_ref, sub_ref, turn_ref, meta_ref = refs[:5]
        outs = refs[5 : 5 + GROUP - 1]
        ctf_here, owner_here, sub_here, turn_here, small, sems = refs[5 + GROUP - 1 :]
        fetches = [
            pltpu.make_async_copy(there, here, small.at[i])
            for i, (there, here) in enumerate(
                ((ctf_ref, ctf_here), (owner_ref, owner_here), (sub_ref, sub_here), (turn_ref, turn_here))
            )
        ]
        for fetch in fetches:
            fetch.start()
    count = view_ref.shape[2] if view_ref.shape[0] == 2 else view_ref.shape[0]
    part = count // SPLITS
    copies = [
        pltpu.make_async_copy(
            part_of(view_ref, top_ref[0] ^ (1 - chunk), near_ref[0] ^ (i + 1)).at[
                pl.ds(j * part, part)
            ],
            out.at[pl.ds(j * part, part)],
            sems.at[i * SPLITS + j],
        )
        for i, out in enumerate(outs)
        for j in range(SPLITS)
    ]
    for copy in copies:
        copy.start()
    if chunk == 0:
        for fetch in fetches:
            fetch.wait()
        cycles = ctf_ref.shape[1]
        turn = turn_here[...]
        shape = (count, meta_ref.shape[1] - cycles)
        at = iota(shape, 1)
        rest = jnp.where(at == 0, column((turn >> 4).astype(jnp.float32)), 0.0)
        rest = jnp.where(at == 1, column((turn & 15).astype(jnp.float32)), rest)
        rest = jnp.where(at == 2, column(owner_here[...].astype(jnp.float32)), rest)
        rest = jnp.where(at == 3, column(sub_here[...].astype(jnp.float32)), rest)
        meta_ref[:, :cycles] = ctf_here[...]
        meta_ref[:, cycles:] = rest.astype(jnp.bfloat16)
        for out in outs:
            out[count, :, :] = jnp.zeros(out.shape[1:], out.dtype)
            out[count, :, : meta_ref.shape[1]] = meta_ref[...]
    for copy in copies:
        copy.wait()


def pieces(near, top, view, chunk, others):
    count, width = view.shape[2] if view.shape[0] == 2 else view.shape[0], view.shape[-1]
    out = pltpu.VMEM((count + (chunk == 0), PAD, width), view.dtype)
    shapes = [out] * (GROUP - 1)
    scratch = [pltpu.SemaphoreType.DMA(((GROUP - 1) * SPLITS,))]
    if chunk == 0:
        ctf = others[0]
        shapes = [pltpu.VMEM((count, 2 * ctf.shape[1]), view.dtype)] + shapes
        scratch = [
            pltpu.VMEM(ctf.shape, ctf.dtype),
            pltpu.VMEM((1, count), jnp.int32),
            pltpu.VMEM((1, count), jnp.int32),
            pltpu.VMEM((1, count), jnp.int32),
            pltpu.SemaphoreType.DMA((4,)),
        ] + scratch
    return pl.pallas_call(
        functools.partial(pieces_kernel, chunk=chunk),
        out_shape=shapes,
        in_specs=[SCALARS] * 2 + [THERE] * (1 + len(others)),
        out_specs=[HERE] * len(shapes),
        scratch_shapes=scratch,
        cost_estimate=cost(1.5),
        compiler_params=room(((count * PAD, width), 2 * GROUP)),
    )(near, top, *held_far(view, *others))


def sums_kernel(
    near_ref, top_ref, cls_ref, *refs, slice_cycles, far, chunk, shards,
):
    if chunk == 0:
        meta_ref, refs = refs[0], refs[1:]
    noise_ref, view_ref, refs = refs[0], refs[1], refs[2:]
    given, refs = refs[: GROUP - 1], refs[GROUP - 1 :]
    if chunk == 0:
        keep_ref, give_ref = refs[:2]
        shared, refs = refs[2:6], refs[6:]
        total, own, powers, plan, metas, cos_ref, sin_ref, place_ref, sems = refs
    else:
        plan, metas, cos_ref, sin_ref = refs[:4]
        keep_ref, give_ref, total, own, place_ref, sems = refs[4:]
    cycles, half = PAD, cos_ref.shape[1]
    side = top_ref[0] ^ (1 - chunk)
    particles = cos_ref.shape[0]
    count = particles // GROUP
    width = 2 * half
    size = keep_ref.shape[0] // (shards // 2)
    part = count // SPLITS
    fetches = [
        pltpu.make_async_copy(
            part_of(view_ref, side, near_ref[0]).at[pl.ds(i * part, part)],
            own.at[pl.ds(i * part, part)],
            sems.at[5 + i],
        )
        for i in range(SPLITS)
    ]
    for fetch in fetches:
        fetch.start()
    schedule = pltpu.make_async_copy(plan, place_ref, sems.at[0])
    if chunk == 0:
        metas[:count] = meta_ref[...]
        for g, piece in enumerate(given):
            metas[(g + 1) * count : (g + 2) * count] = piece[count, :, : metas.shape[1]]
        ints = metas[:, LANES : LANES + LANES].astype(jnp.float32).astype(jnp.int32)
        turn = ints[:, 0:1] * 16 + ints[:, 1:2]
        shard, inside = ints[:, 2:3], ints[:, 3:4]
        block = ((shard ^ cls_ref[0]) & 1) * (shards // 2) + (shard >> 1)
        here = iota((particles, LANES), 0) == iota((particles, LANES), 1)

        def in_row(values):
            return jnp.sum(jnp.where(here, values.astype(jnp.float32), 0.0), axis=0, keepdims=True)

        rows = (
            in_row(block * size + inside * cycles),
            in_row(block * PAD + inside),
            in_row(block * (size - PAD) + inside * cycles),
        )
        at = iota(plan.shape, 0)
        places = jnp.where(at == 0, rows[0], jnp.where(at == 1, rows[1], rows[2]))
        plan[...] = places.astype(jnp.int32)
        schedule.start()
        total[...] = jnp.zeros_like(total)
        powers[...] = jnp.zeros_like(powers)
        turns = iota((particles, half), 1) * turn & (width - 1)
        angle = turns.astype(jnp.float32) * (2.0 * math.pi / width)
        cos_ref[...] = jnp.cos(angle)
        sin_ref[...] = jnp.sin(angle)
        saves = [
            pltpu.make_async_copy(here, there, sems.at[1 + i])
            for i, (here, there) in enumerate(zip((plan, metas, cos_ref, sin_ref), shared))
        ]
        for save in saves:
            save.start()
    else:
        schedule.start()
        total[...] = jnp.zeros_like(total)
    r = iota((cycles, LANES), 0)
    domain = (side * (far // 2) + r // slice_cycles) * GROUP + near_ref[0]
    pick = iota((cycles, LANES), 1) == domain * slice_cycles + r % slice_cycles
    batch = 2
    schedule.wait()
    place_at = 0 if chunk == 0 else 2

    def one(n, source):
        ctf = metas[n : n + 1, :LANES].astype(jnp.float32)
        weight_row = ctf / noise_ref[...]
        weight = jnp.sum(
            jnp.where(pick, jnp.broadcast_to(weight_row, pick.shape), 0.0), axis=1, keepdims=True
        )
        x = source[n % count].astype(jnp.float32)
        x_re, x_im = x[:, :half], x[:, half:]
        cosv, sinv = cos_ref[n : n + 1, :], sin_ref[n : n + 1, :]
        re = weight * (x_re * cosv - x_im * sinv)
        im = weight * (x_re * sinv + x_im * cosv)
        return re, im, ctf * weight_row

    for g in (*range(1, GROUP), 0):
        source = given[g - 1] if g else own
        if g == 0:
            for fetch in fetches:
                fetch.wait()
        for start in range(g * count, (g + 1) * count, batch):
            done = [one(n, source) for n in range(start, start + batch)]
            for n, (re, im, power) in zip(range(start, start + batch), done):
                at = pl.ds(pl.multiple_of(place_ref[place_at, n], PAD), cycles)
                total[at, :half] += re
                total[at, half:] += im
                if chunk == 0:
                    powers[pl.ds(place_ref[1, n], 1), :] += power
    if chunk == 0:
        blocks = powers.shape[0] // PAD
        for b in range(blocks):
            at = slice((b + 1) * size - PAD, (b + 1) * size)
            total[at, :LANES] = powers[b * PAD : (b + 1) * PAD]
    rows = keep_ref.shape[0]
    keep_ref[...] = total[:rows]
    give_ref[...] = total[rows:]
    if chunk == 0:
        for save in saves:
            save.wait()


def class_sums(scalars, view, chunk, given, meta, noise, shared, slice_cycles, far, rows, shards):
    width = view.shape[-1]
    count = view.shape[2] if view.shape[0] == 2 else view.shape[0]
    first = chunk == 0
    particles = count * GROUP
    out = pltpu.VMEM((rows, width), jnp.float32)
    kinds = [
        ((8, LANES), jnp.int32),
        ((particles, 2 * LANES), given[0].dtype),
        ((particles, width // 2), jnp.float32),
        ((particles, width // 2), jnp.float32),
    ]
    shapes = [out, out] + ([pltpu.HBM(shape, dtype) for shape, dtype in kinds] if first else [])
    scratch = [
        pltpu.VMEM((2 * rows, width), jnp.float32),
        pltpu.VMEM((count, PAD, width), view.dtype),
    ]
    if first:
        scratch += [pltpu.VMEM((shards * PAD, LANES), jnp.float32)]
        scratch += [pltpu.VMEM(shape, dtype) for shape, dtype in kinds]
    ins = [meta] if first else []
    return pl.pallas_call(
        functools.partial(
            sums_kernel, slice_cycles=slice_cycles, far=far, chunk=chunk, shards=shards
        ),
        out_shape=shapes,
        in_specs=[SCALARS] * 3 + [HERE] * (len(ins) + 1) + [THERE]
        + [HERE] * (GROUP - 1 + len(shared)),
        out_specs=[HERE, HERE] + [THERE] * (len(shapes) - 2),
        scratch_shapes=scratch
        + [pltpu.SMEM((8, LANES), jnp.int32), pltpu.SemaphoreType.DMA((5 + SPLITS,))],
        cost_estimate=cost(2.5),
        compiler_params=room(((2 * rows, width), 8), ((particles * PAD, width), 4)),
    )(*scalars, *held_near(*ins), noise, *held_far(view), *held_near(*given, *shared))


def spans(rows):
    return [(at, min(LANES, rows - at)) for at in range(0, rows, LANES)]


def encode(value, out, rows):
    codes = jnp.zeros((PAD, LANES), jnp.float32)
    blocks = spans(rows)
    for i, (start, size) in enumerate(blocks):
        x = value[start : start + size]
        scaled, code = coded(x)
        out[start : start + size, :] = scaled
        eye = iota((size, LANES), 0) == iota((size, LANES), 1)
        row = jnp.sum(jnp.where(eye, code, 0.0), axis=0, keepdims=True)
        codes = jnp.where(iota((PAD, LANES), 0) == i, row, codes)
    out[rows:, :] = jnp.zeros((PAD, out.shape[1]), jnp.int16)
    if value.shape[0] > rows:
        scaled, code = coded(value[rows:, :LANES])
        out[rows:, :LANES] = scaled
        eye = iota((PAD, LANES), 0) == iota((PAD, LANES), 1)
        row = jnp.sum(jnp.where(eye, code, 0.0), axis=0, keepdims=True)
        codes = jnp.where(iota((PAD, LANES), 0) == len(blocks), row, codes)
    out[rows:, LANES : 2 * LANES] = codes.astype(jnp.int32).astype(jnp.int16)


def coded(x):
    top = jnp.maximum(jnp.max(jnp.abs(x), axis=1, keepdims=True), 1e-30)
    code = jnp.floor(jnp.log(top) / UNIT) + 1.0
    scaled = jnp.round(x * (jnp.exp(-code * UNIT) * 32767.0))
    return jnp.clip(scaled, -32767.0, 32767.0).astype(jnp.int32).astype(jnp.int16), code


def decode(ref):
    rows = ref.shape[0] - PAD
    codes = ref[rows:, LANES : 2 * LANES].astype(jnp.int32).astype(jnp.float32)
    parts = []
    for i, (start, size) in enumerate(spans(rows)):
        parts.append(ref[start : start + size, :].astype(jnp.int32).astype(jnp.float32) * scale(codes, i, size))
    return jnp.concatenate(parts, axis=0)


def decode_power(ref):
    rows = ref.shape[0] - PAD
    codes = ref[rows:, LANES : 2 * LANES].astype(jnp.int32).astype(jnp.float32)
    x = ref[rows:, :LANES].astype(jnp.int32).astype(jnp.float32)
    return x * scale(codes, len(spans(rows)), PAD)


def scale(codes, i, size):
    eye = iota((size, LANES), 0) == iota((size, LANES), 1)
    row = jnp.broadcast_to(codes[i : i + 1], (size, LANES))
    code = jnp.sum(jnp.where(eye, row, 0.0), axis=1, keepdims=True)
    return jnp.exp(code * UNIT) * (1.0 / 32767.0)


def shard_kernel(bit_ref, keep_ref, get_ref, own_ref, code_ref, *, was_coded):
    parts, rows, _ = own_ref.shape
    full = code_ref.shape[1] - PAD
    if was_coded:
        for p in range(2 * parts):
            keep_ref[p, :full] = keep_ref[p, :full] + decode(get_ref.at[p])
            if rows > full:
                keep_ref[p, full:, :LANES] = keep_ref[p, full:, :LANES] + decode_power(get_ref.at[p])
    bit = bit_ref[0]
    for p in range(parts):
        mine, other = bit * parts + p, (1 - bit) * parts + p
        if was_coded:
            encode(keep_ref[other], code_ref.at[p], full)
            own_ref[p] = keep_ref[mine]
        else:
            encode(keep_ref[other] + get_ref[other], code_ref.at[p], full)
            own_ref[p] = keep_ref[mine] + get_ref[mine]


def split_shards(bit, keep, get, full):
    parts, rows, width = keep.shape
    parts = parts // 2
    own = pltpu.VMEM((parts, rows, width), jnp.float32)
    code = pltpu.VMEM((parts, full + PAD, width), jnp.int16)
    return pl.pallas_call(
        functools.partial(shard_kernel, was_coded=get.dtype == jnp.int16),
        out_shape=(own, code),
        in_specs=[SCALARS, HERE, HERE],
        out_specs=(HERE, HERE),
        cost_estimate=cost(1.5),
        compiler_params=room((keep.shape, 16)),
    )(bit, *held_near(keep, get))


def ahead_kernel(keep_ref, get_ref, power_ref, code_ref, total):
    full = keep_ref.shape[0] - PAD
    total[:full] = keep_ref[:full] + decode(get_ref)
    total[full:, :] = jnp.zeros((PAD, total.shape[1]), jnp.float32)
    total[full:, :LANES] = keep_ref[full:, :LANES] + decode_power(get_ref)
    power_ref[...] = total[full:, :LANES]
    encode(total, code_ref, full)


def ahead(keep, get):
    rows, width = keep.shape
    return pl.pallas_call(
        ahead_kernel,
        out_shape=(
            pltpu.VMEM((PAD, LANES), jnp.float32),
            pltpu.VMEM((rows, width), jnp.int16),
        ),
        in_specs=[HERE, HERE],
        out_specs=(HERE, HERE),
        scratch_shapes=[pltpu.VMEM((rows, width), jnp.float32)],
        cost_estimate=cost(1),
        compiler_params=room((keep.shape, 20)),
        name="ahead",
    )(*held_near(keep, get))


def final_kernel(dom_ref, keep_ref, get_ref, power_ref, came_ref, out):
    classes, cycles, _ = out.shape
    sums = keep_ref[...] + decode(get_ref) + decode(came_ref)
    powers = power_ref[...] + decode_power(came_ref)
    r = iota((cycles, LANES), 0)
    pick = iota((cycles, LANES), 1) == dom_ref[0] * cycles + r
    for k in range(classes):
        row = jnp.broadcast_to(powers[k : k + 1], pick.shape)
        denom = jnp.sum(jnp.where(pick, row, 0.0), axis=1, keepdims=True) + 1.0
        out[k] = sums[k * cycles : (k + 1) * cycles, :] / denom


def finish(dom, keep, get, power, came, classes, cycles, width):
    out = (classes, cycles, width)
    return pl.pallas_call(
        final_kernel,
        out_shape=jax.ShapeDtypeStruct(out, jnp.float32),
        in_specs=[SCALARS] + [HERE] * 4,
        out_specs=HERE,
        cost_estimate=cost(1),
        compiler_params=room((out, 16)),
        name="finish",
    )(dom, *held_near(keep, get, power, came))


def decoded(get):
    rows = get.shape[0] - PAD
    codes = get[rows:, LANES : 2 * LANES].astype(jnp.float32)
    values = get.astype(jnp.float32)
    scales = jnp.exp(codes * UNIT) * (1.0 / 32767.0)
    blocks = len(spans(rows))
    full = values[:rows] * scales[:blocks].reshape(-1)[:rows, None]
    return full, values[rows:, :LANES] * scales[blocks, :PAD, None]


def per_device(spectra, ctf, noise_power, references, owner, sub_class, rotation):
    count, cycles, width = spectra.shape
    k_local = references.shape[0]
    domains, shards = lax.axis_size("dom"), lax.axis_size("cls")
    dom, cls = lax.axis_index("dom"), lax.axis_index("cls")
    far = domains // GROUP
    slice_cycles = cycles // domains
    near = (dom & (GROUP - 1)).reshape(1)
    top = (dom // (domains // 2)).reshape(1)
    noise = noise_power.reshape(1, cycles)

    if slice_cycles == PAD:
        view = spectra.reshape(count, 2, GROUP, PAD, width)
    else:
        view = spectra.reshape(count, 2, far // 2, GROUP, slice_cycles, width)
        view = view.transpose(1, 3, 0, 2, 4, 5).reshape(2, GROUP, count, PAD, width)
    rows_of = [v.reshape(1, count) for v in (owner, sub_class, rotation)]
    meta, *sent_0 = pieces(near, top, view, 0, (ctf, *rows_of))
    sent = (sent_0, pieces(near, top, view, 1, ()))
    got = [[swap(sent[c][m - 1], "dom", m) for m in range(1, GROUP)] for c in range(CHUNKS)]

    held, mask = references, 2
    own_side, other_side = references, None
    while mask < shards:
        new = swap(held, "cls", mask)
        other_side = new if other_side is None else jnp.concatenate([other_side, new], axis=0)
        held = jnp.concatenate([held, new], axis=0) if 2 * mask < shards else held
        mask *= 2
    table, low = rotation_table(spectra, references.shape[1])
    near_refs = swap(own_side, "cls", 1)
    per = count // NEAR_CALLS
    before = []
    for i in range(NEAR_CALLS):
        before += score(low, ctf, noise, own_side, near_refs, table, (), i * per, per)
    far_refs = swap(other_side, "cls", 1)
    row = score(low, ctf, noise, other_side, far_refs, table, before, 0, count)
    log_evidence = row.reshape(count)

    scalars = (near, top, cls.reshape(1))
    ends, shared = [], []
    for chunk in range(CHUNKS):
        size = k_local * PAD + (PAD if chunk == 0 else 0)
        keep, give, *more = class_sums(
            scalars, view, chunk, got[chunk], meta, noise, shared, slice_cycles, far,
            shards // 2 * size, shards,
        )
        shared = more
        get = swap(give, "cls", 1)
        shape = (shards // 2, size, width)
        keep, get = keep.reshape(shape), get.reshape(shape)
        mask = shards // 2
        while mask >= 2:
            bit = ((cls // mask) & 1).reshape(1)
            keep, code = split_shards(bit, keep, get, k_local * PAD)
            get = swap(code, "cls", mask)
            mask //= 2
        ends.append((keep[0], get[0]))
    power, code = ahead(*ends[0])
    came = swap(code, "dom", domains // 2)
    if far == 2:
        new_refs = finish(dom.reshape(1), *ends[1], power, came, k_local, slice_cycles, width)
        return (new_refs, log_evidence)

    came, came_power = decoded(came)
    keep, get = ends[1]
    numer = (keep + decoded(get)[0] + came).reshape(k_local, PAD, width)
    power = power + came_power
    left, mask = PAD, domains // 4
    while mask >= GROUP:
        bit = (dom // mask) & 1
        left = left // 2
        own = lax.dynamic_slice_in_dim(numer, bit * left, left, 1)
        other = lax.dynamic_slice_in_dim(numer, (1 - bit) * left, left, 1)
        numer = own + swap(other, "dom", mask)
        power = power + swap(power, "dom", mask)
        mask //= 2
    denom = lax.dynamic_slice_in_dim(power[:k_local], dom * left, left, 1)
    return (numer / (denom + 1.0)[:, :, None], log_evidence)


def solution(mesh):
    return jax.shard_map(
        per_device,
        mesh=mesh,
        in_specs=(
            P(("dom", "cls"), None, None),
            P(("dom", "cls"), None),
            P(),
            P("cls", None, None),
            P(("dom", "cls"), None),
            P(("dom", "cls")),
            P(("dom", "cls")),
        ),
        out_specs=(P("cls", "dom", None), P(("dom", "cls"))),
        check_vma=False,
    )
```

```python
import functools
import math

import jax
import jax.numpy as jnp
from jax import lax
from jax.experimental import pallas as pl
from jax.experimental.pallas import tpu as pltpu
from jax.sharding import PartitionSpec as P


CHUNKS = 2
GROUP = 4
NEAR_CALLS = 2
SPLITS = 4
LANES = 128
PAD = 16
STEPS = 64.0
UNIT = math.log(2.0) / STEPS


def table_kernel(image_ref, out_ref, low_ref, sems):
    width, turns_all = out_ref.shape
    count, cycles, _ = low_ref.shape
    part = count // SPLITS
    copies = [
        pltpu.make_async_copy(
            image_ref.at[pl.ds(i * part, part), :cycles, :], low_ref.at[pl.ds(i * part, part)], sems.at[i]
        )
        for i in range(SPLITS)
    ]
    for copy in copies:
        copy.start()
    half = width // 2
    quarter = half // 2
    step = 32
    for at in range(0, quarter, step):
        shape = (step, turns_all)
        turns = (iota(shape, 0) + at) * iota(shape, 1) & (turns_all - 1)
        angle = turns.astype(jnp.float32) * (2.0 * math.pi / turns_all)
        cosv, sinv = jnp.cos(angle), jnp.sin(angle)
        odd, back = (iota(shape, 1) & 1) == 1, (iota(shape, 1) & 2) == 2
        cos_on, sin_on = jnp.where(odd, -sinv, cosv), jnp.where(odd, cosv, sinv)
        cos_on, sin_on = jnp.where(back, -cos_on, cos_on), jnp.where(back, -sin_on, sin_on)
        out_ref[at : at + step, :] = cosv.astype(jnp.bfloat16)
        out_ref[quarter + at : quarter + at + step, :] = cos_on.astype(jnp.bfloat16)
        out_ref[half + at : half + at + step, :] = (-sinv).astype(jnp.bfloat16)
        at = half + quarter + at
        out_ref[at : at + step, :] = (-sin_on).astype(jnp.bfloat16)
    for copy in copies:
        copy.wait()


def rotation_table(spectra, cycles):
    count, _, width = spectra.shape
    return pl.pallas_call(
        table_kernel,
        out_shape=(
            pltpu.VMEM((width, width), jnp.bfloat16),
            pltpu.VMEM((count, cycles, width), spectra.dtype),
        ),
        in_specs=[THERE],
        out_specs=(HERE, HERE),
        scratch_shapes=[pltpu.SemaphoreType.DMA((SPLITS,))],
        cost_estimate=cost(2),
        compiler_params=room(((width, width), 4)),
        name="table",
    )(*held_far(spectra))


def held_near(*values):
    return [pltpu.with_memory_space_constraint(v, pltpu.VMEM) for v in values]


def held_far(*values):
    return [pltpu.with_memory_space_constraint(v, pltpu.HBM) for v in values]


def swap(value, axis, mask):
    size = lax.axis_size(axis)
    return lax.ppermute(value, axis, [(i, i ^ mask) for i in range(size)])


def iota(shape, axis):
    return lax.broadcasted_iota(jnp.int32, shape, axis)


HERE = pl.BlockSpec(memory_space=pltpu.VMEM)
SCALARS = pl.BlockSpec(memory_space=pltpu.SMEM)
THERE = pl.BlockSpec(memory_space=pltpu.HBM)


def room(*arrays):
    size = sum(math.prod(shape) * bits for shape, bits in arrays)
    return pltpu.CompilerParams(vmem_limit_bytes=size + (8 << 20))


def cost(us):
    return pl.CostEstimate(flops=0, transcendentals=0, bytes_accessed=int(us * 3.6e6))


def score_kernel(
    low_ref, ctf_ref, noise_ref, first_ref, second_ref, table_ref, *refs, merge, start
):
    before, refs = refs[:merge], refs[merge:]
    found = None
    if merge and start:
        found, refs = refs[0], refs[1:]
    outs, refs = refs[: 1 if merge else 2], refs[1 if merge else 2 :]
    image, image_sum, staged, classes, cross = refs[:5]
    copies = []
    if merge:
        there, first_ref, sems = first_ref, refs[5], refs[6]
        part = there.shape[0] // SPLITS
        copies = [
            pltpu.make_async_copy(
                there.at[pl.ds(i * part, part)], first_ref.at[pl.ds(i * part, part)], sems.at[i]
            )
            for i in range(SPLITS)
        ]
    for copy in copies:
        copy.start()
    _, cycles, width = low_ref.shape
    tiles = width // LANES
    pairs = tiles // 2
    count = image.shape[1] // cycles
    kinds = cross.shape[0] // count
    part = first_ref.shape[0]
    ctf = ctf_ref[start : start + count, :].astype(jnp.float32)
    weight = ctf / noise_ref[...]
    power = ctf * weight
    eye = iota((cycles, LANES), 0) == iota((cycles, LANES), 1)
    for n in range(count):
        row = jnp.broadcast_to(weight[n : n + 1, :], (cycles, LANES))
        column = jnp.sum(jnp.where(eye, row, 0.0), axis=1, keepdims=True)
        low = low_ref[start + n].astype(jnp.float32)
        weighted = (column * low).astype(jnp.bfloat16).astype(jnp.float32)
        for f in range(tiles):
            image[f, n * cycles : (n + 1) * cycles, :] = weighted[:, f * LANES : (f + 1) * LANES]
        for f in range(pairs):
            re = weighted[:, f * LANES : (f + 1) * LANES]
            im = weighted[:, (f + pairs) * LANES : (f + pairs + 1) * LANES]
            image_sum[f, n * cycles : (n + 1) * cycles, :] = re + im
    for copy in copies:
        copy.wait()
    for at, ref in ((0, first_ref), (part, second_ref)):
        for f in range(tiles):
            staged[f, at : at + part, :] = ref[:, f * LANES : (f + 1) * LANES].astype(jnp.float32)
    blocks = kinds // 8
    zero = jnp.zeros((8, LANES), jnp.float32)
    norms = []
    for b in range(blocks):
        square = jnp.zeros((cycles, 8, LANES), jnp.float32)
        for f in range(pairs):
            rows = pl.ds(b * 8 * cycles, 8 * cycles)
            re = jnp.swapaxes(staged[f, rows, :].reshape(8, cycles, LANES), 0, 1)
            im = jnp.swapaxes(staged[f + pairs, rows, :].reshape(8, cycles, LANES), 0, 1)
            classes[3 * f, :, b * 8 : b * 8 + 8, :] = re
            classes[3 * f + 1, :, b * 8 : b * 8 + 8, :] = re - im
            classes[3 * f + 2, :, b * 8 : b * 8 + 8, :] = re + im
            square = square + (re * re + im * im)
        norm = zero
        for r in range(cycles):
            total = jnp.sum(square[r], axis=1, keepdims=True)
            norm = jnp.where(iota((8, LANES), 1) == r, total, norm)
        norms.append(norm)
    group = 2
    for f in range(pairs):

        def particles(g, _):
            def cycle(r, sums):
                new = list(sums)
                for i in range(group):
                    row = pl.ds((g * group + i) * cycles + r, 8, stride=0)
                    a_sum, a_im, a_re = image_sum[f, row, :], image[f + pairs, row, :], image[f, row, :]
                    for b in range(blocks):
                        at = slice(b * 8, b * 8 + 8)
                        j = 3 * (i * blocks + b)
                        new[j] = new[j] + classes[3 * f, r, at, :] * a_sum
                        new[j + 1] = new[j + 1] + classes[3 * f + 1, r, at, :] * a_im
                        new[j + 2] = new[j + 2] + classes[3 * f + 2, r, at, :] * a_re
                return tuple(new)

            sums = lax.fori_loop(0, cycles, cycle, (zero,) * (3 * group * blocks), unroll=16)
            for i in range(group):
                for b in range(blocks):
                    s1, s2, s3 = sums[3 * (i * blocks + b) : 3 * (i * blocks + b) + 3]
                    at = pl.ds(pl.multiple_of((g * group + i) * kinds + b * 8, 8), 8)
                    cross[at, f * LANES : (f + 1) * LANES] = s1 - s2
                    cross[at, (f + pairs) * LANES : (f + pairs + 1) * LANES] = s1 - s3
            return 0

        lax.fori_loop(0, count // group, particles, 0)
    scores = jnp.dot(
        cross[...].astype(jnp.bfloat16), table_ref[...], preferred_element_type=jnp.float32
    )
    cross[...] = scores
    inner = iota((8, LANES), 1) < cycles
    tops, totals = [], []
    for n in range(count):
        powers = jnp.where(inner, jnp.broadcast_to(power[n : n + 1, :], (8, LANES)), 0.0)
        most = None
        for b in range(blocks):
            energy = jnp.sum(powers * norms[b], axis=1, keepdims=True)
            at = n * kinds + b * 8
            mine = cross[at : at + 8, :] - 0.5 * energy
            cross[at : at + 8, :] = mine
            most = mine if most is None else jnp.maximum(most, mine)
        tops.append(jnp.max(most, axis=(0, 1), keepdims=True))
    if merge:
        per = count // (merge // 2)
        old = [
            [before[n // per * 2 + i][n % per : n % per + 1, :1] for n in range(count)] for i in range(2)
        ]
        tops = [jnp.maximum(top, was) for top, was in zip(tops, old[0])]
    for n in range(count):
        mine = jnp.exp(cross[n * kinds : (n + 1) * kinds, :] - tops[n])
        part_sum = mine[:8]
        for b in range(1, blocks):
            part_sum = part_sum + mine[b * 8 : b * 8 + 8]
        totals.append(jnp.sum(part_sum, axis=(0, 1), keepdims=True))
    if not merge:
        for n in range(count):
            outs[0][n : n + 1, :] = jnp.broadcast_to(tops[n], (1, LANES))
            outs[1][n : n + 1, :] = jnp.broadcast_to(totals[n], (1, LANES))
        return
    row_top = jnp.zeros(outs[0].shape, jnp.float32)
    row_was, row_total, row_old = row_top, row_top, row_top
    for n in range(count):
        here = iota(row_top.shape, 1) == start + n
        row_top = jnp.where(here, tops[n], row_top)
        row_total = jnp.where(here, totals[n], row_total)
        row_was = jnp.where(here, old[0][n], row_was)
        row_old = jnp.where(here, old[1][n], row_old)
    result = row_top + jnp.log(row_total + row_old * jnp.exp(row_was - row_top))
    at = iota(row_top.shape, 1)
    earlier = row_top if found is None else found[...]
    outs[0][...] = jnp.where((at >= start) & (at < start + count), result, earlier)


def score(low, ctf, noise, first, second, table, before, found, start, count):
    _, cycles, width = low.shape
    kinds = 2 * first.shape[0]
    merge = len(before)
    each = pltpu.VMEM((count, LANES), jnp.float32)
    row = jax.ShapeDtypeStruct((1, ctf.shape[0]), jnp.float32)
    part = (kinds // 2 * cycles, width)
    return pl.pallas_call(
        functools.partial(score_kernel, merge=merge, start=start),
        out_shape=row if merge else (each, each),
        in_specs=[HERE] * 3 + [THERE if merge else HERE] + [HERE] * (2 + merge + len(found)),
        out_specs=HERE if merge else (HERE, HERE),
        scratch_shapes=[
            pltpu.VMEM((width // LANES, count * cycles, LANES), jnp.float32),
            pltpu.VMEM((width // LANES // 2, count * cycles, LANES), jnp.float32),
            pltpu.VMEM((width // LANES, kinds * cycles, LANES), jnp.float32),
            pltpu.VMEM((width // LANES // 2 * 3, cycles, kinds, LANES), jnp.float32),
            pltpu.VMEM((count * kinds, width), jnp.float32),
        ]
        + ([pltpu.VMEM(part, first.dtype), pltpu.SemaphoreType.DMA((SPLITS,))] if merge else []),
        cost_estimate=cost(count / 2),
        compiler_params=room(
            ((count * cycles, width), 8),
            ((kinds * cycles, width), 12),
            ((count * kinds, width), 8),
            (table.shape, 2),
        ),
    )(
        *held_near(low), ctf, noise, *(held_far if merge else held_near)(first.reshape(part)),
        *held_near(second.reshape(part), table),
        *before, *found,
    )


def part_of(view_ref, top, near):
    if view_ref.shape[0] == 2:
        return view_ref.at[top, near]
    return view_ref.at[:, top, near]


def column(row):
    size = row.shape[1]
    eye = iota((size, size), 0) == iota((size, size), 1)
    return jnp.sum(jnp.where(eye, jnp.broadcast_to(row, (size, size)), 0.0), axis=1, keepdims=True)


def pieces_kernel(near_ref, top_ref, view_ref, *refs, chunk):
    outs, sems = refs[-GROUP:-1], refs[-1]
    if chunk == 0:
        ctf_ref, owner_ref, sub_ref, turn_ref, meta_ref = refs[:5]
        outs = refs[5 : 5 + GROUP - 1]
        ctf_here, owner_here, sub_here, turn_here, small, sems = refs[5 + GROUP - 1 :]
        fetches = [
            pltpu.make_async_copy(there, here, small.at[i])
            for i, (there, here) in enumerate(
                ((ctf_ref, ctf_here), (owner_ref, owner_here), (sub_ref, sub_here), (turn_ref, turn_here))
            )
        ]
        for fetch in fetches:
            fetch.start()
    count = view_ref.shape[2] if view_ref.shape[0] == 2 else view_ref.shape[0]
    part = count // SPLITS
    copies = [
        pltpu.make_async_copy(
            part_of(view_ref, top_ref[0] ^ (1 - chunk), near_ref[0] ^ (i + 1)).at[
                pl.ds(j * part, part)
            ],
            out.at[pl.ds(j * part, part)],
            sems.at[i * SPLITS + j],
        )
        for i, out in enumerate(outs)
        for j in range(SPLITS)
    ]
    for copy in copies:
        copy.start()
    if chunk == 0:
        for fetch in fetches:
            fetch.wait()
        cycles = ctf_ref.shape[1]
        turn = turn_here[...]
        shape = (count, meta_ref.shape[1] - cycles)
        at = iota(shape, 1)
        rest = jnp.where(at == 0, column((turn >> 4).astype(jnp.float32)), 0.0)
        rest = jnp.where(at == 1, column((turn & 15).astype(jnp.float32)), rest)
        rest = jnp.where(at == 2, column(owner_here[...].astype(jnp.float32)), rest)
        rest = jnp.where(at == 3, column(sub_here[...].astype(jnp.float32)), rest)
        meta_ref[:, :cycles] = ctf_here[...]
        meta_ref[:, cycles:] = rest.astype(jnp.bfloat16)
        for out in outs:
            out[count, :, :] = jnp.zeros(out.shape[1:], out.dtype)
            out[count, :, : meta_ref.shape[1]] = meta_ref[...]
    for copy in copies:
        copy.wait()


def pieces(near, top, view, chunk, others):
    count, width = view.shape[2] if view.shape[0] == 2 else view.shape[0], view.shape[-1]
    out = pltpu.VMEM((count + (chunk == 0), PAD, width), view.dtype)
    shapes = [out] * (GROUP - 1)
    scratch = [pltpu.SemaphoreType.DMA(((GROUP - 1) * SPLITS,))]
    if chunk == 0:
        ctf = others[0]
        shapes = [pltpu.VMEM((count, 2 * ctf.shape[1]), view.dtype)] + shapes
        scratch = [
            pltpu.VMEM(ctf.shape, ctf.dtype),
            pltpu.VMEM((1, count), jnp.int32),
            pltpu.VMEM((1, count), jnp.int32),
            pltpu.VMEM((1, count), jnp.int32),
            pltpu.SemaphoreType.DMA((4,)),
        ] + scratch
    return pl.pallas_call(
        functools.partial(pieces_kernel, chunk=chunk),
        out_shape=shapes,
        in_specs=[SCALARS] * 2 + [THERE] * (1 + len(others)),
        out_specs=[HERE] * len(shapes),
        scratch_shapes=scratch,
        cost_estimate=cost(1.5),
        compiler_params=room(((count * PAD, width), 2 * GROUP)),
    )(near, top, *held_far(view, *others))


def sums_kernel(
    near_ref, top_ref, cls_ref, *refs, slice_cycles, far, chunk, shards,
):
    if chunk == 0:
        meta_ref, refs = refs[0], refs[1:]
    noise_ref, view_ref, refs = refs[0], refs[1], refs[2:]
    given, refs = refs[: GROUP - 1], refs[GROUP - 1 :]
    if chunk == 0:
        keep_ref, give_ref = refs[:2]
        shared, refs = refs[2:6], refs[6:]
        total, own, powers, plan, metas, cos_ref, sin_ref, place_ref, sems = refs
    else:
        plan, metas, cos_ref, sin_ref = refs[:4]
        keep_ref, give_ref, total, own, place_ref, sems = refs[4:]
    cycles, half = PAD, cos_ref.shape[1]
    side = top_ref[0] ^ (1 - chunk)
    particles = cos_ref.shape[0]
    count = particles // GROUP
    width = 2 * half
    size = keep_ref.shape[0] // (shards // 2)
    part = count // SPLITS
    fetches = [
        pltpu.make_async_copy(
            part_of(view_ref, side, near_ref[0]).at[pl.ds(i * part, part)],
            own.at[pl.ds(i * part, part)],
            sems.at[5 + i],
        )
        for i in range(SPLITS)
    ]
    for fetch in fetches:
        fetch.start()
    schedule = pltpu.make_async_copy(plan, place_ref, sems.at[0])
    if chunk == 0:
        metas[:count] = meta_ref[...]
        for g, piece in enumerate(given):
            metas[(g + 1) * count : (g + 2) * count] = piece[count, :, : metas.shape[1]]
        ints = metas[:, LANES : LANES + LANES].astype(jnp.float32).astype(jnp.int32)
        turn = ints[:, 0:1] * 16 + ints[:, 1:2]
        shard, inside = ints[:, 2:3], ints[:, 3:4]
        block = ((shard ^ cls_ref[0]) & 1) * (shards // 2) + (shard >> 1)
        here = iota((particles, LANES), 0) == iota((particles, LANES), 1)

        def in_row(values):
            return jnp.sum(jnp.where(here, values.astype(jnp.float32), 0.0), axis=0, keepdims=True)

        rows = (
            in_row(block * size + inside * cycles),
            in_row(block * PAD + inside),
            in_row(block * (size - PAD) + inside * cycles),
        )
        at = iota(plan.shape, 0)
        places = jnp.where(at == 0, rows[0], jnp.where(at == 1, rows[1], rows[2]))
        plan[...] = places.astype(jnp.int32)
        schedule.start()
        total[...] = jnp.zeros_like(total)
        powers[...] = jnp.zeros_like(powers)
        turns = iota((particles, half), 1) * turn & (width - 1)
        angle = turns.astype(jnp.float32) * (2.0 * math.pi / width)
        cos_ref[...] = jnp.cos(angle)
        sin_ref[...] = jnp.sin(angle)
        saves = [
            pltpu.make_async_copy(here, there, sems.at[1 + i])
            for i, (here, there) in enumerate(zip((plan, metas, cos_ref, sin_ref), shared))
        ]
        for save in saves:
            save.start()
    else:
        schedule.start()
        total[...] = jnp.zeros_like(total)
    r = iota((cycles, LANES), 0)
    domain = (side * (far // 2) + r // slice_cycles) * GROUP + near_ref[0]
    pick = iota((cycles, LANES), 1) == domain * slice_cycles + r % slice_cycles
    batch = 2
    schedule.wait()
    place_at = 0 if chunk == 0 else 2

    def one(n, source):
        ctf = metas[n : n + 1, :LANES].astype(jnp.float32)
        weight_row = ctf / noise_ref[...]
        weight = jnp.sum(
            jnp.where(pick, jnp.broadcast_to(weight_row, pick.shape), 0.0), axis=1, keepdims=True
        )
        x = source[n % count].astype(jnp.float32)
        x_re, x_im = x[:, :half], x[:, half:]
        cosv, sinv = cos_ref[n : n + 1, :], sin_ref[n : n + 1, :]
        re = weight * (x_re * cosv - x_im * sinv)
        im = weight * (x_re * sinv + x_im * cosv)
        return re, im, ctf * weight_row

    for g in (*range(1, GROUP), 0):
        source = given[g - 1] if g else own
        if g == 0:
            for fetch in fetches:
                fetch.wait()
        for start in range(g * count, (g + 1) * count, batch):
            done = [one(n, source) for n in range(start, start + batch)]
            for n, (re, im, power) in zip(range(start, start + batch), done):
                at = pl.ds(pl.multiple_of(place_ref[place_at, n], PAD), cycles)
                total[at, :half] += re
                total[at, half:] += im
                if chunk == 0:
                    powers[pl.ds(place_ref[1, n], 1), :] += power
    if chunk == 0:
        blocks = powers.shape[0] // PAD
        for b in range(blocks):
            at = slice((b + 1) * size - PAD, (b + 1) * size)
            total[at, :LANES] = powers[b * PAD : (b + 1) * PAD]
    rows = keep_ref.shape[0]
    keep_ref[...] = total[:rows]
    give_ref[...] = total[rows:]
    if chunk == 0:
        for save in saves:
            save.wait()


def class_sums(scalars, view, chunk, given, meta, noise, shared, slice_cycles, far, rows, shards):
    width = view.shape[-1]
    count = view.shape[2] if view.shape[0] == 2 else view.shape[0]
    first = chunk == 0
    particles = count * GROUP
    out = pltpu.VMEM((rows, width), jnp.float32)
    kinds = [
        ((8, LANES), jnp.int32),
        ((particles, 2 * LANES), given[0].dtype),
        ((particles, width // 2), jnp.float32),
        ((particles, width // 2), jnp.float32),
    ]
    shapes = [out, out] + ([pltpu.HBM(shape, dtype) for shape, dtype in kinds] if first else [])
    scratch = [
        pltpu.VMEM((2 * rows, width), jnp.float32),
        pltpu.VMEM((count, PAD, width), view.dtype),
    ]
    if first:
        scratch += [pltpu.VMEM((shards * PAD, LANES), jnp.float32)]
        scratch += [pltpu.VMEM(shape, dtype) for shape, dtype in kinds]
    ins = [meta] if first else []
    return pl.pallas_call(
        functools.partial(
            sums_kernel, slice_cycles=slice_cycles, far=far, chunk=chunk, shards=shards
        ),
        out_shape=shapes,
        in_specs=[SCALARS] * 3 + [HERE] * (len(ins) + 1) + [THERE]
        + [HERE] * (GROUP - 1 + len(shared)),
        out_specs=[HERE, HERE] + [THERE] * (len(shapes) - 2),
        scratch_shapes=scratch
        + [pltpu.SMEM((8, LANES), jnp.int32), pltpu.SemaphoreType.DMA((5 + SPLITS,))],
        cost_estimate=cost(2.5),
        compiler_params=room(((2 * rows, width), 8), ((particles * PAD, width), 4)),
    )(*scalars, *held_near(*ins), noise, *held_far(view), *held_near(*given, *shared))


def spans(rows):
    return [(at, min(LANES, rows - at)) for at in range(0, rows, LANES)]


def encode(value, out, rows):
    codes = jnp.zeros((PAD, LANES), jnp.float32)
    blocks = spans(rows)
    for i, (start, size) in enumerate(blocks):
        x = value[start : start + size]
        scaled, code = coded(x)
        out[start : start + size, :] = scaled
        eye = iota((size, LANES), 0) == iota((size, LANES), 1)
        row = jnp.sum(jnp.where(eye, code, 0.0), axis=0, keepdims=True)
        codes = jnp.where(iota((PAD, LANES), 0) == i, row, codes)
    out[rows:, :] = jnp.zeros((PAD, out.shape[1]), jnp.int16)
    if value.shape[0] > rows:
        scaled, code = coded(value[rows:, :LANES])
        out[rows:, :LANES] = scaled
        eye = iota((PAD, LANES), 0) == iota((PAD, LANES), 1)
        row = jnp.sum(jnp.where(eye, code, 0.0), axis=0, keepdims=True)
        codes = jnp.where(iota((PAD, LANES), 0) == len(blocks), row, codes)
    out[rows:, LANES : 2 * LANES] = codes.astype(jnp.int32).astype(jnp.int16)


def coded(x):
    top = jnp.maximum(jnp.max(jnp.abs(x), axis=1, keepdims=True), 1e-30)
    code = jnp.floor(jnp.log(top) / UNIT) + 1.0
    scaled = jnp.round(x * (jnp.exp(-code * UNIT) * 32767.0))
    return jnp.clip(scaled, -32767.0, 32767.0).astype(jnp.int32).astype(jnp.int16), code


def decode(ref):
    rows = ref.shape[0] - PAD
    codes = ref[rows:, LANES : 2 * LANES].astype(jnp.int32).astype(jnp.float32)
    parts = []
    for i, (start, size) in enumerate(spans(rows)):
        parts.append(ref[start : start + size, :].astype(jnp.int32).astype(jnp.float32) * scale(codes, i, size))
    return jnp.concatenate(parts, axis=0)


def decode_power(ref):
    rows = ref.shape[0] - PAD
    codes = ref[rows:, LANES : 2 * LANES].astype(jnp.int32).astype(jnp.float32)
    x = ref[rows:, :LANES].astype(jnp.int32).astype(jnp.float32)
    return x * scale(codes, len(spans(rows)), PAD)


def scale(codes, i, size):
    eye = iota((size, LANES), 0) == iota((size, LANES), 1)
    row = jnp.broadcast_to(codes[i : i + 1], (size, LANES))
    code = jnp.sum(jnp.where(eye, row, 0.0), axis=1, keepdims=True)
    return jnp.exp(code * UNIT) * (1.0 / 32767.0)


def shard_kernel(bit_ref, keep_ref, get_ref, own_ref, code_ref, *, was_coded):
    parts, rows, _ = own_ref.shape
    full = code_ref.shape[1] - PAD
    if was_coded:
        for p in range(2 * parts):
            keep_ref[p, :full] = keep_ref[p, :full] + decode(get_ref.at[p])
            if rows > full:
                keep_ref[p, full:, :LANES] = keep_ref[p, full:, :LANES] + decode_power(get_ref.at[p])
    bit = bit_ref[0]
    for p in range(parts):
        mine, other = bit * parts + p, (1 - bit) * parts + p
        if was_coded:
            encode(keep_ref[other], code_ref.at[p], full)
            own_ref[p] = keep_ref[mine]
        else:
            encode(keep_ref[other] + get_ref[other], code_ref.at[p], full)
            own_ref[p] = keep_ref[mine] + get_ref[mine]


def split_shards(bit, keep, get, full):
    parts, rows, width = keep.shape
    parts = parts // 2
    own = pltpu.VMEM((parts, rows, width), jnp.float32)
    code = pltpu.VMEM((parts, full + PAD, width), jnp.int16)
    return pl.pallas_call(
        functools.partial(shard_kernel, was_coded=get.dtype == jnp.int16),
        out_shape=(own, code),
        in_specs=[SCALARS, HERE, HERE],
        out_specs=(HERE, HERE),
        cost_estimate=cost(1.5),
        compiler_params=room((keep.shape, 16)),
    )(bit, *held_near(keep, get))


def ahead_kernel(keep_ref, get_ref, power_ref, code_ref, total):
    full = keep_ref.shape[0] - PAD
    total[:full] = keep_ref[:full] + decode(get_ref)
    total[full:, :] = jnp.zeros((PAD, total.shape[1]), jnp.float32)
    total[full:, :LANES] = keep_ref[full:, :LANES] + decode_power(get_ref)
    power_ref[...] = total[full:, :LANES]
    encode(total, code_ref, full)


def ahead(keep, get):
    rows, width = keep.shape
    return pl.pallas_call(
        ahead_kernel,
        out_shape=(
            pltpu.VMEM((PAD, LANES), jnp.float32),
            pltpu.VMEM((rows, width), jnp.int16),
        ),
        in_specs=[HERE, HERE],
        out_specs=(HERE, HERE),
        scratch_shapes=[pltpu.VMEM((rows, width), jnp.float32)],
        cost_estimate=cost(1),
        compiler_params=room((keep.shape, 20)),
        name="ahead",
    )(*held_near(keep, get))


def final_kernel(dom_ref, keep_ref, get_ref, power_ref, came_ref, out):
    classes, cycles, _ = out.shape
    sums = keep_ref[...] + decode(get_ref) + decode(came_ref)
    powers = power_ref[...] + decode_power(came_ref)
    r = iota((cycles, LANES), 0)
    pick = iota((cycles, LANES), 1) == dom_ref[0] * cycles + r
    for k in range(classes):
        row = jnp.broadcast_to(powers[k : k + 1], pick.shape)
        denom = jnp.sum(jnp.where(pick, row, 0.0), axis=1, keepdims=True) + 1.0
        out[k] = sums[k * cycles : (k + 1) * cycles, :] / denom


def finish(dom, keep, get, power, came, classes, cycles, width):
    out = (classes, cycles, width)
    return pl.pallas_call(
        final_kernel,
        out_shape=jax.ShapeDtypeStruct(out, jnp.float32),
        in_specs=[SCALARS] + [HERE] * 4,
        out_specs=HERE,
        cost_estimate=cost(1),
        compiler_params=room((out, 16)),
        name="finish",
    )(dom, *held_near(keep, get, power, came))


def decoded(get):
    rows = get.shape[0] - PAD
    codes = get[rows:, LANES : 2 * LANES].astype(jnp.float32)
    values = get.astype(jnp.float32)
    scales = jnp.exp(codes * UNIT) * (1.0 / 32767.0)
    blocks = len(spans(rows))
    full = values[:rows] * scales[:blocks].reshape(-1)[:rows, None]
    return full, values[rows:, :LANES] * scales[blocks, :PAD, None]


def per_device(spectra, ctf, noise_power, references, owner, sub_class, rotation):
    count, cycles, width = spectra.shape
    k_local = references.shape[0]
    domains, shards = lax.axis_size("dom"), lax.axis_size("cls")
    dom, cls = lax.axis_index("dom"), lax.axis_index("cls")
    far = domains // GROUP
    slice_cycles = cycles // domains
    near = (dom & (GROUP - 1)).reshape(1)
    top = (dom // (domains // 2)).reshape(1)
    noise = noise_power.reshape(1, cycles)

    if slice_cycles == PAD:
        view = spectra.reshape(count, 2, GROUP, PAD, width)
    else:
        view = spectra.reshape(count, 2, far // 2, GROUP, slice_cycles, width)
        view = view.transpose(1, 3, 0, 2, 4, 5).reshape(2, GROUP, count, PAD, width)
    rows_of = [v.reshape(1, count) for v in (owner, sub_class, rotation)]
    meta, *sent_0 = pieces(near, top, view, 0, (ctf, *rows_of))
    sent = (sent_0, pieces(near, top, view, 1, ()))
    got = [[swap(sent[c][m - 1], "dom", m) for m in range(1, GROUP)] for c in range(CHUNKS)]

    held, mask = references, 2
    own_side, other_side = references, None
    while mask < shards:
        new = swap(held, "cls", mask)
        other_side = new if other_side is None else jnp.concatenate([other_side, new], axis=0)
        held = jnp.concatenate([held, new], axis=0) if 2 * mask < shards else held
        mask *= 2
    table, low = rotation_table(spectra, references.shape[1])
    near_refs = swap(own_side, "cls", 1)
    per = count // NEAR_CALLS
    before = []
    for i in range(NEAR_CALLS):
        before += score(low, ctf, noise, own_side, near_refs, table, (), (), i * per, per)
    far_refs = swap(other_side, "cls", 1)
    row = ()
    for i in range(NEAR_CALLS):
        row = (
            score(
                low, ctf, noise, other_side, far_refs, table, before[2 * i : 2 * i + 2], row, i * per,
                per,
            ),
        )
    log_evidence = row[0].reshape(count)

    scalars = (near, top, cls.reshape(1))
    ends, shared = [], []
    for chunk in range(CHUNKS):
        size = k_local * PAD + (PAD if chunk == 0 else 0)
        keep, give, *more = class_sums(
            scalars, view, chunk, got[chunk], meta, noise, shared, slice_cycles, far,
            shards // 2 * size, shards,
        )
        shared = more
        get = swap(give, "cls", 1)
        shape = (shards // 2, size, width)
        keep, get = keep.reshape(shape), get.reshape(shape)
        mask = shards // 2
        while mask >= 2:
            bit = ((cls // mask) & 1).reshape(1)
            keep, code = split_shards(bit, keep, get, k_local * PAD)
            get = swap(code, "cls", mask)
            mask //= 2
        ends.append((keep[0], get[0]))
    power, code = ahead(*ends[0])
    came = swap(code, "dom", domains // 2)
    if far == 2:
        new_refs = finish(dom.reshape(1), *ends[1], power, came, k_local, slice_cycles, width)
        return (new_refs, log_evidence)

    came, came_power = decoded(came)
    keep, get = ends[1]
    numer = (keep + decoded(get)[0] + came).reshape(k_local, PAD, width)
    power = power + came_power
    left, mask = PAD, domains // 4
    while mask >= GROUP:
        bit = (dom // mask) & 1
        left = left // 2
        own = lax.dynamic_slice_in_dim(numer, bit * left, left, 1)
        other = lax.dynamic_slice_in_dim(numer, (1 - bit) * left, left, 1)
        numer = own + swap(other, "dom", mask)
        power = power + swap(power, "dom", mask)
        mask //= 2
    denom = lax.dynamic_slice_in_dim(power[:k_local], dom * left, left, 1)
    return (numer / (denom + 1.0)[:, :, None], log_evidence)


def solution(mesh):
    return jax.shard_map(
        per_device,
        mesh=mesh,
        in_specs=(
            P(("dom", "cls"), None, None),
            P(("dom", "cls"), None),
            P(),
            P("cls", None, None),
            P(("dom", "cls"), None),
            P(("dom", "cls")),
            P(("dom", "cls")),
        ),
        out_specs=(P("cls", "dom", None), P(("dom", "cls"))),
        check_vma=False,
    )
```
